32 devices in a mesh: dp: 4 (over y, x), seq: 8 (over z, core).
Axes of the slice: x: 2, y: 2, z: 4, core: 2. Of those that a mesh axis runs over, the one named last changes fastest.
Arguments:
- layer_in: float32 [4096, 2048], P(('dp', 'seq')), may hold values from -6 to 6
- norm1_gain: float32 [2048], replicated, may hold values from 0.25 to 1.75
- qkv_weight: bfloat16 [2048, 6144], P('dp'), may hold values from -0.79549513 to 0.79549513
- out_weight: bfloat16 [2048, 2048], P('dp'), may hold values from -2 to 2
- norm2_gain: float32 [2048], replicated, may hold values from 0.25 to 1.75
- gate_up_weight: bfloat16 [2048, 16384], P('dp'), may hold values from -0.125 to 0.125
- down_weight: bfloat16 [2048, 8192], P('dp'), may hold values from -0.0625 to 0.0625
- cotangent: float32 [4096, 2048], P(('dp', 'seq')), may hold values from -6 to 6
Outputs:
- layer_out: float32 [4096, 2048], P(('dp', 'seq'))
- input_grad: float32 [4096, 2048], P(('dp', 'seq'))
- norm1_grad: float32 [2048], P(('dp', 'seq'))
- qkv_grad: float32 [2048, 6144], P(('dp', 'seq'))
- out_grad: float32 [2048, 2048], P(('dp', 'seq'))
- norm2_grad: float32 [2048], P(('dp', 'seq'))
- gate_up_grad: float32 [2048, 16384], P(('dp', 'seq'))
- down_grad: float32 [2048, 8192], P(('dp', 'seq'))
The draws below stay inside these ranges and needn't reach their ends.
All inputs are finite; a program needn't handle non-finite values.
Results may differ from the reference program's by a relative error of at most 0.018.
Values may be sent and summed in bfloat16 or wider, within the bound.
No kernel may reach another device: no remote copies, remote signals or barrier semaphores. Data moves between devices by JAX's collectives and lax.ppermute only.
A program may use at most 384 MiB of HBM per device.

```python
import jax
import jax.numpy as jnp
from jax import lax

D = 2048
H = 32
HD = 64
FF = 8192
LENGTH = 1024
SEQS = 4
TOKENS = 4096


def draw_qkv_weight(key, part):
    base_key = jax.random.fold_in(key, 11)
    value_key = jax.random.fold_in(key, 12)
    other_key = jax.random.fold_in(key, 13)
    base = jnp.clip(jax.random.normal(base_key, (D, D), jnp.float32), -6.0, 6.0) * D ** (-0.5)
    value_part = jnp.clip(jax.random.normal(value_key, (D, D), jnp.float32), -6.0, 6.0) * D ** (-0.5)
    query_part = base
    key_part = jnp.clip(jax.random.normal(other_key, (D, D), jnp.float32), -6.0, 6.0) * D ** (-0.5)
    return jnp.concatenate([query_part, key_part, value_part], 1).astype(jnp.bfloat16)


def strengthened(values, stream_key, source, target, parts, factor):
    def block_of(position):
        return (jnp.arange(values.shape[position]) // (values.shape[position] // parts)).reshape((-1,) + (1,) * (values.ndim - 1 - position))

    first = jax.random.permutation(stream_key, parts)[block_of(target)]
    far = (block_of(target) + parts // 2) % parts
    return jnp.where((block_of(source) == first) | (block_of(source) == far), factor * values, values)


def block_scale(stream_key, shape, cuts, low, largest):
    loudness = 1.0
    for position, shards_of in cuts:
        draws = jax.random.uniform(jax.random.fold_in(jax.random.fold_in(stream_key, 6), position), (shards_of,), jnp.float32, low / len(cuts), largest / len(cuts))
        loudness = loudness * jnp.repeat(jnp.exp(draws), shape[position] // shards_of).reshape((-1,) + (1,) * (len(shape) - 1 - position))
    return loudness


def gaussian(key, shape, width, bound, shards=(), dtype=jnp.bfloat16):
    array = jax.random.normal(key, shape, jnp.float32) * width
    if len(shards) > 0:
        array = block_scale(key, shape, shards, -0.22, 0.18) * array
    return jnp.clip(array, min=-bound, max=bound).astype(dtype)


def noise_with(own_key, dims, scale, bound, cuts, heavy, dtype=jnp.bfloat16):
    drawn = scale * jax.random.normal(own_key, dims, jnp.float32)
    if cuts:
        drawn = drawn * block_scale(own_key, dims, cuts, -0.22, 0.18)
    return jnp.clip(strengthened(drawn, jax.random.fold_in(own_key, 3), *heavy), -bound, bound).astype(dtype)


def setup_inputs(seed: int = 0) -> dict:
    seeds = jax.random.split(jax.random.key(seed), 9)
    layer_in = gaussian(seeds[0], (TOKENS, D), 1.0, 6.0, ((0, 32),), jnp.float32)
    norm1_gain = jnp.clip(1.0 + 0.15 * jax.random.normal(seeds[1], (D,), jnp.float32), 0.25, 1.75)
    qkv_weight = draw_qkv_weight(jax.random.fold_in(seeds[8], 71), 0)
    out_weight = gaussian(seeds[3], (D, D), (max(D // 256, 1)) ** -0.5, 2.0, ((0, 4),))
    norm2_gain = jnp.clip(1.0 + 0.15 * jax.random.normal(seeds[4], (D,), jnp.float32), 0.25, 1.75)
    gate_up_weight = gaussian(seeds[5], (D, 2 * FF), D ** -0.5, 0.125, ((0, 4),))
    down_weight = gaussian(seeds[6], (D, FF), FF ** -0.5, 0.0625, ((0, 4),))
    cotangent = noise_with(seeds[7], (TOKENS, D), 1.0, 6.0, ((0, 32),), (0, 1, 32, 2.75), jnp.float32)
    return {"layer_in": layer_in, "norm1_gain": norm1_gain, "qkv_weight": qkv_weight, "out_weight": out_weight, "norm2_gain": norm2_gain, "gate_up_weight": gate_up_weight, "down_weight": down_weight, "cotangent": cotangent}


EPS = 1e-05
THETA = 130000.0

def rotary_tables(length, head_dim):
    half_dim = head_dim // 2
    inverse = THETA ** (-(jnp.arange(half_dim).astype(jnp.float32) * 2.0) / head_dim)
    angles = jnp.arange(length).astype(jnp.float32)[:, None] * inverse[None, :]
    cosine = jnp.cos(angles)
    sine = jnp.sin(angles)
    return (jnp.concatenate([cosine, cosine], 1), jnp.concatenate([sine, sine], 1))

def rotate(values, cosine, sine):
    half_dim = values.shape[-1] // 2
    turned = jnp.concatenate([-values[..., half_dim:], values[..., :half_dim]], -1)
    return values * cosine[:, None, :] + turned * sine[:, None, :]

def scores_for(queries, key_rot, first_row, length, score_scale):
    block_rows = queries.shape[0]
    raw_scores = jnp.einsum('qhd,khd->hqk', queries.astype(jnp.float32), key_rot.astype(jnp.float32)) * score_scale
    query_pos = first_row + jnp.arange(block_rows)
    key_pos = jnp.arange(length)
    allowed = key_pos[None, :] <= query_pos[:, None]
    return jnp.where(allowed[None], raw_scores, -1e+30)

def attend_forward(query_rot, key_rot, value_heads):
    length, head_count, head_dim = query_rot.shape
    block_rows = min(512, length)
    score_scale = head_dim ** (-0.5)

    def one_block(block_index):
        first_row = block_index * block_rows
        queries = lax.dynamic_slice_in_dim(query_rot, first_row, block_rows, 0)
        scores = scores_for(queries, key_rot, first_row, length, score_scale)
        row_max = lax.optimization_barrier(jnp.max(scores, axis=2, keepdims=True))
        row_total = lax.optimization_barrier(jnp.sum(jnp.exp(scores - row_max), axis=2, keepdims=True))
        log_total = row_max + jnp.log(row_total)
        prob_low = jnp.exp(scores - log_total).astype(jnp.bfloat16)
        mixed = jnp.einsum('hqk,khd->qhd', prob_low.astype(jnp.float32), value_heads.astype(jnp.float32))
        return (mixed.astype(jnp.bfloat16), log_total[:, :, 0])
    mixed, log_total = lax.map(one_block, jnp.arange(length // block_rows))
    return (mixed.reshape(length, head_count, head_dim), log_total)

def attend_backward(query_rot, key_rot, value_heads, mixed, log_total, grad_mixed):
    length, head_count, head_dim = query_rot.shape
    block_rows = min(512, length)
    score_scale = head_dim ** (-0.5)
    row_delta = lax.optimization_barrier(jnp.sum(grad_mixed.astype(jnp.float32) * mixed.astype(jnp.float32), axis=2))

    def one_block(carry, block_index):
        grad_keys, grad_values = carry
        first_row = block_index * block_rows
        queries = lax.dynamic_slice_in_dim(query_rot, first_row, block_rows, 0)
        grad_rows = lax.dynamic_slice_in_dim(grad_mixed, first_row, block_rows, 0).astype(jnp.float32)
        delta_rows = lax.dynamic_slice_in_dim(row_delta, first_row, block_rows, 0)
        scores = scores_for(queries, key_rot, first_row, length, score_scale)
        probs = jnp.exp(scores - log_total[block_index][:, :, None])
        prob_low = probs.astype(jnp.bfloat16).astype(jnp.float32)
        grad_values = grad_values + jnp.einsum('hqk,qhd->khd', prob_low, grad_rows)
        grad_probs = jnp.einsum('qhd,khd->hqk', grad_rows, value_heads.astype(jnp.float32))
        grad_scores = (score_scale * probs * (grad_probs - delta_rows.T[:, :, None])).astype(jnp.bfloat16)
        grad_scores = grad_scores.astype(jnp.float32)
        grad_queries = jnp.einsum('hqk,khd->qhd', grad_scores, key_rot.astype(jnp.float32))
        grad_keys = grad_keys + jnp.einsum('hqk,qhd->khd', grad_scores, queries.astype(jnp.float32))
        return ((grad_keys, grad_values), grad_queries)
    empty = jnp.zeros((length, head_count, head_dim), jnp.float32)
    (grad_keys, grad_values), grad_queries = lax.scan(one_block, (empty, empty), jnp.arange(length // block_rows))
    return (grad_queries.reshape(length, head_count, head_dim), grad_keys, grad_values)

def norm_backward(grad_normed, normed, gain, inv_rms):
    grad_hat = grad_normed * gain
    return inv_rms * (grad_hat - normed * lax.optimization_barrier(jnp.mean(grad_hat * normed, axis=1, keepdims=True)))

def reference(layer_in, norm1_gain, qkv_weight, out_weight, norm2_gain, gate_up_weight, down_weight, cotangent):
    model_width = layer_in.shape[1]
    length = LENGTH
    hidden_units = down_weight.shape[1]
    cosine, sine = rotary_tables(length, HD)
    seq_in = layer_in.reshape(SEQS, length, model_width)
    seq_grad = cotangent.reshape(SEQS, length, model_width)

    def one_sequence(totals, inputs):
        resid, grad_out = inputs
        inv_rms1 = lax.rsqrt(lax.optimization_barrier(jnp.mean(resid * resid, axis=1, keepdims=True)) + EPS)
        normed1 = resid * inv_rms1
        xn_first = (normed1 * norm1_gain).astype(jnp.bfloat16)
        qkv_low = jnp.dot(xn_first, qkv_weight, preferred_element_type=jnp.float32).astype(jnp.bfloat16)
        head_qkv = qkv_low.reshape(length, 3, H, HD)
        query_rot = rotate(head_qkv[:, 0].astype(jnp.float32), cosine, sine).astype(jnp.bfloat16)
        key_rot = rotate(head_qkv[:, 1].astype(jnp.float32), cosine, sine).astype(jnp.bfloat16)
        value_heads = head_qkv[:, 2]
        mixed, log_total = attend_forward(query_rot, key_rot, value_heads)
        attn_low = mixed.reshape(length, model_width)
        hidden_res = resid + jnp.dot(attn_low, out_weight, preferred_element_type=jnp.float32)
        inv_rms2 = lax.rsqrt(lax.optimization_barrier(jnp.mean(hidden_res * hidden_res, axis=1, keepdims=True)) + EPS)
        normed2 = hidden_res * inv_rms2
        xn_second = (normed2 * norm2_gain).astype(jnp.bfloat16)
        gate_up = jnp.dot(xn_second, gate_up_weight, preferred_element_type=jnp.float32)
        gate = gate_up[:, :hidden_units]
        up_part = gate_up[:, hidden_units:]
        sigmoid_gate = jax.nn.sigmoid(gate)
        act_low = (gate * sigmoid_gate * up_part).astype(jnp.bfloat16)
        layer_out = hidden_res + jnp.dot(act_low, down_weight.T, preferred_element_type=jnp.float32)
        grad_low = grad_out.astype(jnp.bfloat16)
        grad_act = jnp.dot(grad_low, down_weight, preferred_element_type=jnp.float32)
        grad_gate = grad_act * up_part * sigmoid_gate * (1.0 + gate * (1.0 - sigmoid_gate))
        grad_up = grad_act * gate * sigmoid_gate
        grad_gate_up = jnp.concatenate([grad_gate, grad_up], 1).astype(jnp.bfloat16)
        grad_xn2 = jnp.dot(grad_gate_up, gate_up_weight.T, preferred_element_type=jnp.float32)
        norm2_term = lax.optimization_barrier(jnp.sum(grad_xn2 * normed2, axis=0))
        grad_hidden = grad_out + norm_backward(grad_xn2, normed2, norm2_gain, inv_rms2)
        hidden_low = grad_hidden.astype(jnp.bfloat16)
        grad_attn = jnp.dot(hidden_low, out_weight.T, preferred_element_type=jnp.float32).astype(jnp.bfloat16)
        grad_query, grad_key, grad_value = attend_backward(query_rot, key_rot, value_heads, mixed, log_total, grad_attn.reshape(length, H, HD))
        grad_query = rotate(grad_query, cosine, -sine)
        grad_key = rotate(grad_key, cosine, -sine)
        grad_qkv = jnp.stack([grad_query, grad_key, grad_value], 1).reshape(length, 3 * model_width).astype(jnp.bfloat16)
        grad_xn1 = jnp.dot(grad_qkv, qkv_weight.T, preferred_element_type=jnp.float32)
        norm1_term = lax.optimization_barrier(jnp.sum(grad_xn1 * normed1, axis=0))
        input_grad = grad_hidden + norm_backward(grad_xn1, normed1, norm1_gain, inv_rms1)
        terms = (norm1_term, jnp.dot(xn_first.T, grad_qkv, preferred_element_type=jnp.float32), jnp.dot(attn_low.T, hidden_low, preferred_element_type=jnp.float32), norm2_term, jnp.dot(xn_second.T, grad_gate_up, preferred_element_type=jnp.float32), jnp.dot(grad_low.T, act_low, preferred_element_type=jnp.float32))
        new_totals = jax.tree.map(lambda left, right: left + right, totals, terms)
        return (new_totals, (layer_out, input_grad))
    start_totals = (jnp.zeros((model_width,), jnp.float32), jnp.zeros((model_width, 3 * model_width), jnp.float32), jnp.zeros((model_width, model_width), jnp.float32), jnp.zeros((model_width,), jnp.float32), jnp.zeros((model_width, 2 * hidden_units), jnp.float32), jnp.zeros((model_width, hidden_units), jnp.float32))
    totals, outputs = lax.scan(one_sequence, start_totals, (seq_in, seq_grad))
    layer_out, input_grad = outputs
    layer_out = layer_out.reshape(-1, model_width)
    input_grad = input_grad.reshape(-1, model_width)
    return (layer_out, input_grad, totals[0], totals[1], totals[2], totals[3], totals[4], totals[5])
```

```python
import functools

import jax
import jax.numpy as jnp
from jax import lax
from jax.experimental import pallas as pl
from jax.experimental.pallas import tpu as pltpu
from jax.sharding import PartitionSpec as P

HD = 64
EPS = 1e-05
THETA = 130000.0
BF = jnp.bfloat16
F32 = jnp.float32

GRAY = (0, 1, 3, 2)


def rotary_tables(length):
    half = HD // 2
    inverse = THETA ** (-(jnp.arange(half).astype(F32) * 2.0) / HD)
    angles = jnp.arange(length).astype(F32)[:, None] * inverse[None, :]
    cosine = jnp.cos(angles)
    sine = jnp.sin(angles)
    return (
        jnp.concatenate([cosine] * 4, 1),
        jnp.concatenate([-sine, sine, -sine, sine], 1),
    )


def half_turn(values):
    lane = lax.broadcasted_iota(jnp.int32, values.shape, 1)
    upper = (lane & (HD // 2)) != 0
    return jnp.where(
        upper, pltpu.roll(values, HD // 2, 1), pltpu.roll(values, 128 - HD // 2, 1)
    )


def contract_last(left, right):
    return lax.dot_general(left, right, (((1,), (1,)), ((), ())), preferred_element_type=F32)


def contract_first(left, right):
    return lax.dot_general(left, right, (((0,), (0,)), ((), ())), preferred_element_type=F32)


def head_only(values, head):
    lane = lax.broadcasted_iota(jnp.int32, values.shape, 1)
    return jnp.where(lane // HD == head, values, jnp.zeros_like(values))


def causal(block):
    key_pos = lax.broadcasted_iota(jnp.int32, (block, block), 0)
    query_pos = lax.broadcasted_iota(jnp.int32, (block, block), 1)
    return key_pos <= query_pos


def attention_forward_kernel(
    block, qkv_ref, cos_ref, sin_ref, attn_ref, q_ref, k_ref, lse_ref, vt_ref, ot_ref
):
    head = pl.program_id(0)
    length, width = q_ref.shape
    scale = HD ** (-0.5)

    @pl.when(head == 0)
    def _():
        for c in range(width // 128):
            for source, target, factor in ((0, q_ref, scale), (width, k_ref, 1.0)):
                u = qkv_ref[:, source + c * 128 : source + (c + 1) * 128].astype(F32)
                turned = u * cos_ref[...] + half_turn(u) * sin_ref[...]
                target[:, c * 128 : (c + 1) * 128] = turned.astype(BF) * factor
            v = qkv_ref[:, 2 * width + c * 128 : 2 * width + (c + 1) * 128]
            vt_ref[c * 128 : (c + 1) * 128, :] = v.astype(F32).T.astype(BF)

    rows = pl.ds(pl.multiple_of(head * HD, HD), HD)
    for i in range(length // block):
        low, high = i * block, (i + 1) * block
        query = head_only(q_ref[low:high, :], head)
        near = contract_last(k_ref[low:high, :], query)
        near = jnp.where(causal(block), near, -1e30)
        top = jnp.max(near, axis=0, keepdims=True)
        if i:
            far = contract_last(k_ref[0:low, :], query)
            top = jnp.maximum(top, jnp.max(far, axis=0, keepdims=True))
        near = jnp.exp(near - top)
        total = jnp.sum(near, axis=0, keepdims=True)
        mixed = jnp.dot(vt_ref[rows, low:high], near.astype(BF), preferred_element_type=F32)
        if i:
            far = jnp.exp(far - top)
            total = total + jnp.sum(far, axis=0, keepdims=True)
            mixed = mixed + jnp.dot(
                vt_ref[rows, 0:low], far.astype(BF), preferred_element_type=F32
            )
        ot_ref[rows, low:high] = mixed / total
        lse_ref[pl.ds(head, 1), low:high] = top + jnp.log(total)

    @pl.when(head == pl.num_programs(0) - 1)
    def _():
        attn_ref[...] = ot_ref[...].T.astype(BF)


def attention_backward_kernel(
    block, q_ref, k_ref, qkv_ref, attn_ref, grad_ref, lse_ref, cos_ref, sin_ref,
    out_ref, dq_ref, dk_ref, dv_ref, delta_ref,
):
    head = pl.program_id(0)
    length, width = q_ref.shape
    scale = HD ** (-0.5)

    @pl.when(head == 0)
    def _():
        dq_ref[...] = jnp.zeros_like(dq_ref)
        dk_ref[...] = jnp.zeros_like(dk_ref)
        dv_ref[...] = jnp.zeros_like(dv_ref)
        product = grad_ref[...].astype(F32) * attn_ref[...].astype(F32)
        which = lax.broadcasted_iota(jnp.int32, (8, width), 0)
        lane = lax.broadcasted_iota(jnp.int32, (8, width), 1)
        picks = (lane // HD == which).astype(F32)
        delta_ref[...] = lax.dot_general(
            picks, product, (((1,), (1,)), ((), ())),
            precision=lax.Precision.HIGHEST, preferred_element_type=F32,
        )

    def piece(keys, low, high, query, grad, diagonal):
        values = qkv_ref[keys, 2 * width : 3 * width]
        prob = jnp.exp(contract_last(k_ref[keys, :], query) - lse_ref[pl.ds(head, 1), low:high])
        if diagonal:
            prob = jnp.where(causal(block), prob, 0.0)
        dprob = contract_last(values, grad)
        dscore = (prob * (dprob - delta_ref[pl.ds(head, 1), low:high])).astype(BF)
        dv_ref[keys, :] += jnp.dot(prob.astype(BF), grad, preferred_element_type=F32)
        dk_ref[keys, :] += jnp.dot(dscore, query, preferred_element_type=F32)
        dq_ref[low:high, :] += contract_first(dscore, head_only(k_ref[keys, :], head))

    for i in range(length // block):
        low, high = i * block, (i + 1) * block
        query = head_only(q_ref[low:high, :], head)
        grad = head_only(grad_ref[low:high, :], head)
        piece(slice(low, high), low, high, query, grad, True)
        if i:
            piece(slice(0, low), low, high, query, grad, False)

    @pl.when(head == pl.num_programs(0) - 1)
    def _():
        for c in range(width // 128):
            cols = slice(c * 128, (c + 1) * 128)
            for source, target, factor in ((dq_ref, 0, scale), (dk_ref, width, 1.0)):
                u = source[:, cols] * factor
                turned = u * cos_ref[...] - half_turn(u) * sin_ref[...]
                out_ref[:, target + c * 128 : target + (c + 1) * 128] = turned.astype(BF)
        out_ref[:, 2 * width : 3 * width] = dv_ref[...].astype(BF)


def whole(shape):
    return pl.BlockSpec(shape, lambda h: tuple(0 for _ in shape))


def attention_forward(qkv, cosine, sine):
    length, width = qkv.shape[0], qkv.shape[1] // 3
    heads = width // HD
    block = min(256, length)
    pairs = heads * length * length
    return pl.pallas_call(
        functools.partial(attention_forward_kernel, block),
        grid=(heads,),
        in_specs=[whole(qkv.shape), whole(cosine.shape), whole(sine.shape)],
        out_specs=[whole((length, width))] * 3 + [whole((8, length))],
        out_shape=[jax.ShapeDtypeStruct((length, width), BF)] * 3
        + [jax.ShapeDtypeStruct((8, length), F32)],
        scratch_shapes=[pltpu.VMEM((width, length), BF), pltpu.VMEM((width, length), F32)],
        cost_estimate=pl.CostEstimate(
            flops=2 * pairs * HD, bytes_accessed=8 * length * width, transcendentals=pairs // 2
        ),
        name="attention_forward",
    )(qkv, cosine, sine)


def attention_backward(query, key, qkv, attn, grad, lse, cosine, sine):
    length, width = query.shape
    heads = width // HD
    block = min(256, length)
    pairs = heads * length * length
    flat = whole((length, width))
    return pl.pallas_call(
        functools.partial(attention_backward_kernel, block),
        grid=(heads,),
        in_specs=[flat, flat, whole(qkv.shape), flat, flat, whole((8, length))]
        + [whole(cosine.shape)] * 2,
        out_specs=whole(qkv.shape),
        out_shape=jax.ShapeDtypeStruct(qkv.shape, BF),
        scratch_shapes=[pltpu.VMEM((length, width), F32)] * 3 + [pltpu.VMEM((8, length), F32)],
        cost_estimate=pl.CostEstimate(
            flops=5 * pairs * HD, bytes_accessed=20 * length * width, transcendentals=pairs // 2
        ),
        name="attention_backward",
    )(query, key, qkv, attn, grad, lse, cosine, sine)


def strided_heads_kernel(which_ref, first_ref, second_ref, out_ref):
    parity = which_ref[0] % 2

    @pl.when(parity == 0)
    def _():
        out_ref[...] = jnp.concatenate([first_ref[:, :HD], second_ref[:, :HD]], 1)

    @pl.when(parity == 1)
    def _():
        out_ref[...] = jnp.concatenate([first_ref[:, HD:], second_ref[:, HD:]], 1)


def strided_heads(weight, group, group_count):
    rows, columns = weight.shape
    run = group_count * HD // 128
    runs = columns // (group_count * HD)
    return pl.pallas_call(
        strided_heads_kernel,
        grid_spec=pltpu.PrefetchScalarGridSpec(
            num_scalar_prefetch=1,
            grid=(runs // 2,),
            in_specs=[
                pl.BlockSpec((rows, 128), lambda g, w: (0, 2 * g * run + w[0] // 2)),
                pl.BlockSpec((rows, 128), lambda g, w: (0, (2 * g + 1) * run + w[0] // 2)),
            ],
            out_specs=pl.BlockSpec((rows, 128), lambda g, w: (0, g)),
        ),
        out_shape=jax.ShapeDtypeStruct((rows, runs * HD), weight.dtype),
        name="strided_heads",
    )(group.reshape(1), weight, weight)


def partner(array, bits, count):
    return lax.ppermute(array, "dp", [(i, i ^ bits) for i in range(count)])


class Quad:
    def __init__(self, index):
        self.index = index

    def to_local(self, values):
        width = values.shape[1] // 4
        return jnp.concatenate(
            [
                lax.dynamic_slice_in_dim(values, (g ^ self.index) * width, width, 1)
                for g in GRAY
            ],
            1,
        )

    def to_global(self, values):
        width = values.shape[1] // 4
        pieces = []
        for j in range(4):
            k = self.index ^ j
            pieces.append(lax.dynamic_slice_in_dim(values, (k ^ (k >> 1)) * width, width, 1))
        return jnp.concatenate(pieces, 1)

    def gather_direct(self, block):
        return [block] + [partner(block, k, 4) for k in (1, 2, 3)]

    def gather_staged(self, first, second):
        a = {0: first, 1: partner(first, 1, 4)}
        b = {0: second, 2: partner(second, 2, 4)}
        a[2], b[1] = partner(a[0], 2, 4), partner(b[0], 1, 4)
        a[3], b[3] = partner(a[1], 2, 4), partner(b[2], 1, 4)
        return [a[k] for k in range(4)], [b[k] for k in range(4)]


def product_rows(left, right, low, high):
    return contract_first(left[:, low:high], right).astype(BF)


def add(*terms):
    total = terms[0].astype(F32)
    for term in terms[1:]:
        total = total + term.astype(F32)
    return total.astype(BF)


def reduce_x_then_y(left, right):
    rows = left.shape[1] // 4
    sent = partner(product_rows(left, right, rows, 3 * rows), 1, 4)
    keep_far = product_rows(left, right, 3 * rows, 4 * rows)
    keep = product_rows(left, right, 0, rows)
    far = partner(add(keep_far, sent[rows:]), 2, 4)
    return add(keep, sent[:rows], far)


def reduce_y_then_x(left, right):
    rows = left.shape[1] // 4
    sent = partner(product_rows(left, right, 2 * rows, 4 * rows), 2, 4)
    keep = product_rows(left, right, 0, 2 * rows)
    far = partner(add(keep[rows:], sent[:rows]), 1, 4)
    return add(keep[:rows], sent[rows:], far)


def reduce_direct(left, right):
    rows = left.shape[1] // 4
    own = product_rows(left, right, 0, rows)
    others = [
        partner(product_rows(left, right, p * rows, (p + 1) * rows), GRAY[p], 4)
        for p in (1, 2, 3)
    ]
    return add(own, *others)


def reduce_plain(left, right):
    return lax.psum_scatter(
        contract_first(left, right).astype(BF), "dp", scatter_dimension=0, tiled=True
    )


def over_seq(values):
    return lax.all_gather(values, "seq", axis=0, tiled=True)


def sum_over_seq(values):
    return lax.psum_scatter(values.astype(BF), "seq", scatter_dimension=0, tiled=True).astype(F32)


def exchange_rows(values, group_count):
    blocks = values.reshape(group_count, values.shape[0] // group_count, values.shape[1])
    return lax.all_to_all(blocks, "seq", split_axis=0, concat_axis=0, tiled=True)


def norm_backward(grad_normed, normed, gain, inv_rms):
    grad_hat = grad_normed * gain
    return inv_rms * (grad_hat - normed * jnp.mean(grad_hat * normed, axis=1, keepdims=True))


def join_gate_up(part_a, part_b, hidden):
    split = 2 * hidden - part_a[0].shape[1]
    order = GRAY
    gate_up = jnp.concatenate(
        [jnp.concatenate([part_a[k], part_b[k][:, :split]], 1) for k in order], 0
    )
    down = jnp.concatenate([part_b[k][:, split:] for k in order], 0)
    return gate_up, down


def shards(
    layer_in, norm1_gain, qkv_weight, out_weight, norm2_gain, gate_up_weight, down_weight, cotangent
):
    token_rows, model_width = layer_in.shape
    group_count = lax.axis_size("seq")
    dp_count = lax.axis_size("dp")
    group = lax.axis_index("seq")
    member = lax.axis_index("dp")
    length = token_rows * group_count
    dp_rows = model_width // dp_count
    shard_rows = dp_rows // group_count
    hidden_units = down_weight.shape[1]
    hidden = hidden_units // group_count
    width = model_width // group_count
    quad = Quad(member) if dp_count == 4 else None
    strided = quad is not None and shard_rows == HD and model_width == dp_count * group_count * HD

    def to_local(values):
        return quad.to_local(values) if quad else values

    def to_global(values):
        return quad.to_global(values) if quad else values

    inv_rms1 = lax.rsqrt(jnp.mean(layer_in * layer_in, axis=1, keepdims=True) + EPS)
    normed1 = layer_in * inv_rms1
    xn1 = over_seq(to_local((normed1 * norm1_gain).astype(BF)))

    if strided:
        qkv_piece = strided_heads(qkv_weight, group, group_count)
        out_piece = lax.dynamic_slice_in_dim(out_weight, group * HD, HD, 0)
        blocks = quad.gather_direct(qkv_piece)
        qkv_full = jnp.concatenate([blocks[k] for k in GRAY], 0)
        out_blocks = jnp.stack(quad.gather_direct(out_piece))
        out_full = jnp.concatenate(
            [lax.dynamic_index_in_dim(out_blocks, member ^ j, 0, False) for j in range(4)], 0
        )
    else:
        qkv_piece = lax.dynamic_slice_in_dim(
            qkv_weight.reshape(dp_rows, 3, model_width), group * width, width, 2
        ).reshape(dp_rows, 3 * width)
        qkv_full = lax.all_gather(qkv_piece, "dp", axis=0, tiled=True)
        if quad:
            qkv_full = jnp.concatenate(
                [
                    lax.dynamic_slice_in_dim(qkv_full, (g ^ member) * dp_rows, dp_rows, 0)
                    for g in GRAY
                ],
                0,
            )
        out_full = lax.dynamic_slice_in_dim(
            lax.all_gather(out_weight, "dp", axis=0, tiled=True), group * width, width, 0
        )

    def hidden_columns(weight, start):
        return lax.dynamic_slice_in_dim(weight, start + group * hidden, hidden, 1)

    gate_piece = hidden_columns(gate_up_weight, 0)
    up_piece = hidden_columns(gate_up_weight, hidden_units)
    down_piece = hidden_columns(down_weight, 0)
    if quad:
        half = hidden // 2
        part_a = jnp.concatenate([gate_piece, up_piece[:, :half]], 1)
        part_b = jnp.concatenate([up_piece[:, half:], down_piece], 1)
        part_a, part_b, _ = lax.optimization_barrier((part_a, part_b, qkv_full))
        gate_up_full, down_full = join_gate_up(*quad.gather_staged(part_a, part_b), hidden)
    else:
        gate_up_full = lax.all_gather(
            jnp.concatenate([gate_piece, up_piece], 1), "dp", axis=0, tiled=True
        )
        down_full = lax.all_gather(down_piece, "dp", axis=0, tiled=True)

    cosine, sine = rotary_tables(length)
    qkv = jnp.dot(xn1, qkv_full, preferred_element_type=F32).astype(BF)
    attn, query, key, lse = attention_forward(qkv, cosine, sine)
    dy = over_seq(to_local(cotangent.astype(BF)))
    hidden_res = layer_in + sum_over_seq(jnp.dot(attn, out_full, preferred_element_type=F32))

    inv_rms2 = lax.rsqrt(jnp.mean(hidden_res * hidden_res, axis=1, keepdims=True) + EPS)
    normed2 = hidden_res * inv_rms2
    xn2 = over_seq(to_local((normed2 * norm2_gain).astype(BF)))
    gate_up = jnp.dot(xn2, gate_up_full, preferred_element_type=F32)
    gate = gate_up[:, :hidden]
    up_part = gate_up[:, hidden:]
    sigmoid_gate = jax.nn.sigmoid(gate)
    act = (gate * sigmoid_gate * up_part).astype(BF)

    grad_act = jnp.dot(dy, down_full, preferred_element_type=F32)
    grad_gate = grad_act * up_part * sigmoid_gate * (1.0 + gate * (1.0 - sigmoid_gate))
    grad_up = grad_act * gate * sigmoid_gate
    grad_gate_up = jnp.concatenate([grad_gate, grad_up], 1).astype(BF)
    grad_xn2 = to_global(sum_over_seq(contract_last(grad_gate_up, gate_up_full)))
    grad_hidden = cotangent + norm_backward(grad_xn2, normed2, norm2_gain, inv_rms2)
    hidden_low = over_seq(grad_hidden.astype(BF))
    layer_out = hidden_res + to_global(sum_over_seq(contract_last(act, down_full)))

    grad_attn = contract_last(hidden_low, out_full).astype(BF)
    grad_qkv = attention_backward(query, key, qkv, attn, grad_attn, lse, cosine, sine)
    grad_xn1 = to_global(sum_over_seq(contract_last(grad_qkv, qkv_full)))
    input_grad = grad_hidden + norm_backward(grad_xn1, normed1, norm1_gain, inv_rms1)

    if quad:
        cut = 2 * hidden - hidden // 2
        feed = jnp.concatenate(
            [
                reduce_x_then_y(xn2, grad_gate_up[:, :cut]),
                reduce_y_then_x(xn2, grad_gate_up[:, cut:]),
                reduce_y_then_x(dy, act),
            ],
            1,
        )
        qkv_rows = reduce_direct(xn1, grad_qkv)
    else:
        feed = jnp.concatenate(
            [reduce_plain(xn2, grad_gate_up), reduce_plain(dy, act)], 1
        )
        qkv_rows = reduce_plain(xn1, grad_qkv)
    out_partial = contract_first(attn, hidden_low).astype(BF)
    if strided:
        stacked = out_partial.reshape(4, HD, model_width)
        own = lax.dynamic_index_in_dim(stacked, member, 0, False)
        others = [
            partner(lax.dynamic_index_in_dim(stacked, member ^ k, 0, False), k, 4)
            for k in (1, 2, 3)
        ]
        out_grad = sum((o.astype(F32) for o in others), own.astype(F32))
    else:
        spread = lax.dynamic_update_slice_in_dim(
            jnp.zeros((model_width, model_width), BF), out_partial, group * width, 0
        )
        out_grad = lax.psum_scatter(
            lax.psum_scatter(spread, "dp", scatter_dimension=0, tiled=True),
            "seq", scatter_dimension=0, tiled=True,
        ).astype(F32)

    feed = exchange_rows(feed, group_count)

    def columns(low, high):
        return feed[:, :, low:high].astype(F32).transpose(1, 0, 2).reshape(shard_rows, hidden_units)

    gate_up_grad = jnp.concatenate([columns(0, hidden), columns(hidden, 2 * hidden)], 1)
    down_grad = columns(2 * hidden, 3 * hidden)
    qkv_rows = exchange_rows(qkv_rows, group_count).astype(F32)
    if strided:
        qkv_grad = (
            qkv_rows.reshape(group_count, shard_rows, 3 * dp_count, HD)
            .transpose(1, 2, 0, 3)
            .reshape(shard_rows, 3 * model_width)
        )
    else:
        qkv_grad = (
            qkv_rows.reshape(group_count, shard_rows, 3, width)
            .transpose(1, 2, 0, 3)
            .reshape(shard_rows, 3 * model_width)
        )

    def gain_grad(grad, weight, gain):
        rows = lax.dynamic_slice_in_dim(weight, group * shard_rows, shard_rows, 0)
        own_gain = lax.dynamic_slice_in_dim(gain, member * dp_rows + group * shard_rows, shard_rows, 0)
        return jnp.sum(grad * rows.astype(F32), axis=1) / own_gain

    return (
        layer_out,
        input_grad,
        gain_grad(qkv_grad, qkv_weight, norm1_gain),
        qkv_grad,
        out_grad,
        gain_grad(gate_up_grad, gate_up_weight, norm2_gain),
        gate_up_grad,
        down_grad,
    )


def solution(mesh):
    rows = P(("dp", "seq"), None)
    in_specs = (
        rows, P(), P("dp", None), P("dp", None), P(), P("dp", None), P("dp", None), rows,
    )
    vector = P(("dp", "seq"))
    out_specs = (rows, rows, vector, rows, rows, vector, rows, rows)
    return jax.shard_map(shards, mesh=mesh, in_specs=in_specs, out_specs=out_specs, check_vma=False)
```

```python
import functools

import jax
import jax.numpy as jnp
from jax import lax
from jax.experimental import pallas as pl
from jax.experimental.pallas import tpu as pltpu
from jax.sharding import PartitionSpec as P


HD = 64
EPS = 1e-05
THETA = 130000.0
BF = jnp.bfloat16
F32 = jnp.float32

GRAY = (0, 1, 3, 2)


def after(values, *earlier):
    return lax.optimization_barrier((values, *earlier))[0]


def rotary_tables(length):
    half = HD // 2
    inverse = THETA ** (-(jnp.arange(half).astype(F32) * 2.0) / HD)
    angles = jnp.arange(length).astype(F32)[:, None] * inverse[None, :]
    cosine = jnp.cos(angles)
    sine = jnp.sin(angles)
    return (
        jnp.concatenate([cosine] * 4, 1),
        jnp.concatenate([-sine, sine, -sine, sine], 1),
    )


def contract_last(left, right):
    return lax.dot_general(left, right, (((1,), (1,)), ((), ())), preferred_element_type=F32)


def contract_first(left, right):
    return lax.dot_general(left, right, (((0,), (0,)), ((), ())), preferred_element_type=F32)


def half_turn(values):
    lane = lax.broadcasted_iota(jnp.int32, values.shape, 1)
    upper = (lane & (HD // 2)) != 0
    return jnp.where(
        upper, pltpu.roll(values, HD // 2, 1), pltpu.roll(values, 128 - HD // 2, 1)
    )


def head_only(values, head):
    lane = lax.broadcasted_iota(jnp.int32, values.shape, 1)
    return jnp.where(lane // HD == head, values, jnp.zeros_like(values))


def causal(block):
    key_pos = lax.broadcasted_iota(jnp.int32, (block, block), 0)
    query_pos = lax.broadcasted_iota(jnp.int32, (block, block), 1)
    return key_pos <= query_pos


def assembled(pieces, per_row, target_ref, sems):
    copies, row = [], 0
    for first in range(0, len(pieces), per_row):
        column = 0
        for piece in pieces[first : first + per_row]:
            rows, columns = piece.shape
            place = target_ref.at[pl.ds(row, rows), pl.ds(column, columns)]
            copies.append(pltpu.make_async_copy(piece, place, sems.at[len(copies)]))
            column += columns
        row += rows
    return copies


def attention_forward_kernel(block, count, per_row, xn_ref, *refs):
    pieces, refs = refs[:count], refs[count:]
    cos_ref, sin_ref, attn_ref, q_ref, k_ref, v_ref, lse_ref, weight_ref, vt_ref, sems = refs
    head = pl.program_id(0)
    length, width = q_ref.shape
    tokens = attn_ref.shape[3]
    scale = HD ** (-0.5)

    @pl.when(head == 0)
    def _():
        copies = assembled(pieces, per_row, weight_ref, sems)
        for copy in copies:
            copy.start()
        for copy in copies:
            copy.wait()

        @pl.loop(0, length // block)
        def _(i):
            at = pl.ds(pl.multiple_of(i * block, block), block)
            qkv = jnp.dot(xn_ref[at, :], weight_ref[...], preferred_element_type=F32).astype(BF)
            v_ref[at, :] = qkv[:, 2 * width :]
            for c in range(width // 128):
                for source, target, factor in ((0, q_ref, scale), (width, k_ref, 1.0)):
                    u = qkv[:, source + c * 128 : source + (c + 1) * 128].astype(F32)
                    turned = u * cos_ref[at, :] + half_turn(u) * sin_ref[at, :]
                    target[at, c * 128 : (c + 1) * 128] = turned.astype(BF) * factor

        for c in range(width // 128):
            cols = slice(c * 128, (c + 1) * 128)
            vt_ref[cols, :] = v_ref[:, cols].astype(F32).T.astype(BF)

    rows = pl.ds(pl.multiple_of(head * HD, HD), HD)
    for i in range(length // block):
        low, high = i * block, (i + 1) * block
        query = head_only(q_ref[low:high, :], head)
        near = contract_last(k_ref[low:high, :], query)
        near = jnp.where(causal(block), near, -1e30)
        top = jnp.max(near, axis=0, keepdims=True)
        if i:
            far = contract_last(k_ref[0:low, :], query)
            top = jnp.maximum(top, jnp.max(far, axis=0, keepdims=True))
        near = jnp.exp(near - top)
        total = jnp.sum(near, axis=0, keepdims=True)
        mixed = jnp.dot(vt_ref[rows, low:high], near.astype(BF), preferred_element_type=F32)
        if i:
            far = jnp.exp(far - top)
            total = total + jnp.sum(far, axis=0, keepdims=True)
            mixed = mixed + jnp.dot(
                vt_ref[rows, 0:low], far.astype(BF), preferred_element_type=F32
            )
        mixed = (mixed / total).astype(BF)
        for part in range(block // tokens):
            attn_ref[head, low // tokens + part] = mixed[:, part * tokens : (part + 1) * tokens]
        lse_ref[pl.ds(head, 1), low:high] = top + jnp.log(total)


def attention_backward_kernel(
    block, count, per_row, q_ref, k_ref, v_ref, attn_ref, grad_ref, lse_ref, cos_ref, sin_ref, *refs
):
    pieces, refs = refs[:count], refs[count:]
    out_ref, dxn_ref, weight_ref, dq_ref, dk_ref, dv_ref, delta_ref, flat_ref, sems = refs
    head = pl.program_id(0)
    length, width = q_ref.shape
    tokens = attn_ref.shape[3]
    scale = HD ** (-0.5)

    @pl.when(head == 0)
    def _():
        for copy in assembled(pieces, per_row, weight_ref, sems):
            copy.start()
        dq_ref[...] = jnp.zeros_like(dq_ref)
        dk_ref[...] = jnp.zeros_like(dk_ref)
        dv_ref[...] = jnp.zeros_like(dv_ref)
        for c in range(width // 128):
            for j in range(length // tokens):
                pair = jnp.concatenate([grad_ref[2 * c, j], grad_ref[2 * c + 1, j]], 0)
                flat_ref[j * tokens : (j + 1) * tokens, c * 128 : (c + 1) * 128] = (
                    pair.astype(F32).T.astype(BF)
                )

    for j in range(length // tokens):
        product = grad_ref[head, j].astype(F32) * attn_ref[head, j].astype(F32)
        delta_ref[:, j * tokens : (j + 1) * tokens] = jnp.sum(product, axis=0, keepdims=True)

    def piece(keys, low, high, query, grad, diagonal):
        prob = jnp.exp(contract_last(k_ref[keys, :], query) - lse_ref[pl.ds(head, 1), low:high])
        if diagonal:
            prob = jnp.where(causal(block), prob, 0.0)
        dprob = contract_last(v_ref[keys, :], grad)
        dscore = (prob * (dprob - delta_ref[:, low:high])).astype(BF)
        dv_ref[keys, :] += jnp.dot(prob.astype(BF), grad, preferred_element_type=F32)
        dk_ref[keys, :] += jnp.dot(dscore, query, preferred_element_type=F32)
        dq_ref[low:high, :] += contract_first(dscore, head_only(k_ref[keys, :], head))

    for i in range(length // block):
        low, high = i * block, (i + 1) * block
        query = head_only(q_ref[low:high, :], head)
        grad = head_only(flat_ref[low:high, :], head)
        piece(slice(low, high), low, high, query, grad, True)
        if i:
            piece(slice(0, low), low, high, query, grad, False)

    @pl.when(head == pl.num_programs(0) - 1)
    def _():
        for copy in assembled(pieces, per_row, weight_ref, sems):
            copy.wait()

        @pl.loop(0, length // block)
        def _(i):
            at = pl.ds(pl.multiple_of(i * block, block), block)
            for c in range(width // 128):
                cols = slice(c * 128, (c + 1) * 128)
                for source, target, factor in ((dq_ref, 0, scale), (dk_ref, width, 1.0)):
                    u = source[at, cols] * factor
                    turned = u * cos_ref[at, :] - half_turn(u) * sin_ref[at, :]
                    out_ref[at, target + c * 128 : target + (c + 1) * 128] = turned.astype(BF)
            out_ref[at, 2 * width : 3 * width] = dv_ref[at, :].astype(BF)
            dxn_ref[at, :] = contract_last(out_ref[at, :], weight_ref[...]).astype(BF)


def resident(shape):
    return pl.BlockSpec(shape, lambda h: tuple(0 for _ in shape))


def attention_forward(xn, pieces, per_row, cosine, sine, tokens):
    length, model_width = xn.shape
    width = sum(piece.shape[1] for piece in pieces[:per_row]) // 3
    heads = width // HD
    block = min(256, length)
    pairs = heads * length * length
    out = (heads, length // tokens, HD, tokens)
    return pl.pallas_call(
        functools.partial(attention_forward_kernel, block, len(pieces), per_row),
        grid=(heads,),
        in_specs=[resident(xn.shape)]
        + [pl.BlockSpec(memory_space=pl.ANY)] * len(pieces)
        + [resident(cosine.shape)] * 2,
        out_specs=[resident(out)] + [resident((length, width))] * 3 + [resident((8, length))],
        out_shape=[jax.ShapeDtypeStruct(out, BF)]
        + [jax.ShapeDtypeStruct((length, width), BF)] * 3
        + [jax.ShapeDtypeStruct((8, length), F32)],
        scratch_shapes=[
            pltpu.VMEM((model_width, 3 * width), BF),
            pltpu.VMEM((width, length), BF),
            pltpu.SemaphoreType.DMA((len(pieces),)),
        ],
        cost_estimate=pl.CostEstimate(
            flops=2 * pairs * HD + 6 * length * model_width * width,
            bytes_accessed=8 * length * width + 2 * model_width * (length + 3 * width),
            transcendentals=pairs // 2,
        ),
        name="attention_forward",
    )(xn, *pieces, cosine, sine)


def attention_backward(query, key, value, attn, grad, lse, cosine, sine, pieces, per_row):
    length, width = query.shape
    model_width = sum(piece.shape[0] for piece in pieces[::per_row])
    heads = width // HD
    block = min(256, length)
    pairs = heads * length * length
    flat = resident((length, width))
    return pl.pallas_call(
        functools.partial(attention_backward_kernel, block, len(pieces), per_row),
        grid=(heads,),
        in_specs=[flat, flat, flat, resident(attn.shape), resident(attn.shape)]
        + [resident((8, length))]
        + [resident(cosine.shape)] * 2
        + [pl.BlockSpec(memory_space=pl.ANY)] * len(pieces),
        out_specs=[resident((length, 3 * width)), resident((length, model_width))],
        out_shape=[
            jax.ShapeDtypeStruct((length, 3 * width), BF),
            jax.ShapeDtypeStruct((length, model_width), BF),
        ],
        scratch_shapes=[pltpu.VMEM((model_width, 3 * width), BF)]
        + [pltpu.VMEM((length, width), F32)] * 3
        + [
            pltpu.VMEM((1, length), F32),
            pltpu.VMEM((length, width), BF),
            pltpu.SemaphoreType.DMA((len(pieces),)),
        ],
        cost_estimate=pl.CostEstimate(
            flops=5 * pairs * HD + 6 * length * model_width * width,
            bytes_accessed=20 * length * width + 2 * model_width * (length + 3 * width),
            transcendentals=pairs // 2,
        ),
        name="attention_backward",
    )(query, key, value, attn, grad, lse, cosine, sine, *pieces)


def strided_heads_kernel(which_ref, *refs):
    runs, outs = refs[:-2], refs[-2:]
    parity = which_ref[0] % 2
    half = len(runs) // 2

    for odd in range(2):

        @pl.when(parity == odd)
        def _():
            cols = slice(odd * HD, (odd + 1) * HD)
            for out, first in zip(outs, (0, half)):
                for r in range(0, half, 2):
                    out[:, r * HD : (r + 2) * HD] = jnp.concatenate(
                        [runs[first + r][:, cols], runs[first + r + 1][:, cols]], 1
                    )


def strided_heads(weight, group, group_count):
    rows, columns = weight.shape
    run = group_count * HD // 128
    runs = columns // (group_count * HD)

    def spec(r):
        return pl.BlockSpec((rows, 128), lambda g, w: (0, r * run + w[0] // 2))

    half = (rows, runs // 2 * HD)
    return pl.pallas_call(
        strided_heads_kernel,
        grid_spec=pltpu.PrefetchScalarGridSpec(
            num_scalar_prefetch=1,
            grid=(1,),
            in_specs=[spec(r) for r in range(runs)],
            out_specs=[pl.BlockSpec(half, lambda g, w: (0, 0))] * 2,
        ),
        out_shape=[jax.ShapeDtypeStruct(half, weight.dtype)] * 2,
        name="strided_heads",
    )(group.reshape(1), *[weight] * runs)


def strided_rows_kernel(which_ref, in_ref, weight_ref, out_ref, sum_ref):
    groups, rows, width = in_ref.shape
    total = jnp.zeros((rows, 128), F32)
    for b in range(width // HD):
        cols = slice(b * HD, (b + 1) * HD)
        for pair in range(groups // 2):
            both = jnp.concatenate(
                [in_ref[2 * pair, :, cols], in_ref[2 * pair + 1, :, cols]], 1
            ).astype(F32)
            at = (b * groups + 2 * pair) * HD
            out_ref[:, at : at + 128] = both
            total = total + both * weight_ref[:, at : at + 128].astype(F32)
    sum_ref[...] = jnp.broadcast_to(jnp.sum(total, axis=1, keepdims=True), sum_ref.shape)


def strided_rows(parts, weight, group):
    _, rows, _ = parts.shape
    return pl.pallas_call(
        strided_rows_kernel,
        grid_spec=pltpu.PrefetchScalarGridSpec(
            num_scalar_prefetch=1,
            grid=(1,),
            in_specs=[
                pl.BlockSpec(parts.shape, lambda g, w: (0, 0, 0)),
                pl.BlockSpec((rows, weight.shape[1]), lambda g, w: (w[0], 0)),
            ],
            out_specs=[
                pl.BlockSpec((rows, weight.shape[1]), lambda g, w: (0, 0)),
                pl.BlockSpec((rows, 128), lambda g, w: (0, 0)),
            ],
        ),
        out_shape=[
            jax.ShapeDtypeStruct((rows, weight.shape[1]), F32),
            jax.ShapeDtypeStruct((rows, 128), F32),
        ],
        name="strided_rows",
    )(group.reshape(1), parts, weight)


def side_rows_kernel(runs, which_ref, *refs):
    parts, (weight_ref, out_ref, sum_ref) = refs[:runs], refs[runs:]
    groups, rows, piece = parts[0].shape

    @pl.when(pl.program_id(0) == 0)
    def _():
        sum_ref[...] = jnp.zeros_like(sum_ref)

    for run in range(runs):

        @pl.when(pl.program_id(0) == run)
        def _():
            total = jnp.zeros((rows, 128), F32)
            for s in range(groups):
                values = parts[run][s].astype(F32)
                cols = slice(s * piece, (s + 1) * piece)
                out_ref[:, cols] = values
                product = values * weight_ref[:, cols].astype(F32)
                for c in range(piece // 128):
                    total = total + product[:, c * 128 : (c + 1) * 128]
            sum_ref[...] += jnp.broadcast_to(jnp.sum(total, axis=1, keepdims=True), sum_ref.shape)


def side_rows(parts, weight, group):
    groups, rows, piece = parts[0].shape
    runs = len(parts)
    return pl.pallas_call(
        functools.partial(side_rows_kernel, runs),
        grid_spec=pltpu.PrefetchScalarGridSpec(
            num_scalar_prefetch=1,
            grid=(runs,),
            in_specs=[pl.BlockSpec((groups, rows, piece), lambda c, w: (0, 0, 0))] * runs
            + [pl.BlockSpec((rows, groups * piece), lambda c, w: (w[0], c))],
            out_specs=[
                pl.BlockSpec((rows, groups * piece), lambda c, w: (0, c)),
                pl.BlockSpec((rows, 128), lambda c, w: (0, 0)),
            ],
        ),
        out_shape=[
            jax.ShapeDtypeStruct((rows, runs * groups * piece), F32),
            jax.ShapeDtypeStruct((rows, 128), F32),
        ],
        name="side_rows",
    )(group.reshape(1), *parts, weight)


def at_block(ref, index):
    width = ref.shape[1] // BLOCKS
    return ref.at[:, pl.ds(pl.multiple_of(index * width, width), width)]


BLOCKS = 4


def norm_in_kernel(orders_ref, x_ref, gain_ref, grad_ref, xn_ref, dy_ref):
    x = x_ref[...]
    inv = lax.rsqrt(jnp.mean(x * x, axis=1, keepdims=True) + EPS)
    for p in range(BLOCKS):
        block = orders_ref[p]
        normed = at_block(x_ref, block)[...] * inv * at_block(gain_ref, block)[...]
        at_block(xn_ref, p)[...] = normed.astype(BF)
        at_block(dy_ref, p)[...] = at_block(grad_ref, block)[...].astype(BF)


def norm_mid_kernel(orders_ref, x_ref, own_ref, *refs):
    others, (gain_ref, mid_ref, xn_ref) = refs[:-3], refs[-3:]
    mid = x_ref[...] + own_ref[...]
    for other in others:
        mid = mid + other[...].astype(F32)
    mid_ref[...] = mid
    inv = lax.rsqrt(jnp.mean(mid * mid, axis=1, keepdims=True) + EPS)
    for p in range(BLOCKS):
        block = orders_ref[p]
        normed = at_block(mid_ref, block)[...] * inv * at_block(gain_ref, block)[...]
        at_block(xn_ref, p)[...] = normed.astype(BF)


def norm_grad_kernel(places_ref, x_ref, base_ref, grad_ref, gain_ref, out_ref, *low_ref):
    x = x_ref[...]
    inv = lax.rsqrt(jnp.mean(x * x, axis=1, keepdims=True) + EPS)
    grad = jnp.concatenate(
        [at_block(grad_ref, places_ref[j])[...] for j in range(BLOCKS)], 1
    ).astype(F32)
    normed = x * inv
    grad_hat = grad * gain_ref[...]
    mean = jnp.mean(grad_hat * normed, axis=1, keepdims=True)
    out = base_ref[...] + inv * (grad_hat - normed * mean)
    out_ref[...] = out
    for ref in low_ref:
        ref[...] = out.astype(BF)


def add_placed_kernel(places_ref, base_ref, part_ref, out_ref):
    for j in range(BLOCKS):
        part = at_block(part_ref, places_ref[j])[...].astype(F32)
        at_block(out_ref, j)[...] = at_block(base_ref, j)[...] + part


def on_rows(kernel, table, inputs, out_types):
    rows, width = inputs[0].shape
    block = rows

    def spec(shape):
        if shape[0] == 1:
            return pl.BlockSpec(shape, lambda i, t: (0, 0))
        return pl.BlockSpec((block, width), lambda i, t: (i, 0))

    return pl.pallas_call(
        kernel,
        grid_spec=pltpu.PrefetchScalarGridSpec(
            num_scalar_prefetch=1,
            grid=(rows // block,),
            in_specs=[spec(v.shape) for v in inputs],
            out_specs=[spec((rows, width)) for _ in out_types],
        ),
        out_shape=[jax.ShapeDtypeStruct((rows, width), t) for t in out_types],
    )(table, *inputs)


def placed(pieces, column, columns, target_ref, at_column, sems, copies):
    row = 0
    for piece in pieces:
        rows = piece.shape[0]
        source = piece.at[:, pl.ds(column, columns)]
        place = target_ref.at[pl.ds(row, rows), pl.ds(at_column, columns)]
        copies.append(pltpu.make_async_copy(source, place, sems.at[len(copies)]))
        row += rows


def feed_kernel(count_a, count_b, xn_ref, dy_ref, *refs):
    part_a, part_b, refs = refs[:count_a], refs[count_a : count_a + count_b], refs[count_a + count_b :]
    act_ref, grad_ref, dxn_ref, gate_up_ref, down_ref, sems = refs
    cut = part_a[0].shape[1]
    hidden = act_ref.shape[1]
    split = 2 * hidden - cut

    @pl.when(pl.program_id(0) == 0)
    def _():
        copies = []
        placed(part_a, 0, cut, gate_up_ref, 0, sems, copies)
        placed(part_b, 0, split, gate_up_ref, cut, sems, copies)
        placed(part_b, split, hidden, down_ref, 0, sems, copies)
        for copy in copies:
            copy.start()
        for copy in copies:
            copy.wait()

    gate_up = jnp.dot(xn_ref[...], gate_up_ref[...], preferred_element_type=F32)
    gate, up_part = gate_up[:, :hidden], gate_up[:, hidden:]
    sigmoid_gate = jax.nn.sigmoid(gate)
    gated = gate * sigmoid_gate
    act_ref[...] = (gated * up_part).astype(BF)
    grad_act = jnp.dot(dy_ref[...], down_ref[...], preferred_element_type=F32)
    grad_gate = grad_act * up_part * sigmoid_gate * (1.0 + gate * (1.0 - sigmoid_gate))
    grad_ref[:, :hidden] = grad_gate.astype(BF)
    grad_ref[:, hidden:] = (grad_act * gated).astype(BF)
    dxn_ref[...] = contract_last(grad_ref[...], gate_up_ref[...]).astype(BF)


OVER_X_FIRST = ((1, 2), (3,), (0,))
OVER_Y_FIRST = ((2, 3), (1,), (0,))
ONE_EACH = ((0,), (1,), (2,), (3,))


def outer_kernel(layouts, left_ref, right_ref, *out_refs):
    step = pl.program_id(0)
    turned = left_ref[...].T
    column = 0
    refs = iter(out_refs)
    for layout in layouts:
        targets = [next(refs) for _ in layout]
        width = targets[0].shape[1]
        right = right_ref[:, column : column + width]
        block = jnp.dot(turned, right, preferred_element_type=F32).astype(BF)
        column += width
        for target, held in zip(targets, layout):

            @pl.when((step >= held[0]) & (step <= held[-1]))
            def _():
                target[...] = block


def outer_blocks(left, right, layouts):
    tokens, rows = left.shape
    width = right.shape[1] // len(layouts)
    block = rows // 4
    held = [blocks for layout in layouts for blocks in layout]

    def spec(blocks):
        return pl.BlockSpec(
            (block, width), lambda p: (jnp.clip(p - blocks[0], 0, len(blocks) - 1), 0)
        )

    outs = pl.pallas_call(
        functools.partial(outer_kernel, layouts),
        grid=(4,),
        in_specs=[
            pl.BlockSpec((tokens, block), lambda p: (0, p)),
            pl.BlockSpec(right.shape, lambda p: (0, 0)),
        ],
        out_specs=[spec(blocks) for blocks in held],
        out_shape=[jax.ShapeDtypeStruct((len(blocks) * block, width), BF) for blocks in held],
        cost_estimate=pl.CostEstimate(
            flops=2 * tokens * rows * right.shape[1],
            bytes_accessed=2 * (tokens * (rows + right.shape[1]) + rows * right.shape[1]),
            transcendentals=0,
        ),
        name="outer_blocks",
    )(left, right)
    outs = iter(outs)
    return [[next(outs) for _ in layout] for layout in layouts]


def in_order(parts):
    return [piece for k in GRAY for piece in parts[k]]


def feed_forward(xn, dy, part_a, part_b, hidden):
    tokens, model_width = xn.shape
    block = min(256, tokens)
    part_a, part_b = in_order(part_a), in_order(part_b)

    def blocks(columns):
        return pl.BlockSpec((block, columns), lambda i: (i, 0))

    return pl.pallas_call(
        functools.partial(feed_kernel, len(part_a), len(part_b)),
        grid=(tokens // block,),
        in_specs=[blocks(model_width)] * 2
        + [pl.BlockSpec(memory_space=pl.ANY)] * (len(part_a) + len(part_b)),
        out_specs=[blocks(hidden), blocks(2 * hidden), blocks(model_width)],
        out_shape=[
            jax.ShapeDtypeStruct((tokens, columns), BF)
            for columns in (hidden, 2 * hidden, model_width)
        ],
        scratch_shapes=[
            pltpu.VMEM((model_width, 2 * hidden), BF),
            pltpu.VMEM((model_width, hidden), BF),
            pltpu.SemaphoreType.DMA((len(part_a) + 2 * len(part_b),)),
        ],
        cost_estimate=pl.CostEstimate(
            flops=10 * tokens * model_width * hidden,
            bytes_accessed=2 * (4 * tokens * model_width + 3 * model_width * hidden),
            transcendentals=tokens * hidden,
        ),
        name="feed_forward",
    )(xn, dy, *part_a, *part_b)


def feed_out_kernel(count, act_ref, *refs):
    pieces, (out_ref, down_ref, sems) = refs[:count], refs[count:]
    hidden = act_ref.shape[1]

    @pl.when(pl.program_id(0) == 0)
    def _():
        copies = []
        placed(pieces, pieces[0].shape[1] - hidden, hidden, down_ref, 0, sems, copies)
        for copy in copies:
            copy.start()
        for copy in copies:
            copy.wait()

    out_ref[...] = contract_last(act_ref[...], down_ref[...]).astype(BF)


def feed_out(act, part_b, model_width):
    tokens, hidden = act.shape
    block = min(256, tokens)
    pieces = in_order(part_b)
    return pl.pallas_call(
        functools.partial(feed_out_kernel, len(pieces)),
        grid=(tokens // block,),
        in_specs=[pl.BlockSpec((block, hidden), lambda i: (i, 0))]
        + [pl.BlockSpec(memory_space=pl.ANY)] * len(pieces),
        out_specs=pl.BlockSpec((block, model_width), lambda i: (i, 0)),
        out_shape=jax.ShapeDtypeStruct((tokens, model_width), BF),
        scratch_shapes=[
            pltpu.VMEM((model_width, hidden), BF), pltpu.SemaphoreType.DMA((len(pieces),))
        ],
        cost_estimate=pl.CostEstimate(
            flops=2 * tokens * model_width * hidden,
            bytes_accessed=2 * (tokens + model_width) * hidden + 2 * tokens * model_width,
            transcendentals=0,
        ),
        name="feed_out",
    )(act, *pieces)


def partner(array, bits):
    return lax.ppermute(array, "dp", [(i, i ^ bits) for i in range(4)])


class Quad:
    def __init__(self, index):
        self.index = index

    def gather_direct(self, block):
        return [block] + [partner(block, k) for k in (1, 2, 3)]

    def gather(self, first, second):
        a = {0: [first], 1: [partner(first, 1)]}
        b = {0: [second], 2: [partner(second, 2)]}
        a[2], b[1] = [partner(first, 2)], [partner(second, 1)]
        a[3], b[3] = [partner(a[1][0], 2)], [partner(b[2][0], 1)]
        return a, b

    def gather_late(self, first, second, first_high, second_high):
        rows = first_high.shape[0]
        a = {0: [first], 1: [partner(first, 1)]}
        b = {0: [second], 2: [partner(second, 2)]}
        a[2], b[1] = [partner(first_high, 2)], [partner(second_high, 1)]

        def late(*earlier):
            first_low, second_low, near_a, near_b = (
                after(v, *earlier) for v in (first[rows:], second[rows:], a[1][0], b[2][0])
            )
            a[2].append(partner(first_low, 2))
            b[1].append(partner(second_low, 1))
            a[3], b[3] = [partner(near_a, 2)], [partner(near_b, 1)]
            return a, b

        return late


def add(*terms):
    total = terms[0].astype(F32)
    for term in terms[1:]:
        total = total + term.astype(F32)
    return total.astype(BF)


class PairSum:
    def __init__(self, first, second):
        (send_a, *self.keep_a), (send_b, *self.keep_b) = first, second
        self.sent_a = partner(send_a, 1)
        self.sent_b = partner(send_b, 2)

    def second(self):
        rows = self.keep_a[0].shape[0]
        send_a = add(self.keep_a[0], self.sent_a[rows:])
        send_b = add(self.keep_b[0], self.sent_b[:rows])
        self.far_a = partner(send_a, 2)
        self.far_b = partner(send_b, 1)

    def total(self):
        rows = self.keep_a[0].shape[0]
        return jnp.concatenate(
            [
                add(self.keep_a[1], self.sent_a[:rows], self.far_a),
                add(self.keep_b[1], self.sent_b[rows:], self.far_b),
            ],
            1,
        )


def sum_direct(blocks):
    others = [partner(blocks[p], GRAY[p]) for p in (1, 2, 3)]
    return add(blocks[0], *others)


def reduce_plain(left, right):
    return lax.psum_scatter(
        contract_first(left, right).astype(BF), "dp", scatter_dimension=0, tiled=True
    )


def over_seq(values):
    return lax.all_gather(values, "seq", axis=0, tiled=True)


def sum_over_seq(values):
    return lax.psum_scatter(values.astype(BF), "seq", scatter_dimension=0, tiled=True)


def exchange(values, axes):
    return lax.all_to_all(values, axes, split_axis=0, concat_axis=0, tiled=True)


def exchange_rows(values, group_count):
    return exchange(
        values.reshape(group_count, values.shape[0] // group_count, values.shape[1]), "seq"
    )


def feed_forward_plain(xn, dy, gate_up_full, down_full, hidden):
    gate_up = jnp.dot(xn, gate_up_full, preferred_element_type=F32)
    gate, up_part = gate_up[:, :hidden], gate_up[:, hidden:]
    sigmoid_gate = jax.nn.sigmoid(gate)
    act = (gate * sigmoid_gate * up_part).astype(BF)
    grad_act = jnp.dot(dy, down_full, preferred_element_type=F32)
    grad_gate = grad_act * up_part * sigmoid_gate * (1.0 + gate * (1.0 - sigmoid_gate))
    grad_up = grad_act * gate * sigmoid_gate
    grad_gate_up = jnp.concatenate([grad_gate, grad_up], 1).astype(BF)
    return act, grad_gate_up, contract_last(grad_gate_up, gate_up_full).astype(BF)


def shards(
    layer_in, norm1_gain, qkv_weight, out_weight, norm2_gain, gate_up_weight, down_weight, cotangent
):
    token_rows, model_width = layer_in.shape
    group_count = lax.axis_size("seq")
    dp_count = lax.axis_size("dp")
    group = lax.axis_index("seq")
    member = lax.axis_index("dp")
    length = token_rows * group_count
    dp_rows = model_width // dp_count
    shard_rows = dp_rows // group_count
    hidden_units = down_weight.shape[1]
    hidden = hidden_units // group_count
    width = model_width // group_count
    quad = Quad(member) if dp_count == 4 else None
    strided = quad is not None and shard_rows == HD

    blocks_at = jnp.arange(4, dtype=jnp.int32)
    if quad:
        orders = (blocks_at ^ (blocks_at >> 1)) ^ member
        places = blocks_at ^ member
        places = places ^ (places >> 1)
    else:
        orders, places = blocks_at, blocks_at
    gain1, gain2 = norm1_gain[None, :], norm2_gain[None, :]

    xn1_own, dy_own = on_rows(norm_in_kernel, orders, (layer_in, gain1, cotangent), (BF, BF))
    xn1 = over_seq(xn1_own)

    if strided:
        left, right = strided_heads(qkv_weight, group, group_count)
    else:
        qkv_piece = jnp.concatenate(
            [
                lax.dynamic_slice_in_dim(qkv_weight, part * model_width + group * width, width, 1)
                for part in range(3)
            ],
            1,
        )
    gate_piece = lax.dynamic_slice_in_dim(gate_up_weight, group * hidden, hidden, 1)
    up_piece = lax.dynamic_slice_in_dim(gate_up_weight, hidden_units + group * hidden, hidden, 1)
    down_piece = lax.dynamic_slice_in_dim(down_weight, group * hidden, hidden, 1)
    if quad:
        if not strided:
            cut = qkv_piece.shape[1] // 2
            left, right = qkv_piece[:, :cut], qkv_piece[:, cut:]
        left, right = quad.gather(left, right)
        blocks = (left[3][0], right[3][0])
        qkv_pieces = [part[k][0] for k in GRAY for part in (left, right)]
        per_row = 2
        half = hidden // 2
        part_a = after(jnp.concatenate([gate_piece, up_piece[:, :half]], 1), *blocks)
        part_b = after(jnp.concatenate([up_piece[:, half:], down_piece], 1), *blocks)
        high_a, high_b = part_a[: dp_rows // 2], part_b[: dp_rows // 2]
        xn1, high_a, high_b = lax.optimization_barrier((xn1, high_a, high_b))
        rest_of_weights = quad.gather_late(part_a, part_b, high_a, high_b)
    else:
        qkv_pieces, per_row = [lax.all_gather(qkv_piece, "dp", axis=0, tiled=True)], 1
        gate_up_full = lax.all_gather(
            jnp.concatenate([gate_piece, up_piece], 1), "dp", axis=0, tiled=True
        )
        down_full = lax.all_gather(down_piece, "dp", axis=0, tiled=True)

    cosine, sine = rotary_tables(length)
    attn, query, key, value, lse = attention_forward(
        xn1, qkv_pieces, per_row, cosine, sine, token_rows
    )

    dy = over_seq(after(dy_own, attn))

    def to_features(by_head):
        if strided:
            moved = exchange(by_head.reshape(-1, HD, token_rows), ("dp", "seq"))
        else:
            by_tokens = by_head.transpose(1, 0, 2, 3).reshape(group_count, width, token_rows)
            moved = exchange(exchange(by_tokens, "seq").reshape(dp_count, dp_rows, token_rows), "dp")
        return moved.reshape(dp_count, dp_rows, token_rows)

    def to_heads(features):
        if strided:
            moved = exchange(features.reshape(-1, HD, token_rows), ("dp", "seq"))
            return moved.reshape(-1, group_count, HD, token_rows)
        moved = exchange(features, "dp").reshape(group_count, width, token_rows)
        moved = exchange(moved, "seq").reshape(group_count, width // HD, HD, token_rows)
        return moved.transpose(1, 0, 2, 3)

    features = to_features(attn)
    if quad:
        features = jnp.stack(
            [lax.dynamic_index_in_dim(features, member ^ k, 0, False) for k in range(4)]
        )
        parts = [contract_first(features[k], out_weight) for k in range(4)]
        others = [partner(parts[k].astype(BF), k) for k in (1, 2, 3)]
        partials = (parts[0], *others)
    else:
        partials = (
            lax.psum_scatter(
                jnp.einsum("dft,fn->dtn", features, out_weight, preferred_element_type=F32)
                .astype(BF)
                .reshape(dp_count * token_rows, model_width),
                "dp", scatter_dimension=0, tiled=True,
            ).astype(F32),
        )

    hidden_res, xn2_own = on_rows(norm_mid_kernel, orders, (layer_in, *partials, gain2), (F32, BF))
    xn2 = over_seq(xn2_own)
    if quad:
        part_a, part_b = rest_of_weights(*partials)
        act, grad_gate_up, partial_xn2 = feed_forward(xn2, dy, part_a, part_b, hidden)
        feed_sum = feed_out(after(act, partial_xn2), part_b, model_width)
    else:
        act, grad_gate_up, partial_xn2 = feed_forward_plain(
            xn2, dy, gate_up_full, down_full, hidden
        )
        feed_sum = contract_last(act, down_full).astype(BF)
    raw_xn2 = sum_over_seq(partial_xn2)
    feed_sum = after(feed_sum, raw_xn2)
    grad_hidden, hidden_low = on_rows(
        norm_grad_kernel, places, (hidden_res, cotangent, raw_xn2, gain2), (F32, BF)
    )
    feed_sum = sum_over_seq(feed_sum)
    if quad:
        halves = outer_blocks(dy, act, (OVER_X_FIRST, OVER_Y_FIRST))
        down_sum = PairSum(*halves)
        halves = outer_blocks(xn2, grad_gate_up, (OVER_X_FIRST, OVER_Y_FIRST) * 2)
        gate_sum, up_sum = PairSum(*halves[:2]), PairSum(*halves[2:])
        rows_low = quad.gather_direct(hidden_low)
        rows_low = jnp.stack(rows_low)
    else:
        down_rows = reduce_plain(dy, act)
        gate_rows = reduce_plain(xn2, grad_gate_up[:, :hidden])
        up_rows = reduce_plain(xn2, grad_gate_up[:, hidden:])
        rows_low = lax.all_gather(hidden_low, "dp", axis=0)

    grad_features = jnp.einsum(
        "fn,ktn->kft", out_weight, rows_low, preferred_element_type=F32
    ).astype(BF)
    if quad:
        grad_features = jnp.stack(
            [lax.dynamic_index_in_dim(grad_features, member ^ j, 0, False) for j in range(4)]
        )
    grad_attn = to_heads(grad_features)
    if quad:
        down_sum.second()
        gate_sum.second()
        up_sum.second()
    out_rows = jnp.einsum("kft,ktn->fn", features, rows_low, preferred_element_type=F32)
    out_rows = out_rows.astype(BF)
    out_grad = sum_over_seq(out_rows).astype(F32)
    grad_qkv, partial_xn1 = attention_backward(
        query, key, value, attn, grad_attn, lse, cosine, sine, qkv_pieces, per_row
    )
    raw_xn1 = sum_over_seq(partial_xn1)
    (input_grad,) = on_rows(
        norm_grad_kernel, places, (layer_in, grad_hidden, raw_xn1, gain1), (F32,)
    )
    (layer_out,) = on_rows(
        add_placed_kernel, places, (hidden_res, after(feed_sum, partial_xn1)), (F32,)
    )

    if quad:
        (blocks,) = outer_blocks(xn1, grad_qkv, (ONE_EACH,))
        qkv_rows = sum_direct(blocks)
        down_rows, gate_rows, up_rows = down_sum.total(), gate_sum.total(), up_sum.total()
    else:
        qkv_rows = reduce_plain(xn1, grad_qkv)
    down_parts = exchange_rows(down_rows, group_count)
    gate_parts = exchange_rows(gate_rows, group_count)
    up_parts = exchange_rows(up_rows, group_count)
    qkv_parts = exchange_rows(qkv_rows, group_count)
    down_grad, _ = side_rows([down_parts], down_weight, group)
    gate_up_grad, gain2_sum = side_rows([gate_parts, up_parts], gate_up_weight, group)
    if strided:
        qkv_grad, gain1_sum = strided_rows(qkv_parts, qkv_weight, group)
    else:
        thirds = [qkv_parts[:, :, i * width : (i + 1) * width] for i in range(3)]
        qkv_grad, gain1_sum = side_rows(thirds, qkv_weight, group)

    def gain_grad(sums, gain):
        own = lax.dynamic_slice_in_dim(gain, member * dp_rows + group * shard_rows, shard_rows, 0)
        return sums[:, 0] / own

    return (
        layer_out,
        input_grad,
        gain_grad(gain1_sum, norm1_gain),
        qkv_grad,
        out_grad,
        gain_grad(gain2_sum, norm2_gain),
        gate_up_grad,
        down_grad,
    )


def solution(mesh):
    rows = P(("dp", "seq"), None)
    in_specs = (
        rows, P(), P("dp", None), P("dp", None), P(), P("dp", None), P("dp", None), rows,
    )
    vector = P(("dp", "seq"))
    out_specs = (rows, rows, vector, rows, rows, vector, rows, rows)
    return jax.shard_map(shards, mesh=mesh, in_specs=in_specs, out_specs=out_specs, check_vma=False)
```

```python
import functools

import jax
import jax.numpy as jnp
from jax import lax
from jax.experimental import pallas as pl
from jax.experimental.pallas import tpu as pltpu
from jax.sharding import PartitionSpec as P


HD = 64
EPS = 1e-05
THETA = 130000.0
BF = jnp.bfloat16
F32 = jnp.float32

GRAY = (0, 1, 3, 2)


def after(values, *earlier):
    return lax.optimization_barrier((values, *earlier))[0]


def rotary_kernel(inverse_ref, cos_ref, sin_ref):
    step = min(32, cos_ref.shape[0])

    @pl.loop(0, cos_ref.shape[0] // step)
    def _(i):
        at = pl.ds(pl.multiple_of(i * step, step), step)
        position = i * step + lax.broadcasted_iota(jnp.int32, (step, 128), 0)
        angles = position.astype(F32) * inverse_ref[...]
        lane = lax.broadcasted_iota(jnp.int32, (step, 128), 1)
        sine = jnp.sin(angles)
        cos_ref[at, :] = jnp.cos(angles)
        sin_ref[at, :] = jnp.where((lane & (HD // 2)) != 0, sine, -sine)


def rotary_tables(length):
    half = HD // 2
    inverse = THETA ** (-(jnp.arange(half).astype(F32) * 2.0) / HD)
    table = jax.ShapeDtypeStruct((length, 128), F32)
    return pl.pallas_call(rotary_kernel, out_shape=[table, table], name="rotary")(
        jnp.tile(inverse, 4)[None, :]
    )


def contract_last(left, right):
    return lax.dot_general(left, right, (((1,), (1,)), ((), ())), preferred_element_type=F32)


def contract_first(left, right):
    return lax.dot_general(left, right, (((0,), (0,)), ((), ())), preferred_element_type=F32)


def half_turn(values):
    lane = lax.broadcasted_iota(jnp.int32, values.shape, 1)
    upper = (lane & (HD // 2)) != 0
    return jnp.where(
        upper, pltpu.roll(values, HD // 2, 1), pltpu.roll(values, 128 - HD // 2, 1)
    )


def head_only(values, head):
    lane = lax.broadcasted_iota(jnp.int32, values.shape, 1)
    return jnp.where(lane // HD == head, values, jnp.zeros_like(values))


def causal(block):
    key_pos = lax.broadcasted_iota(jnp.int32, (block, block), 0)
    query_pos = lax.broadcasted_iota(jnp.int32, (block, block), 1)
    return key_pos <= query_pos


def assembled(pieces, per_row, target_ref, sems):
    copies, row = [], 0
    for first in range(0, len(pieces), per_row):
        column = 0
        for piece in pieces[first : first + per_row]:
            rows, columns = piece.shape
            place = target_ref.at[pl.ds(row, rows), pl.ds(column, columns)]
            copies.append(pltpu.make_async_copy(piece, place, sems.at[len(copies)]))
            column += columns
        row += rows
    return copies


def attention_forward_kernel(block, count, per_row, xn_ref, *refs):
    pieces, refs = refs[:count], refs[count:]
    cos_ref, sin_ref, attn_ref, q_ref, k_ref, v_ref, lse_ref, weight_ref, vt_ref, sems = refs
    head = pl.program_id(0)
    length, width = q_ref.shape
    tokens = attn_ref.shape[3]
    scale = HD ** (-0.5)

    @pl.when(head == 0)
    def _():
        copies = assembled(pieces, per_row, weight_ref, sems)
        for copy in copies:
            copy.start()
        for copy in copies:
            copy.wait()

        @pl.loop(0, length // block)
        def _(i):
            at = pl.ds(pl.multiple_of(i * block, block), block)
            qkv = jnp.dot(xn_ref[at, :], weight_ref[...], preferred_element_type=F32).astype(BF)
            v_ref[at, :] = qkv[:, 2 * width :]
            for c in range(width // 128):
                for source, target, factor in ((0, q_ref, scale), (width, k_ref, 1.0)):
                    u = qkv[:, source + c * 128 : source + (c + 1) * 128].astype(F32)
                    turned = u * cos_ref[at, :] + half_turn(u) * sin_ref[at, :]
                    target[at, c * 128 : (c + 1) * 128] = turned.astype(BF) * factor

        for c in range(width // 128):
            cols = slice(c * 128, (c + 1) * 128)
            vt_ref[cols, :] = v_ref[:, cols].astype(F32).T.astype(BF)

    rows = pl.ds(pl.multiple_of(head * HD, HD), HD)
    for i in range(length // block):
        low, high = i * block, (i + 1) * block
        query = head_only(q_ref[low:high, :], head)
        near = contract_last(k_ref[low:high, :], query)
        near = jnp.where(causal(block), near, -1e30)
        top = jnp.max(near, axis=0, keepdims=True)
        if i:
            far = contract_last(k_ref[0:low, :], query)
            top = jnp.maximum(top, jnp.max(far, axis=0, keepdims=True))
        near = jnp.exp(near - top)
        total = jnp.sum(near, axis=0, keepdims=True)
        mixed = jnp.dot(vt_ref[rows, low:high], near.astype(BF), preferred_element_type=F32)
        if i:
            far = jnp.exp(far - top)
            total = total + jnp.sum(far, axis=0, keepdims=True)
            mixed = mixed + jnp.dot(
                vt_ref[rows, 0:low], far.astype(BF), preferred_element_type=F32
            )
        mixed = (mixed / total).astype(BF)
        for part in range(block // tokens):
            attn_ref[head, low // tokens + part] = mixed[:, part * tokens : (part + 1) * tokens]
        lse_ref[pl.ds(head, 1), low:high] = top + jnp.log(total)


def attention_backward_kernel(
    block, count, per_row, q_ref, k_ref, v_ref, attn_ref, grad_ref, lse_ref, cos_ref, sin_ref, *refs
):
    pieces, refs = refs[:count], refs[count:]
    out_ref, dxn_ref, weight_ref, dq_ref, dk_ref, dv_ref, delta_ref, flat_ref, sems = refs
    head = pl.program_id(0)
    length, width = q_ref.shape
    tokens = attn_ref.shape[3]
    scale = HD ** (-0.5)

    @pl.when(head == 0)
    def _():
        for copy in assembled(pieces, per_row, weight_ref, sems):
            copy.start()
        dq_ref[...] = jnp.zeros_like(dq_ref)
        dk_ref[...] = jnp.zeros_like(dk_ref)
        dv_ref[...] = jnp.zeros_like(dv_ref)
        for c in range(width // 128):
            for j in range(length // tokens):
                pair = jnp.concatenate([grad_ref[2 * c, j], grad_ref[2 * c + 1, j]], 0)
                flat_ref[j * tokens : (j + 1) * tokens, c * 128 : (c + 1) * 128] = (
                    pair.astype(F32).T.astype(BF)
                )

    for j in range(length // tokens):
        product = grad_ref[head, j].astype(F32) * attn_ref[head, j].astype(F32)
        delta_ref[:, j * tokens : (j + 1) * tokens] = jnp.sum(product, axis=0, keepdims=True)

    def piece(keys, low, high, query, grad, diagonal):
        prob = jnp.exp(contract_last(k_ref[keys, :], query) - lse_ref[pl.ds(head, 1), low:high])
        if diagonal:
            prob = jnp.where(causal(block), prob, 0.0)
        dprob = contract_last(v_ref[keys, :], grad)
        dscore = (prob * (dprob - delta_ref[:, low:high])).astype(BF)
        dv_ref[keys, :] += jnp.dot(prob.astype(BF), grad, preferred_element_type=F32)
        dk_ref[keys, :] += jnp.dot(dscore, query, preferred_element_type=F32)
        dq_ref[low:high, :] += contract_first(dscore, head_only(k_ref[keys, :], head))

    for i in range(length // block):
        low, high = i * block, (i + 1) * block
        query = head_only(q_ref[low:high, :], head)
        grad = head_only(flat_ref[low:high, :], head)
        piece(slice(low, high), low, high, query, grad, True)
        if i:
            piece(slice(0, low), low, high, query, grad, False)

    @pl.when(head == pl.num_programs(0) - 1)
    def _():
        for copy in assembled(pieces, per_row, weight_ref, sems):
            copy.wait()

        @pl.loop(0, length // block)
        def _(i):
            at = pl.ds(pl.multiple_of(i * block, block), block)
            for c in range(width // 128):
                cols = slice(c * 128, (c + 1) * 128)
                for source, target, factor in ((dq_ref, 0, scale), (dk_ref, width, 1.0)):
                    u = source[at, cols] * factor
                    turned = u * cos_ref[at, :] - half_turn(u) * sin_ref[at, :]
                    out_ref[at, target + c * 128 : target + (c + 1) * 128] = turned.astype(BF)
            out_ref[at, 2 * width : 3 * width] = dv_ref[at, :].astype(BF)
            dxn_ref[at, :] = contract_last(out_ref[at, :], weight_ref[...]).astype(BF)


def resident(shape):
    return pl.BlockSpec(shape, lambda h: tuple(0 for _ in shape))


def attention_forward(xn, pieces, per_row, cosine, sine, tokens):
    length, model_width = xn.shape
    width = sum(piece.shape[1] for piece in pieces[:per_row]) // 3
    heads = width // HD
    block = min(256, length)
    pairs = heads * length * length
    out = (heads, length // tokens, HD, tokens)
    return pl.pallas_call(
        functools.partial(attention_forward_kernel, block, len(pieces), per_row),
        grid=(heads,),
        in_specs=[resident(xn.shape)]
        + [pl.BlockSpec(memory_space=pl.ANY)] * len(pieces)
        + [resident(cosine.shape)] * 2,
        out_specs=[resident(out)] + [resident((length, width))] * 3 + [resident((8, length))],
        out_shape=[jax.ShapeDtypeStruct(out, BF)]
        + [jax.ShapeDtypeStruct((length, width), BF)] * 3
        + [jax.ShapeDtypeStruct((8, length), F32)],
        scratch_shapes=[
            pltpu.VMEM((model_width, 3 * width), BF),
            pltpu.VMEM((width, length), BF),
            pltpu.SemaphoreType.DMA((len(pieces),)),
        ],
        cost_estimate=pl.CostEstimate(
            flops=2 * pairs * HD + 6 * length * model_width * width,
            bytes_accessed=8 * length * width + 2 * model_width * (length + 3 * width),
            transcendentals=pairs // 2,
        ),
        name="attention_forward",
    )(xn, *pieces, cosine, sine)


def attention_backward(query, key, value, attn, grad, lse, cosine, sine, pieces, per_row):
    length, width = query.shape
    model_width = sum(piece.shape[0] for piece in pieces[::per_row])
    heads = width // HD
    block = min(256, length)
    pairs = heads * length * length
    flat = resident((length, width))
    return pl.pallas_call(
        functools.partial(attention_backward_kernel, block, len(pieces), per_row),
        grid=(heads,),
        in_specs=[flat, flat, flat, resident(attn.shape), resident(attn.shape)]
        + [resident((8, length))]
        + [resident(cosine.shape)] * 2
        + [pl.BlockSpec(memory_space=pl.ANY)] * len(pieces),
        out_specs=[resident((length, 3 * width)), resident((length, model_width))],
        out_shape=[
            jax.ShapeDtypeStruct((length, 3 * width), BF),
            jax.ShapeDtypeStruct((length, model_width), BF),
        ],
        scratch_shapes=[pltpu.VMEM((model_width, 3 * width), BF)]
        + [pltpu.VMEM((length, width), F32)] * 3
        + [
            pltpu.VMEM((1, length), F32),
            pltpu.VMEM((length, width), BF),
            pltpu.SemaphoreType.DMA((len(pieces),)),
        ],
        cost_estimate=pl.CostEstimate(
            flops=5 * pairs * HD + 6 * length * model_width * width,
            bytes_accessed=20 * length * width + 2 * model_width * (length + 3 * width),
            transcendentals=pairs // 2,
        ),
        name="attention_backward",
    )(query, key, value, attn, grad, lse, cosine, sine, *pieces)


def strided_heads_kernel(which_ref, *refs):
    runs, outs = refs[:-2], refs[-2:]
    parity = which_ref[0] % 2
    half = len(runs) // 2

    for odd in range(2):

        @pl.when(parity == odd)
        def _():
            cols = slice(odd * HD, (odd + 1) * HD)
            for out, first in zip(outs, (0, half)):
                for r in range(0, half, 2):
                    out[:, r * HD : (r + 2) * HD] = jnp.concatenate(
                        [runs[first + r][:, cols], runs[first + r + 1][:, cols]], 1
                    )


def strided_heads(weight, group, group_count):
    rows, columns = weight.shape
    run = group_count * HD // 128
    runs = columns // (group_count * HD)

    def spec(r):
        return pl.BlockSpec((rows, 128), lambda g, w: (0, r * run + w[0] // 2))

    half = (rows, runs // 2 * HD)
    return pl.pallas_call(
        strided_heads_kernel,
        grid_spec=pltpu.PrefetchScalarGridSpec(
            num_scalar_prefetch=1,
            grid=(1,),
            in_specs=[spec(r) for r in range(runs)],
            out_specs=[pl.BlockSpec(half, lambda g, w: (0, 0))] * 2,
        ),
        out_shape=[jax.ShapeDtypeStruct(half, weight.dtype)] * 2,
        name="strided_heads",
    )(group.reshape(1), *[weight] * runs)


def lane_sums(values):
    return jnp.sum(values.T, axis=0, keepdims=True)


def strided_rows_kernel(first, which_ref, in_ref, weight_ref, gain_ref, out_ref, sum_ref):
    groups, rows, width = in_ref.shape
    total = jnp.zeros((rows, 128), F32)
    for b in range((width - first) // HD):
        cols = slice(first + b * HD, first + (b + 1) * HD)
        for pair in range(groups // 2):
            both = jnp.concatenate(
                [in_ref[2 * pair, :, cols], in_ref[2 * pair + 1, :, cols]], 1
            ).astype(F32)
            at = (b * groups + 2 * pair) * HD
            out_ref[:, at : at + 128] = both
            total = total + both * weight_ref[:, at : at + 128].astype(F32)
    sum_ref[...] = lane_sums(total) / gain_ref[...]


def strided_rows(parts, first, weight, gain, group):
    _, rows, _ = parts.shape
    return pl.pallas_call(
        functools.partial(strided_rows_kernel, first),
        grid_spec=pltpu.PrefetchScalarGridSpec(
            num_scalar_prefetch=1,
            grid=(1,),
            in_specs=[
                pl.BlockSpec(parts.shape, lambda g, w: (0, 0, 0)),
                pl.BlockSpec((rows, weight.shape[1]), lambda g, w: (w[0], 0)),
                pl.BlockSpec((1, rows), lambda g, w: (0, 0)),
            ],
            out_specs=[
                pl.BlockSpec((rows, weight.shape[1]), lambda g, w: (0, 0)),
                pl.BlockSpec((1, rows), lambda g, w: (0, 0)),
            ],
        ),
        out_shape=[
            jax.ShapeDtypeStruct((rows, weight.shape[1]), F32),
            jax.ShapeDtypeStruct((1, rows), F32),
        ],
        name="strided_rows",
    )(group.reshape(1), parts, weight, gain)


def side_rows_kernel(runs, which_ref, *refs):
    parts, (weight_ref, gain_ref, out_ref, sum_ref) = refs[:runs], refs[runs:]
    groups, rows, piece = parts[0].shape

    @pl.when(pl.program_id(0) == 0)
    def _():
        sum_ref[...] = jnp.zeros_like(sum_ref)

    for run in range(runs):

        @pl.when(pl.program_id(0) == run)
        def _():
            def step(s, total):
                values = parts[run][s].astype(F32)
                cols = pl.ds(pl.multiple_of(s * piece, piece), piece)
                out_ref[:, cols] = values
                product = values * weight_ref[:, cols].astype(F32)
                for c in range(piece // 128):
                    total = total + product[:, c * 128 : (c + 1) * 128]
                return total

            total = lax.fori_loop(0, groups, step, jnp.zeros((rows, 128), F32))
            sum_ref[...] += lane_sums(total) / gain_ref[...]


def side_rows(parts, piece, weight, gain, group):
    groups, rows, _ = parts[0][0].shape
    runs = len(parts)

    def spec(place):
        return pl.BlockSpec((groups, rows, piece), lambda c, w: (0, 0, place))

    return pl.pallas_call(
        functools.partial(side_rows_kernel, runs),
        grid_spec=pltpu.PrefetchScalarGridSpec(
            num_scalar_prefetch=1,
            grid=(runs,),
            in_specs=[spec(place) for _, place in parts]
            + [
                pl.BlockSpec((rows, groups * piece), lambda c, w: (w[0], c)),
                pl.BlockSpec((1, rows), lambda c, w: (0, 0)),
            ],
            out_specs=[
                pl.BlockSpec((rows, groups * piece), lambda c, w: (0, c)),
                pl.BlockSpec((1, rows), lambda c, w: (0, 0)),
            ],
        ),
        out_shape=[
            jax.ShapeDtypeStruct((rows, runs * groups * piece), F32),
            jax.ShapeDtypeStruct((1, rows), F32),
        ],
        name="side_rows",
    )(group.reshape(1), *[array for array, _ in parts], weight, gain)


BLOCKS = 4


def at_block(ref, rows, index):
    width = ref.shape[1] // BLOCKS
    return ref.at[rows, pl.ds(pl.multiple_of(index * width, width), width)]


def by_rows(kernel):
    def run(table_ref, x_ref, *refs):
        step = min(32, x_ref.shape[0])

        @pl.loop(0, x_ref.shape[0] // step)
        def _(i):
            kernel(pl.ds(pl.multiple_of(i * step, step), step), table_ref, x_ref, *refs)

    return run


ALL = slice(None)


def norm_in_kernel(rows, orders_ref, x_ref, gain_ref, grad_ref, xn_ref, dy_ref):
    x = x_ref[rows, :]
    inv = lax.rsqrt(jnp.mean(x * x, axis=1, keepdims=True) + EPS)
    for p in range(BLOCKS):
        block = orders_ref[p]
        normed = at_block(x_ref, rows, block)[...] * inv * at_block(gain_ref, ALL, block)[...]
        at_block(xn_ref, rows, p)[...] = normed.astype(BF)
        at_block(dy_ref, rows, p)[...] = at_block(grad_ref, rows, block)[...].astype(BF)


def norm_mid_kernel(rows, orders_ref, x_ref, own_ref, *refs):
    others, (gain_ref, mid_ref, xn_ref) = refs[:-3], refs[-3:]
    mid = x_ref[rows, :] + own_ref[rows, :]
    for other in others:
        mid = mid + other[rows, :].astype(F32)
    mid_ref[rows, :] = mid
    inv = lax.rsqrt(jnp.mean(mid * mid, axis=1, keepdims=True) + EPS)
    for p in range(BLOCKS):
        block = orders_ref[p]
        normed = at_block(mid_ref, rows, block)[...] * inv * at_block(gain_ref, ALL, block)[...]
        at_block(xn_ref, rows, p)[...] = normed.astype(BF)


def norm_grad_kernel(rows, places_ref, x_ref, base_ref, grad_ref, gain_ref, out_ref, *low_ref):
    x = x_ref[rows, :]
    inv = lax.rsqrt(jnp.mean(x * x, axis=1, keepdims=True) + EPS)
    grad = jnp.concatenate(
        [at_block(grad_ref, rows, places_ref[j])[...] for j in range(BLOCKS)], 1
    ).astype(F32)
    normed = x * inv
    grad_hat = grad * gain_ref[...]
    mean = jnp.mean(grad_hat * normed, axis=1, keepdims=True)
    out = base_ref[rows, :] + inv * (grad_hat - normed * mean)
    out_ref[rows, :] = out
    for ref in low_ref:
        ref[rows, :] = out.astype(BF)


def add_placed_kernel(rows, places_ref, base_ref, part_ref, out_ref):
    for j in range(BLOCKS):
        part = at_block(part_ref, rows, places_ref[j])[...].astype(F32)
        at_block(out_ref, rows, j)[...] = at_block(base_ref, rows, j)[...] + part


def on_rows(kernel, table, inputs, out_types):
    rows, width = inputs[0].shape
    block = rows

    def spec(shape):
        if shape[0] == 1:
            return pl.BlockSpec(shape, lambda i, t: (0, 0))
        return pl.BlockSpec((block, width), lambda i, t: (i, 0))

    return pl.pallas_call(
        by_rows(kernel),
        grid_spec=pltpu.PrefetchScalarGridSpec(
            num_scalar_prefetch=1,
            grid=(rows // block,),
            in_specs=[spec(v.shape) for v in inputs],
            out_specs=[spec((rows, width)) for _ in out_types],
        ),
        out_shape=[jax.ShapeDtypeStruct((rows, width), t) for t in out_types],
    )(table, *inputs)


def placed(pieces, column, columns, target_ref, at_column, sems, copies):
    row = 0
    for piece in pieces:
        rows = piece.shape[0]
        source = piece.at[:, pl.ds(column, columns)]
        place = target_ref.at[pl.ds(row, rows), pl.ds(at_column, columns)]
        copies.append(pltpu.make_async_copy(source, place, sems.at[len(copies)]))
        row += rows


def feed_kernel(count_a, count_b, xn_ref, dy_ref, *refs):
    part_a, part_b, refs = refs[:count_a], refs[count_a : count_a + count_b], refs[count_a + count_b :]
    act_ref, grad_ref, dxn_ref, gate_up_ref, down_ref, sems = refs
    cut = part_a[0].shape[1]
    hidden = act_ref.shape[1]
    split = 2 * hidden - cut

    copies = []
    placed(part_a, 0, cut, gate_up_ref, 0, sems, copies)
    placed(part_b, 0, split, gate_up_ref, cut, sems, copies)
    placed(part_b, split, hidden, down_ref, 0, sems, copies)

    @pl.when(pl.program_id(0) == 0)
    def _():
        for copy in copies:
            copy.start()
        for copy in copies[: count_a + count_b]:
            copy.wait()

    gate_up = jnp.dot(xn_ref[...], gate_up_ref[...], preferred_element_type=F32)
    gate, up_part = gate_up[:, :hidden], gate_up[:, hidden:]
    sigmoid_gate = jax.nn.sigmoid(gate)
    gated = gate * sigmoid_gate
    act_ref[...] = (gated * up_part).astype(BF)

    @pl.when(pl.program_id(0) == 0)
    def _():
        for copy in copies[count_a + count_b :]:
            copy.wait()

    grad_act = jnp.dot(dy_ref[...], down_ref[...], preferred_element_type=F32)
    grad_gate = grad_act * up_part * sigmoid_gate * (1.0 + gate * (1.0 - sigmoid_gate))
    grad_ref[:, :hidden] = grad_gate.astype(BF)
    grad_ref[:, hidden:] = (grad_act * gated).astype(BF)
    columns_last(grad_ref, gate_up_ref, dxn_ref)


def columns_last(left_ref, right_ref, out_ref):
    chunk = min(1024, out_ref.shape[1])

    @pl.loop(0, out_ref.shape[1] // chunk)
    def _(c):
        at = pl.ds(pl.multiple_of(c * chunk, chunk), chunk)
        out_ref[:, at] = contract_last(left_ref[...], right_ref[at, :]).astype(BF)


OVER_X_FIRST = ((1, 3), (3, 4), (0, 1))
OVER_Y_FIRST = ((2, 4), (1, 2), (0, 1))
ONE_EACH = ((0, 1), (1, 2), (2, 3), (3, 4))


def outer_kernel(layouts, left_ref, right_ref, *out_refs):
    step = pl.program_id(0)
    steps = pl.num_programs(0) // 4
    turned = left_ref[...].T
    column = 0
    refs = iter(out_refs)
    for layout in layouts:
        targets = [next(refs) for _ in layout]
        width = targets[0].shape[1]
        right = right_ref[:, column : column + width]
        block = jnp.dot(turned, right, preferred_element_type=F32).astype(BF)
        column += width
        for target, (first, end) in zip(targets, layout):

            @pl.when((step >= first * steps) & (step < end * steps))
            def _():
                target[...] = block


def outer_blocks(left, right, layouts, steps=2, side=None):
    tokens, rows = left.shape
    columns = right.shape[1] if side is None else right.shape[1] // 2
    width = columns // len(layouts)
    block = rows // (4 * steps)
    held = [blocks for layout in layouts for blocks in layout]

    def spec(first, end):
        return pl.BlockSpec(
            (block, width),
            lambda p: (jnp.clip(p - first * steps, 0, (end - first) * steps - 1), 0),
        )

    outs = pl.pallas_call(
        functools.partial(outer_kernel, layouts),
        grid=(4 * steps,),
        in_specs=[
            pl.BlockSpec((tokens, block), lambda p: (0, p)),
            pl.BlockSpec((tokens, columns), lambda p: (0, side or 0)),
        ],
        out_specs=[spec(*blocks) for blocks in held],
        out_shape=[
            jax.ShapeDtypeStruct(((end - first) * rows // 4, width), BF) for first, end in held
        ],
        cost_estimate=pl.CostEstimate(
            flops=2 * tokens * rows * columns,
            bytes_accessed=2 * (tokens * (rows + columns) + rows * columns),
            transcendentals=0,
        ),
        name="outer_blocks",
    )(left, right)
    outs = iter(outs)
    return [[next(outs) for _ in layout] for layout in layouts]


def in_order(parts):
    return [piece for k in GRAY for piece in parts[k]]


def feed_forward(xn, dy, part_a, part_b, hidden):
    tokens, model_width = xn.shape
    block = min(256, tokens)
    part_a, part_b = in_order(part_a), in_order(part_b)

    def blocks(columns):
        return pl.BlockSpec((block, columns), lambda i: (i, 0))

    return pl.pallas_call(
        functools.partial(feed_kernel, len(part_a), len(part_b)),
        grid=(tokens // block,),
        in_specs=[blocks(model_width)] * 2
        + [pl.BlockSpec(memory_space=pl.ANY)] * (len(part_a) + len(part_b)),
        out_specs=[blocks(hidden), blocks(2 * hidden), blocks(model_width)],
        out_shape=[
            jax.ShapeDtypeStruct((tokens, columns), BF)
            for columns in (hidden, 2 * hidden, model_width)
        ],
        scratch_shapes=[
            pltpu.VMEM((model_width, 2 * hidden), BF),
            pltpu.VMEM((model_width, hidden), BF),
            pltpu.SemaphoreType.DMA((len(part_a) + 2 * len(part_b),)),
        ],
        cost_estimate=pl.CostEstimate(
            flops=10 * tokens * model_width * hidden,
            bytes_accessed=2 * (4 * tokens * model_width + 3 * model_width * hidden),
            transcendentals=tokens * hidden,
        ),
        name="feed_forward",
    )(xn, dy, *part_a, *part_b)


def feed_out_kernel(count, act_ref, *refs):
    pieces, (out_ref, down_ref, sems) = refs[:count], refs[count:]
    hidden = act_ref.shape[1]

    @pl.when(pl.program_id(0) == 0)
    def _():
        copies = []
        placed(pieces, pieces[0].shape[1] - hidden, hidden, down_ref, 0, sems, copies)
        for copy in copies:
            copy.start()
        for copy in copies:
            copy.wait()

    columns_last(act_ref, down_ref, out_ref)


def feed_out(act, part_b, model_width):
    tokens, hidden = act.shape
    block = min(256, tokens)
    pieces = in_order(part_b)
    return pl.pallas_call(
        functools.partial(feed_out_kernel, len(pieces)),
        grid=(tokens // block,),
        in_specs=[pl.BlockSpec((block, hidden), lambda i: (i, 0))]
        + [pl.BlockSpec(memory_space=pl.ANY)] * len(pieces),
        out_specs=pl.BlockSpec((block, model_width), lambda i: (i, 0)),
        out_shape=jax.ShapeDtypeStruct((tokens, model_width), BF),
        scratch_shapes=[
            pltpu.VMEM((model_width, hidden), BF), pltpu.SemaphoreType.DMA((len(pieces),))
        ],
        cost_estimate=pl.CostEstimate(
            flops=2 * tokens * model_width * hidden,
            bytes_accessed=2 * (tokens + model_width) * hidden + 2 * tokens * model_width,
            transcendentals=0,
        ),
        name="feed_out",
    )(act, *pieces)


def rows_by_member(pieces, places_ref, target_ref, sems):
    height = pieces[0].shape[0]
    copies = [
        pltpu.make_async_copy(
            piece,
            target_ref.at[pl.ds(pl.multiple_of(places_ref[k] * height, height), height)],
            sems.at[k],
        )
        for k, piece in enumerate(pieces)
    ]
    for copy in copies:
        copy.start()
    for copy in copies:
        copy.wait()


def out_rows_kernel(members_ref, features_ref, *refs):
    pieces, (out_ref, rows_ref, sems) = refs[:4], refs[4:]
    rows_by_member(pieces, members_ref, rows_ref, sems)
    left = jnp.concatenate([features_ref[d] for d in range(4)], 1)
    chunk = 512

    @pl.loop(0, out_ref.shape[1] // chunk)
    def _(c):
        at = pl.ds(pl.multiple_of(c * chunk, chunk), chunk)
        out_ref[:, at] = jnp.dot(left, rows_ref[:, at], preferred_element_type=F32).astype(BF)


def out_rows_grad(features, pieces, members):
    tokens, width = pieces[0].shape
    count = features.shape[1]
    return pl.pallas_call(
        out_rows_kernel,
        grid_spec=pltpu.PrefetchScalarGridSpec(
            num_scalar_prefetch=1,
            grid=(1,),
            in_specs=[pl.BlockSpec(features.shape, lambda i, m: (0, 0, 0))]
            + [pl.BlockSpec(memory_space=pl.ANY)] * 4,
            out_specs=pl.BlockSpec((count, width), lambda i, m: (0, 0)),
            scratch_shapes=[pltpu.VMEM((4 * tokens, width), BF), pltpu.SemaphoreType.DMA((4,))],
        ),
        out_shape=jax.ShapeDtypeStruct((count, width), BF),
        name="out_rows",
    )(members, features, *pieces)


def partner(array, bits):
    return lax.ppermute(array, "dp", [(i, i ^ bits) for i in range(4)])


class Quad:
    def __init__(self, index):
        self.index = index

    def gather_direct(self, block):
        return [block] + [partner(block, k) for k in (1, 2, 3)]

    def gather(self, first, second):
        a = {0: [first], 1: [partner(first, 1)]}
        b = {0: [second], 2: [partner(second, 2)]}
        a[2], b[1] = [partner(first, 2)], [partner(second, 1)]
        a[3], b[3] = [partner(a[1][0], 2)], [partner(b[2][0], 1)]
        return a, b

    def gather_late(self, first, second, first_high, second_high):
        rows = first_high.shape[0]
        a = {0: [first], 1: [partner(first, 1)]}
        b = {0: [second], 2: [partner(second, 2)]}
        a[2], b[1] = [partner(first_high, 2)], [partner(second_high, 1)]

        def late(*earlier):
            first_low, second_low, near_a, near_b = (
                after(v, *earlier) for v in (first[rows:], second[rows:], a[1][0], b[2][0])
            )
            a[2].append(partner(first_low, 2))
            b[1].append(partner(second_low, 1))
            a[3], b[3] = [partner(near_a, 2)], [partner(near_b, 1)]
            return a, b

        return late


def add(*terms):
    total = terms[0].astype(F32)
    for term in terms[1:]:
        total = total + term.astype(F32)
    return total.astype(BF)


class PairSum:
    def __init__(self, first, second):
        (send_a, *self.keep_a), (send_b, *self.keep_b) = first, second
        self.sent_a = partner(send_a, 1)
        self.sent_b = partner(send_b, 2)

    def second(self):
        rows = self.keep_a[0].shape[0]
        send_a = add(self.keep_a[0], self.sent_a[rows:])
        send_b = add(self.keep_b[0], self.sent_b[:rows])
        self.far_a = partner(send_a, 2)
        self.far_b = partner(send_b, 1)

    def total(self):
        rows = self.keep_a[0].shape[0]
        return jnp.concatenate(
            [
                add(self.keep_a[1], self.sent_a[:rows], self.far_a),
                add(self.keep_b[1], self.sent_b[rows:], self.far_b),
            ],
            1,
        )


def sum_direct(blocks):
    others = [partner(blocks[p], GRAY[p]) for p in (1, 2, 3)]
    return add(blocks[0], *others)


def reduce_plain(left, right):
    return lax.psum_scatter(
        contract_first(left, right).astype(BF), "dp", scatter_dimension=0, tiled=True
    )


def over_seq(values):
    return lax.all_gather(values, "seq", axis=0, tiled=True)


def sum_over_seq(values):
    return lax.psum_scatter(values.astype(BF), "seq", scatter_dimension=0, tiled=True)


def exchange(values, axes):
    return lax.all_to_all(values, axes, split_axis=0, concat_axis=0, tiled=True)


def exchange_rows(values, group_count):
    return exchange(
        values.reshape(group_count, values.shape[0] // group_count, values.shape[1]), "seq"
    )


def feed_forward_plain(xn, dy, gate_up_full, down_full, hidden):
    gate_up = jnp.dot(xn, gate_up_full, preferred_element_type=F32)
    gate, up_part = gate_up[:, :hidden], gate_up[:, hidden:]
    sigmoid_gate = jax.nn.sigmoid(gate)
    act = (gate * sigmoid_gate * up_part).astype(BF)
    grad_act = jnp.dot(dy, down_full, preferred_element_type=F32)
    grad_gate = grad_act * up_part * sigmoid_gate * (1.0 + gate * (1.0 - sigmoid_gate))
    grad_up = grad_act * gate * sigmoid_gate
    grad_gate_up = jnp.concatenate([grad_gate, grad_up], 1).astype(BF)
    return act, grad_gate_up, contract_last(grad_gate_up, gate_up_full).astype(BF)


def shards(
    layer_in, norm1_gain, qkv_weight, out_weight, norm2_gain, gate_up_weight, down_weight, cotangent
):
    token_rows, model_width = layer_in.shape
    group_count = lax.axis_size("seq")
    dp_count = lax.axis_size("dp")
    group = lax.axis_index("seq")
    member = lax.axis_index("dp")
    length = token_rows * group_count
    dp_rows = model_width // dp_count
    shard_rows = dp_rows // group_count
    hidden_units = down_weight.shape[1]
    hidden = hidden_units // group_count
    width = model_width // group_count
    quad = Quad(member) if dp_count == 4 else None
    strided = quad is not None and shard_rows == HD

    blocks_at = jnp.arange(4, dtype=jnp.int32)
    if quad:
        orders = (blocks_at ^ (blocks_at >> 1)) ^ member
        places = blocks_at ^ member
        places = places ^ (places >> 1)
    else:
        orders, places = blocks_at, blocks_at
    gain1, gain2 = norm1_gain[None, :], norm2_gain[None, :]

    xn1_own, dy_own = on_rows(norm_in_kernel, orders, (layer_in, gain1, cotangent), (BF, BF))
    xn1 = over_seq(xn1_own)

    if strided:
        left, right = strided_heads(qkv_weight, group, group_count)
    else:
        qkv_piece = jnp.concatenate(
            [
                lax.dynamic_slice_in_dim(qkv_weight, part * model_width + group * width, width, 1)
                for part in range(3)
            ],
            1,
        )
    gate_piece = lax.dynamic_slice_in_dim(gate_up_weight, group * hidden, hidden, 1)
    up_piece = lax.dynamic_slice_in_dim(gate_up_weight, hidden_units + group * hidden, hidden, 1)
    down_piece = lax.dynamic_slice_in_dim(down_weight, group * hidden, hidden, 1)
    if quad:
        if not strided:
            cut = qkv_piece.shape[1] // 2
            left, right = qkv_piece[:, :cut], qkv_piece[:, cut:]
        left, right = quad.gather(left, right)
        blocks = (left[3][0], right[3][0])
        qkv_pieces = [part[k][0] for k in GRAY for part in (left, right)]
        per_row = 2
        half = hidden // 2
        part_a = after(jnp.concatenate([gate_piece, up_piece[:, :half]], 1), *blocks)
        part_b = after(jnp.concatenate([up_piece[:, half:], down_piece], 1), *blocks)
        high = dp_rows // 2
        high_a, high_b = part_a[:high], part_b[:high]
        xn1, high_a, high_b = lax.optimization_barrier((xn1, high_a, high_b))
        rest_of_weights = quad.gather_late(part_a, part_b, high_a, high_b)
    else:
        qkv_pieces, per_row = [lax.all_gather(qkv_piece, "dp", axis=0, tiled=True)], 1
        gate_up_full = lax.all_gather(
            jnp.concatenate([gate_piece, up_piece], 1), "dp", axis=0, tiled=True
        )
        down_full = lax.all_gather(down_piece, "dp", axis=0, tiled=True)

    cosine, sine = rotary_tables(length)
    attn, query, key, value, lse = attention_forward(
        xn1, qkv_pieces, per_row, cosine, sine, token_rows
    )

    dy = over_seq(after(dy_own, attn))

    def to_features(by_head):
        if strided:
            moved = exchange(by_head.reshape(-1, HD, token_rows), ("dp", "seq"))
        else:
            by_tokens = by_head.transpose(1, 0, 2, 3).reshape(group_count, width, token_rows)
            moved = exchange(exchange(by_tokens, "seq").reshape(dp_count, dp_rows, token_rows), "dp")
        return moved.reshape(dp_count, dp_rows, token_rows)

    def to_heads(features):
        if strided:
            moved = exchange(features.reshape(-1, HD, token_rows), ("dp", "seq"))
            return moved.reshape(-1, group_count, HD, token_rows)
        moved = exchange(features, "dp").reshape(group_count, width, token_rows)
        moved = exchange(moved, "seq").reshape(group_count, width // HD, HD, token_rows)
        return moved.transpose(1, 0, 2, 3)

    features = to_features(attn)
    if quad:
        parts = [
            contract_first(
                lax.dynamic_index_in_dim(features, member ^ k, 0, False), out_weight
            )
            for k in range(4)
        ]
        others = [partner(parts[k].astype(BF), k) for k in (1, 2, 3)]
        partials = (parts[0], *others)
    else:
        partials = (
            lax.psum_scatter(
                jnp.einsum("dft,fn->dtn", features, out_weight, preferred_element_type=F32)
                .astype(BF)
                .reshape(dp_count * token_rows, model_width),
                "dp", scatter_dimension=0, tiled=True,
            ).astype(F32),
        )

    hidden_res, xn2_own = on_rows(norm_mid_kernel, orders, (layer_in, *partials, gain2), (F32, BF))
    xn2 = over_seq(xn2_own)
    if quad:
        part_a, part_b = rest_of_weights(*partials)
        act, grad_gate_up, partial_xn2 = feed_forward(xn2, dy, part_a, part_b, hidden)
        feed_sum = feed_out(after(act, partial_xn2), part_b, model_width)
    else:
        act, grad_gate_up, partial_xn2 = feed_forward_plain(
            xn2, dy, gate_up_full, down_full, hidden
        )
        feed_sum = contract_last(act, down_full).astype(BF)
    raw_xn2 = sum_over_seq(partial_xn2)
    feed_sum = after(feed_sum, raw_xn2)
    grad_hidden, hidden_low = on_rows(
        norm_grad_kernel, places, (hidden_res, cotangent, raw_xn2, gain2), (F32, BF)
    )
    feed_sum = sum_over_seq(feed_sum)
    if quad:
        sides = (OVER_X_FIRST, OVER_Y_FIRST)
        down_sum = PairSum(*outer_blocks(dy, act, sides, 1))
        gate_sum = PairSum(*outer_blocks(xn2, grad_gate_up, sides, 1, 0))
        up_sum = PairSum(*outer_blocks(xn2, grad_gate_up, sides, 1, 1))
        rows_low = quad.gather_direct(hidden_low)
    else:
        down_rows = reduce_plain(dy, act)
        gate_rows = reduce_plain(xn2, grad_gate_up[:, :hidden])
        up_rows = reduce_plain(xn2, grad_gate_up[:, hidden:])
        rows_low = list(lax.all_gather(hidden_low, "dp", axis=0))

    grad_features = jnp.einsum(
        "fn,ktn->kft", out_weight, jnp.stack(rows_low), preferred_element_type=F32
    ).astype(BF)
    if quad:
        grad_features = jnp.stack(
            [lax.dynamic_index_in_dim(grad_features, member ^ j, 0, False) for j in range(4)]
        )
    grad_attn = to_heads(grad_features)
    if quad:
        down_sum.second()
        gate_sum.second()
        up_sum.second()
    if quad:
        out_rows = out_rows_grad(features, rows_low, blocks_at ^ member)
    else:
        out_rows = jnp.einsum(
            "kft,ktn->fn", features, jnp.stack(rows_low), preferred_element_type=F32
        ).astype(BF)
    out_grad = sum_over_seq(out_rows).astype(F32)
    grad_qkv, partial_xn1 = attention_backward(
        query, key, value, attn, grad_attn, lse, cosine, sine, qkv_pieces, per_row
    )
    raw_xn1 = sum_over_seq(partial_xn1)
    (input_grad,) = on_rows(
        norm_grad_kernel, places, (layer_in, grad_hidden, raw_xn1, gain1), (F32,)
    )
    (layer_out,) = on_rows(
        add_placed_kernel, places, (hidden_res, after(feed_sum, partial_xn1)), (F32,)
    )

    if quad:
        (blocks,) = outer_blocks(xn1, grad_qkv, (ONE_EACH,))
        qkv_rows = sum_direct(blocks)
        down_rows, gate_rows, up_rows = down_sum.total(), gate_sum.total(), up_sum.total()
    else:
        qkv_rows = reduce_plain(xn1, grad_qkv)
    near_parts = exchange_rows(jnp.concatenate([down_rows, gate_rows], 1), group_count)
    far_parts = exchange_rows(jnp.concatenate([up_rows, qkv_rows], 1), group_count)
    own_at = member * dp_rows + group * shard_rows
    own1 = lax.dynamic_slice_in_dim(gain1, own_at, shard_rows, 1)
    own2 = lax.dynamic_slice_in_dim(gain2, own_at, shard_rows, 1)
    down_grad, _ = side_rows([(near_parts, 0)], hidden, down_weight, own2, group)
    gate_up_grad, norm2_grad = side_rows(
        [(near_parts, 1), (far_parts, 0)], hidden, gate_up_weight, own2, group
    )
    if strided:
        qkv_grad, norm1_grad = strided_rows(far_parts, hidden, qkv_weight, own1, group)
    else:
        qkv_parts = far_parts[:, :, hidden:]
        qkv_grad, norm1_grad = side_rows(
            [(qkv_parts, i) for i in range(3)], width, qkv_weight, own1, group
        )

    return (
        layer_out,
        input_grad,
        norm1_grad.reshape(shard_rows),
        qkv_grad,
        out_grad,
        norm2_grad.reshape(shard_rows),
        gate_up_grad,
        down_grad,
    )


def solution(mesh):
    rows = P(("dp", "seq"), None)
    in_specs = (
        rows, P(), P("dp", None), P("dp", None), P(), P("dp", None), P("dp", None), rows,
    )
    vector = P(("dp", "seq"))
    out_specs = (rows, rows, vector, rows, rows, vector, rows, rows)
    return jax.shard_map(shards, mesh=mesh, in_specs=in_specs, out_specs=out_specs, check_vma=False)
```

```python
import functools

import jax
import jax.numpy as jnp
from jax import lax
from jax.experimental import pallas as pl
from jax.experimental.pallas import tpu as pltpu
from jax.sharding import PartitionSpec as P


HD = 64
EPS = 1e-05
THETA = 130000.0
BF = jnp.bfloat16
F32 = jnp.float32

GRAY = (0, 1, 3, 2)


def after(values, *earlier):
    return lax.optimization_barrier((values, *earlier))[0]


def rotary_kernel(inverse_ref, cos_ref, sin_ref):
    step = min(32, cos_ref.shape[0])

    @pl.loop(0, cos_ref.shape[0] // step)
    def _(i):
        at = pl.ds(pl.multiple_of(i * step, step), step)
        position = i * step + lax.broadcasted_iota(jnp.int32, (step, 128), 0)
        angles = position.astype(F32) * inverse_ref[...]
        lane = lax.broadcasted_iota(jnp.int32, (step, 128), 1)
        sine = jnp.sin(angles)
        cos_ref[at, :] = jnp.cos(angles)
        sin_ref[at, :] = jnp.where((lane & (HD // 2)) != 0, sine, -sine)


def rotary_tables(length):
    half = HD // 2
    inverse = THETA ** (-(jnp.arange(half).astype(F32) * 2.0) / HD)
    table = jax.ShapeDtypeStruct((length, 128), F32)
    return pl.pallas_call(rotary_kernel, out_shape=[table, table], name="rotary")(
        jnp.tile(inverse, 4)[None, :]
    )


def contract_last(left, right):
    return lax.dot_general(left, right, (((1,), (1,)), ((), ())), preferred_element_type=F32)


def contract_first(left, right):
    return lax.dot_general(left, right, (((0,), (0,)), ((), ())), preferred_element_type=F32)


def half_turn(values):
    lane = lax.broadcasted_iota(jnp.int32, values.shape, 1)
    upper = (lane & (HD // 2)) != 0
    return jnp.where(
        upper, pltpu.roll(values, HD // 2, 1), pltpu.roll(values, 128 - HD // 2, 1)
    )


def head_only(values, head):
    lane = lax.broadcasted_iota(jnp.int32, values.shape, 1)
    return jnp.where(lane // HD == head, values, jnp.zeros_like(values))


def causal(block):
    key_pos = lax.broadcasted_iota(jnp.int32, (block, block), 0)
    query_pos = lax.broadcasted_iota(jnp.int32, (block, block), 1)
    return key_pos <= query_pos


def assembled(pieces, per_row, target_ref, sems):
    copies, row = [], 0
    for first in range(0, len(pieces), per_row):
        column = 0
        for piece in pieces[first : first + per_row]:
            rows, columns = piece.shape
            place = target_ref.at[pl.ds(row, rows), pl.ds(column, columns)]
            copies.append(pltpu.make_async_copy(piece, place, sems.at[len(copies)]))
            column += columns
        row += rows
    return copies


def attention_forward_kernel(block, count, per_row, xn_ref, *refs):
    pieces, refs = refs[:count], refs[count:]
    cos_ref, sin_ref, attn_ref, q_ref, k_ref, v_ref, lse_ref, weight_ref, vt_ref, sems = refs
    head = pl.program_id(0)
    length, width = q_ref.shape
    tokens = attn_ref.shape[3]
    scale = HD ** (-0.5)

    @pl.when(head == 0)
    def _():
        copies = assembled(pieces, per_row, weight_ref, sems)
        for copy in copies:
            copy.start()
        for copy in copies:
            copy.wait()

        @pl.loop(0, length // block)
        def _(i):
            at = pl.ds(pl.multiple_of(i * block, block), block)
            qkv = jnp.dot(xn_ref[at, :], weight_ref[...], preferred_element_type=F32).astype(BF)
            v_ref[at, :] = qkv[:, 2 * width :]
            for c in range(width // 128):
                for source, target, factor in ((0, q_ref, scale), (width, k_ref, 1.0)):
                    u = qkv[:, source + c * 128 : source + (c + 1) * 128].astype(F32)
                    turned = u * cos_ref[at, :] + half_turn(u) * sin_ref[at, :]
                    target[at, c * 128 : (c + 1) * 128] = turned.astype(BF) * factor

        for c in range(width // 128):
            cols = slice(c * 128, (c + 1) * 128)
            vt_ref[cols, :] = v_ref[:, cols].astype(F32).T.astype(BF)

    rows = pl.ds(pl.multiple_of(head * HD, HD), HD)
    for i in range(length // block):
        low, high = i * block, (i + 1) * block
        query = head_only(q_ref[low:high, :], head)
        near = contract_last(k_ref[low:high, :], query)
        near = jnp.where(causal(block), near, -1e30)
        top = jnp.max(near, axis=0, keepdims=True)
        if i:
            far = contract_last(k_ref[0:low, :], query)
            top = jnp.maximum(top, jnp.max(far, axis=0, keepdims=True))
        near = jnp.exp(near - top)
        total = jnp.sum(near, axis=0, keepdims=True)
        mixed = jnp.dot(vt_ref[rows, low:high], near.astype(BF), preferred_element_type=F32)
        if i:
            far = jnp.exp(far - top)
            total = total + jnp.sum(far, axis=0, keepdims=True)
            mixed = mixed + jnp.dot(
                vt_ref[rows, 0:low], far.astype(BF), preferred_element_type=F32
            )
        mixed = (mixed / total).astype(BF)
        for part in range(block // tokens):
            attn_ref[head, low // tokens + part] = mixed[:, part * tokens : (part + 1) * tokens]
        lse_ref[pl.ds(head, 1), low:high] = top + jnp.log(total)


def attention_backward_kernel(
    block, count, per_row, paired, group_ref,
    q_ref, k_ref, v_ref, attn_ref, grad_ref, lse_ref, cos_ref, sin_ref, *refs
):
    pieces, refs = refs[:count], refs[count:]
    if paired:
        out_ref, mine_ref, theirs_ref, dxn_ref, half_sems, *refs = refs
    else:
        out_ref, dxn_ref, *refs = refs
    weight_ref, dq_ref, dk_ref, dv_ref, delta_ref, flat_ref, sems = refs
    head = pl.program_id(0)
    length, width = q_ref.shape
    tokens = attn_ref.shape[3]
    scale = HD ** (-0.5)

    @pl.when(head == 0)
    def _():
        for copy in assembled(pieces, per_row, weight_ref, sems):
            copy.start()
        dq_ref[...] = jnp.zeros_like(dq_ref)
        dk_ref[...] = jnp.zeros_like(dk_ref)
        dv_ref[...] = jnp.zeros_like(dv_ref)
        for c in range(width // 128):
            for j in range(length // tokens):
                pair = jnp.concatenate([grad_ref[2 * c, j], grad_ref[2 * c + 1, j]], 0)
                flat_ref[j * tokens : (j + 1) * tokens, c * 128 : (c + 1) * 128] = (
                    pair.astype(F32).T.astype(BF)
                )

    for j in range(length // tokens):
        product = grad_ref[head, j].astype(F32) * attn_ref[head, j].astype(F32)
        delta_ref[:, j * tokens : (j + 1) * tokens] = jnp.sum(product, axis=0, keepdims=True)

    def piece(keys, low, high, query, grad, diagonal):
        prob = jnp.exp(contract_last(k_ref[keys, :], query) - lse_ref[pl.ds(head, 1), low:high])
        if diagonal:
            prob = jnp.where(causal(block), prob, 0.0)
        dprob = contract_last(v_ref[keys, :], grad)
        dscore = (prob * (dprob - delta_ref[:, low:high])).astype(BF)
        dv_ref[keys, :] += jnp.dot(prob.astype(BF), grad, preferred_element_type=F32)
        dk_ref[keys, :] += jnp.dot(dscore, query, preferred_element_type=F32)
        dq_ref[low:high, :] += contract_first(dscore, head_only(k_ref[keys, :], head))

    for i in range(length // block):
        low, high = i * block, (i + 1) * block
        query = head_only(q_ref[low:high, :], head)
        grad = head_only(flat_ref[low:high, :], head)
        piece(slice(low, high), low, high, query, grad, True)
        if i:
            piece(slice(0, low), low, high, query, grad, False)

    @pl.when(head == pl.num_programs(0) - 1)
    def _():
        for copy in assembled(pieces, per_row, weight_ref, sems):
            copy.wait()

        @pl.loop(0, length // block)
        def _(i):
            at = pl.ds(pl.multiple_of(i * block, block), block)
            for c in range(width // 128):
                cols = slice(c * 128, (c + 1) * 128)
                for source, target, factor in ((dq_ref, 0, scale), (dk_ref, width, 1.0)):
                    u = source[at, cols] * factor
                    turned = u * cos_ref[at, :] - half_turn(u) * sin_ref[at, :]
                    out_ref[at, target + c * 128 : target + (c + 1) * 128] = turned.astype(BF)
            out_ref[at, 2 * width : 3 * width] = dv_ref[at, :].astype(BF)
            dxn_ref[at, :] = contract_last(out_ref[at, :], weight_ref[...]).astype(BF)

        if paired:
            copies = []
            for i in range(length // (2 * tokens)):
                to = pl.ds(i * tokens, tokens)
                for target, odd in ((theirs_ref, 1), (mine_ref, 0)):
                    row = 2 * i * tokens + (group_ref[0] % 2 ^ odd) * tokens
                    source = dxn_ref.at[pl.ds(pl.multiple_of(row, tokens), tokens)]
                    copies.append(
                        pltpu.make_async_copy(source, target.at[to], half_sems.at[len(copies)])
                    )
            for copy in copies:
                copy.start()
            for copy in copies:
                copy.wait()


def resident(shape):
    return pl.BlockSpec(shape, lambda h: tuple(0 for _ in shape))


def attention_forward(xn, pieces, per_row, cosine, sine, tokens):
    length, model_width = xn.shape
    width = sum(piece.shape[1] for piece in pieces[:per_row]) // 3
    heads = width // HD
    block = min(256, length)
    pairs = heads * length * length
    out = (heads, length // tokens, HD, tokens)
    return pl.pallas_call(
        functools.partial(attention_forward_kernel, block, len(pieces), per_row),
        grid=(heads,),
        in_specs=[resident(xn.shape)]
        + [pl.BlockSpec(memory_space=pl.ANY)] * len(pieces)
        + [resident(cosine.shape)] * 2,
        out_specs=[resident(out)] + [resident((length, width))] * 3 + [resident((8, length))],
        out_shape=[jax.ShapeDtypeStruct(out, BF)]
        + [jax.ShapeDtypeStruct((length, width), BF)] * 3
        + [jax.ShapeDtypeStruct((8, length), F32)],
        scratch_shapes=[
            pltpu.VMEM((model_width, 3 * width), BF),
            pltpu.VMEM((width, length), BF),
            pltpu.SemaphoreType.DMA((len(pieces),)),
        ],
        cost_estimate=pl.CostEstimate(
            flops=2 * pairs * HD + 6 * length * model_width * width,
            bytes_accessed=8 * length * width + 2 * model_width * (length + 3 * width),
            transcendentals=pairs // 2,
        ),
        name="attention_forward",
    )(xn, *pieces, cosine, sine)


def attention_backward(
    group, paired, query, key, value, attn, grad, lse, cosine, sine, pieces, per_row
):
    length, width = query.shape
    tokens = attn.shape[3]
    model_width = sum(piece.shape[0] for piece in pieces[::per_row])
    heads = width // HD
    block = min(256, length)
    pairs = heads * length * length
    flat = resident((length, width))
    anywhere = pl.BlockSpec(memory_space=pl.ANY)
    if paired:
        dxn_specs, dxn_shapes = [anywhere] * 2, [(length // 2, model_width)] * 2
        dxn_scratch = [
            pltpu.VMEM((length, model_width), BF), pltpu.SemaphoreType.DMA((length // tokens,))
        ]
    else:
        dxn_specs, dxn_shapes = [resident((length, model_width))], [(length, model_width)]
        dxn_scratch = []
    return pl.pallas_call(
        functools.partial(attention_backward_kernel, block, len(pieces), per_row, paired),
        grid=(heads,),
        in_specs=[pl.BlockSpec(memory_space=pltpu.SMEM)]
        + [flat, flat, flat, resident(attn.shape), resident(attn.shape)]
        + [resident((8, length))]
        + [resident(cosine.shape)] * 2
        + [anywhere] * len(pieces),
        out_specs=[resident((length, 3 * width))] + dxn_specs,
        out_shape=[
            jax.ShapeDtypeStruct(shape, BF) for shape in [(length, 3 * width)] + dxn_shapes
        ],
        scratch_shapes=dxn_scratch
        + [pltpu.VMEM((model_width, 3 * width), BF)]
        + [pltpu.VMEM((length, width), F32)] * 3
        + [
            pltpu.VMEM((1, length), F32),
            pltpu.VMEM((length, width), BF),
            pltpu.SemaphoreType.DMA((len(pieces),)),
        ],
        cost_estimate=pl.CostEstimate(
            flops=5 * pairs * HD + 6 * length * model_width * width,
            bytes_accessed=20 * length * width + 2 * model_width * (length + 3 * width),
            transcendentals=pairs // 2,
        ),
        name="attention_backward",
    )(group.reshape(1), query, key, value, attn, grad, lse, cosine, sine, *pieces)


def strided_heads_kernel(which_ref, *refs):
    runs, outs = refs[:-2], refs[-2:]
    parity = which_ref[0] % 2
    half = len(runs) // 2

    for odd in range(2):

        @pl.when(parity == odd)
        def _():
            cols = slice(odd * HD, (odd + 1) * HD)
            for out, first in zip(outs, (0, half)):
                for r in range(0, half, 2):
                    out[:, r * HD : (r + 2) * HD] = jnp.concatenate(
                        [runs[first + r][:, cols], runs[first + r + 1][:, cols]], 1
                    )


def strided_heads(weight, group, group_count):
    rows, columns = weight.shape
    run = group_count * HD // 128
    runs = columns // (group_count * HD)

    def spec(r):
        return pl.BlockSpec((rows, 128), lambda g, w: (0, r * run + w[0] // 2))

    half = (rows, runs // 2 * HD)
    return pl.pallas_call(
        strided_heads_kernel,
        grid_spec=pltpu.PrefetchScalarGridSpec(
            num_scalar_prefetch=1,
            grid=(1,),
            in_specs=[spec(r) for r in range(runs)],
            out_specs=[pl.BlockSpec(half, lambda g, w: (0, 0))] * 2,
        ),
        out_shape=[jax.ShapeDtypeStruct(half, weight.dtype)] * 2,
        name="strided_heads",
    )(group.reshape(1), *[weight] * runs)


def lane_sums(values):
    return jnp.sum(values.T, axis=0, keepdims=True)


def strided_rows_kernel(first, which_ref, in_ref, weight_ref, gain_ref, out_ref, sum_ref):
    groups, rows, width = in_ref.shape
    total = jnp.zeros((rows, 128), F32)
    for b in range((width - first) // HD):
        cols = slice(first + b * HD, first + (b + 1) * HD)
        for pair in range(groups // 2):
            both = jnp.concatenate(
                [in_ref[2 * pair, :, cols], in_ref[2 * pair + 1, :, cols]], 1
            ).astype(F32)
            at = (b * groups + 2 * pair) * HD
            out_ref[:, at : at + 128] = both
            total = total + both * weight_ref[:, at : at + 128].astype(F32)
    sum_ref[...] = lane_sums(total) / gain_ref[...]


def strided_rows(parts, first, weight, gain, group):
    _, rows, _ = parts.shape
    return pl.pallas_call(
        functools.partial(strided_rows_kernel, first),
        grid_spec=pltpu.PrefetchScalarGridSpec(
            num_scalar_prefetch=1,
            grid=(1,),
            in_specs=[
                pl.BlockSpec(parts.shape, lambda g, w: (0, 0, 0)),
                pl.BlockSpec((rows, weight.shape[1]), lambda g, w: (w[0], 0)),
                pl.BlockSpec((1, rows), lambda g, w: (0, 0)),
            ],
            out_specs=[
                pl.BlockSpec((rows, weight.shape[1]), lambda g, w: (0, 0)),
                pl.BlockSpec((1, rows), lambda g, w: (0, 0)),
            ],
        ),
        out_shape=[
            jax.ShapeDtypeStruct((rows, weight.shape[1]), F32),
            jax.ShapeDtypeStruct((1, rows), F32),
        ],
        name="strided_rows",
    )(group.reshape(1), parts, weight, gain)


def side_rows_kernel(runs, which_ref, *refs):
    parts, (weight_ref, gain_ref, out_ref, sum_ref) = refs[:runs], refs[runs:]
    groups, rows, piece = parts[0].shape

    @pl.when(pl.program_id(0) == 0)
    def _():
        sum_ref[...] = jnp.zeros_like(sum_ref)

    for run in range(runs):

        @pl.when(pl.program_id(0) == run)
        def _():
            def step(s, total):
                values = parts[run][s].astype(F32)
                cols = pl.ds(pl.multiple_of(s * piece, piece), piece)
                out_ref[:, cols] = values
                product = values * weight_ref[:, cols].astype(F32)
                for c in range(piece // 128):
                    total = total + product[:, c * 128 : (c + 1) * 128]
                return total

            total = lax.fori_loop(0, groups, step, jnp.zeros((rows, 128), F32))
            sum_ref[...] += lane_sums(total) / gain_ref[...]


def side_rows(parts, piece, weight, gain, group):
    groups, rows, _ = parts[0][0].shape
    runs = len(parts)

    def spec(place):
        return pl.BlockSpec((groups, rows, piece), lambda c, w: (0, 0, place))

    return pl.pallas_call(
        functools.partial(side_rows_kernel, runs),
        grid_spec=pltpu.PrefetchScalarGridSpec(
            num_scalar_prefetch=1,
            grid=(runs,),
            in_specs=[spec(place) for _, place in parts]
            + [
                pl.BlockSpec((rows, groups * piece), lambda c, w: (w[0], c)),
                pl.BlockSpec((1, rows), lambda c, w: (0, 0)),
            ],
            out_specs=[
                pl.BlockSpec((rows, groups * piece), lambda c, w: (0, c)),
                pl.BlockSpec((1, rows), lambda c, w: (0, 0)),
            ],
        ),
        out_shape=[
            jax.ShapeDtypeStruct((rows, runs * groups * piece), F32),
            jax.ShapeDtypeStruct((1, rows), F32),
        ],
        name="side_rows",
    )(group.reshape(1), *[array for array, _ in parts], weight, gain)


BLOCKS = 4


def at_block(ref, rows, index):
    width = ref.shape[1] // BLOCKS
    return ref.at[rows, pl.ds(pl.multiple_of(index * width, width), width)]


def by_rows(kernel):
    def run(table_ref, x_ref, *refs):
        step = min(32, x_ref.shape[0])

        @pl.loop(0, x_ref.shape[0] // step)
        def _(i):
            kernel(pl.ds(pl.multiple_of(i * step, step), step), table_ref, x_ref, *refs)

    return run


ALL = slice(None)


def norm_in_kernel(rows, orders_ref, x_ref, gain_ref, grad_ref, xn_ref, dy_ref):
    x = x_ref[rows, :]
    inv = lax.rsqrt(jnp.mean(x * x, axis=1, keepdims=True) + EPS)
    for p in range(BLOCKS):
        block = orders_ref[p]
        normed = at_block(x_ref, rows, block)[...] * inv * at_block(gain_ref, ALL, block)[...]
        at_block(xn_ref, rows, p)[...] = normed.astype(BF)
        at_block(dy_ref, rows, p)[...] = at_block(grad_ref, rows, block)[...].astype(BF)


def norm_mid_kernel(rows, orders_ref, x_ref, own_ref, *refs):
    others, (gain_ref, mid_ref, xn_ref) = refs[:-3], refs[-3:]
    mid = x_ref[rows, :] + own_ref[rows, :]
    for other in others:
        mid = mid + other[rows, :].astype(F32)
    mid_ref[rows, :] = mid
    inv = lax.rsqrt(jnp.mean(mid * mid, axis=1, keepdims=True) + EPS)
    for p in range(BLOCKS):
        block = orders_ref[p]
        normed = at_block(mid_ref, rows, block)[...] * inv * at_block(gain_ref, ALL, block)[...]
        at_block(xn_ref, rows, p)[...] = normed.astype(BF)


def norm_grad_kernel(rows, places_ref, x_ref, base_ref, grad_ref, gain_ref, out_ref, *low_ref):
    x = x_ref[rows, :]
    inv = lax.rsqrt(jnp.mean(x * x, axis=1, keepdims=True) + EPS)
    grad = jnp.concatenate(
        [at_block(grad_ref, rows, places_ref[j])[...] for j in range(BLOCKS)], 1
    ).astype(F32)
    normed = x * inv
    grad_hat = grad * gain_ref[...]
    mean = jnp.mean(grad_hat * normed, axis=1, keepdims=True)
    out = base_ref[rows, :] + inv * (grad_hat - normed * mean)
    out_ref[rows, :] = out
    for ref in low_ref:
        ref[rows, :] = out.astype(BF)


def add_placed_kernel(rows, places_ref, base_ref, part_ref, out_ref):
    for j in range(BLOCKS):
        part = at_block(part_ref, rows, places_ref[j])[...].astype(F32)
        at_block(out_ref, rows, j)[...] = at_block(base_ref, rows, j)[...] + part


def on_rows(kernel, table, inputs, out_types):
    rows, width = inputs[0].shape
    block = rows

    def spec(shape):
        if shape[0] == 1:
            return pl.BlockSpec(shape, lambda i, t: (0, 0))
        return pl.BlockSpec((block, width), lambda i, t: (i, 0))

    return pl.pallas_call(
        by_rows(kernel),
        grid_spec=pltpu.PrefetchScalarGridSpec(
            num_scalar_prefetch=1,
            grid=(rows // block,),
            in_specs=[spec(v.shape) for v in inputs],
            out_specs=[spec((rows, width)) for _ in out_types],
        ),
        out_shape=[jax.ShapeDtypeStruct((rows, width), t) for t in out_types],
    )(table, *inputs)


def placed(pieces, column, columns, target_ref, at_column, sems, copies):
    row = 0
    for piece in pieces:
        rows = piece.shape[0]
        source = piece.at[:, pl.ds(column, columns)]
        place = target_ref.at[pl.ds(row, rows), pl.ds(at_column, columns)]
        copies.append(pltpu.make_async_copy(source, place, sems.at[len(copies)]))
        row += rows


def feed_kernel(count_a, count_b, xn_ref, dy_ref, *refs):
    part_a, part_b, refs = refs[:count_a], refs[count_a : count_a + count_b], refs[count_a + count_b :]
    act_ref, grad_ref, dxn_ref, gate_up_ref, down_ref, sems = refs
    cut = part_a[0].shape[1]
    hidden = act_ref.shape[1]
    split = 2 * hidden - cut

    copies = []
    placed(part_a, 0, cut, gate_up_ref, 0, sems, copies)
    placed(part_b, 0, split, gate_up_ref, cut, sems, copies)
    placed(part_b, split, hidden, down_ref, 0, sems, copies)

    @pl.when(pl.program_id(0) == 0)
    def _():
        for copy in copies:
            copy.start()
        for copy in copies[: count_a + count_b]:
            copy.wait()

    gate_up = jnp.dot(xn_ref[...], gate_up_ref[...], preferred_element_type=F32)
    gate, up_part = gate_up[:, :hidden], gate_up[:, hidden:]
    sigmoid_gate = jax.nn.sigmoid(gate)
    gated = gate * sigmoid_gate
    act_ref[...] = (gated * up_part).astype(BF)

    @pl.when(pl.program_id(0) == 0)
    def _():
        for copy in copies[count_a + count_b :]:
            copy.wait()

    grad_act = jnp.dot(dy_ref[...], down_ref[...], preferred_element_type=F32)
    grad_gate = grad_act * up_part * sigmoid_gate * (1.0 + gate * (1.0 - sigmoid_gate))
    grad_ref[:, :hidden] = grad_gate.astype(BF)
    grad_ref[:, hidden:] = (grad_act * gated).astype(BF)
    columns_last(grad_ref, gate_up_ref, dxn_ref)


def columns_last(left_ref, right_ref, out_ref):
    chunk = min(1024, out_ref.shape[1])

    @pl.loop(0, out_ref.shape[1] // chunk)
    def _(c):
        at = pl.ds(pl.multiple_of(c * chunk, chunk), chunk)
        out_ref[:, at] = contract_last(left_ref[...], right_ref[at, :]).astype(BF)


OVER_X_FIRST = ((1, 3), (3, 4), (0, 1))
OVER_Y_FIRST = ((2, 4), (1, 2), (0, 1))
ONE_EACH = ((0, 1), (1, 2), (2, 3), (3, 4))


def outer_kernel(layouts, left_ref, right_ref, *out_refs):
    step = pl.program_id(0)
    steps = pl.num_programs(0) // 4
    product = contract_first(left_ref[...], right_ref[...]).astype(BF)
    column = 0
    refs = iter(out_refs)
    for layout in layouts:
        targets = [next(refs) for _ in layout]
        width = targets[0].shape[1]
        block = product[:, column : column + width]
        column += width
        for target, (first, end) in zip(targets, layout):

            @pl.when((step >= first * steps) & (step < end * steps))
            def _():
                target[...] = block


def outer_blocks(left, right, layouts, steps=2, side=None):
    tokens, rows = left.shape
    columns = right.shape[1] if side is None else right.shape[1] // 2
    width = columns // len(layouts)
    block = rows // (4 * steps)
    held = [blocks for layout in layouts for blocks in layout]

    def spec(first, end):
        return pl.BlockSpec(
            (block, width),
            lambda p: (jnp.clip(p - first * steps, 0, (end - first) * steps - 1), 0),
        )

    outs = pl.pallas_call(
        functools.partial(outer_kernel, layouts),
        grid=(4 * steps,),
        in_specs=[
            pl.BlockSpec((tokens, block), lambda p: (0, p)),
            pl.BlockSpec((tokens, columns), lambda p: (0, side or 0)),
        ],
        out_specs=[spec(*blocks) for blocks in held],
        out_shape=[
            jax.ShapeDtypeStruct(((end - first) * rows // 4, width), BF) for first, end in held
        ],
        cost_estimate=pl.CostEstimate(
            flops=2 * tokens * rows * columns,
            bytes_accessed=2 * (tokens * (rows + columns) + rows * columns),
            transcendentals=0,
        ),
        name="outer_blocks",
    )(left, right)
    outs = iter(outs)
    return [[next(outs) for _ in layout] for layout in layouts]


def in_order(parts):
    return [piece for k in GRAY for piece in parts[k]]


def feed_forward(xn, dy, part_a, part_b, hidden):
    tokens, model_width = xn.shape
    block = min(256, tokens)
    part_a, part_b = in_order(part_a), in_order(part_b)

    def blocks(columns):
        return pl.BlockSpec((block, columns), lambda i: (i, 0))

    return pl.pallas_call(
        functools.partial(feed_kernel, len(part_a), len(part_b)),
        grid=(tokens // block,),
        in_specs=[blocks(model_width)] * 2
        + [pl.BlockSpec(memory_space=pl.ANY)] * (len(part_a) + len(part_b)),
        out_specs=[blocks(hidden), blocks(2 * hidden), blocks(model_width)],
        out_shape=[
            jax.ShapeDtypeStruct((tokens, columns), BF)
            for columns in (hidden, 2 * hidden, model_width)
        ],
        scratch_shapes=[
            pltpu.VMEM((model_width, 2 * hidden), BF),
            pltpu.VMEM((model_width, hidden), BF),
            pltpu.SemaphoreType.DMA((len(part_a) + 2 * len(part_b),)),
        ],
        cost_estimate=pl.CostEstimate(
            flops=10 * tokens * model_width * hidden,
            bytes_accessed=2 * (4 * tokens * model_width + 3 * model_width * hidden),
            transcendentals=tokens * hidden,
        ),
        name="feed_forward",
    )(xn, dy, *part_a, *part_b)


def feed_out_kernel(count, group_ref, act_ref, *refs):
    pieces, (mine_ref, theirs_ref, out_ref, down_ref, sems) = refs[:count], refs[count:]
    hidden = act_ref.shape[1]
    tokens = mine_ref.shape[0]

    @pl.when(pl.program_id(0) == 0)
    def _():
        copies = []
        placed(pieces, pieces[0].shape[1] - hidden, hidden, down_ref, 0, sems, copies)
        for copy in copies:
            copy.start()
        for copy in copies:
            copy.wait()

    columns_last(act_ref, down_ref, out_ref)
    odd = group_ref[0] % 2
    mine_ref[...] = out_ref[pl.ds(pl.multiple_of(odd * tokens, tokens), tokens), :]
    theirs_ref[...] = out_ref[pl.ds(pl.multiple_of((1 - odd) * tokens, tokens), tokens), :]


def feed_out(act, part_b, model_width, group, run):
    tokens, hidden = act.shape
    block = 2 * run
    pieces = in_order(part_b)
    half = jax.ShapeDtypeStruct((tokens // 2, model_width), BF)
    return pl.pallas_call(
        functools.partial(feed_out_kernel, len(pieces)),
        grid=(tokens // block,),
        in_specs=[pl.BlockSpec(memory_space=pltpu.SMEM)]
        + [pl.BlockSpec((block, hidden), lambda i: (i, 0))]
        + [pl.BlockSpec(memory_space=pl.ANY)] * len(pieces),
        out_specs=[pl.BlockSpec((run, model_width), lambda i: (i, 0))] * 2,
        out_shape=[half, half],
        scratch_shapes=[
            pltpu.VMEM((block, model_width), BF),
            pltpu.VMEM((model_width, hidden), BF),
            pltpu.SemaphoreType.DMA((len(pieces),)),
        ],
        cost_estimate=pl.CostEstimate(
            flops=2 * tokens * model_width * hidden,
            bytes_accessed=2 * (tokens + model_width) * hidden + 2 * tokens * model_width,
            transcendentals=0,
        ),
        name="feed_out",
    )(group.reshape(1), act, *pieces)


def rows_by_member(pieces, places_ref, target_ref, sems):
    height = pieces[0].shape[0]
    copies = [
        pltpu.make_async_copy(
            piece,
            target_ref.at[pl.ds(pl.multiple_of(places_ref[k] * height, height), height)],
            sems.at[k],
        )
        for k, piece in enumerate(pieces)
    ]
    for copy in copies:
        copy.start()
    for copy in copies:
        copy.wait()


def out_rows_kernel(members_ref, features_ref, *refs):
    pieces, (out_ref, rows_ref, sems) = refs[:4], refs[4:]
    rows_by_member(pieces, members_ref, rows_ref, sems)
    left = jnp.concatenate([features_ref[d] for d in range(4)], 1)
    chunk = 512

    @pl.loop(0, out_ref.shape[1] // chunk)
    def _(c):
        at = pl.ds(pl.multiple_of(c * chunk, chunk), chunk)
        out_ref[:, at] = jnp.dot(left, rows_ref[:, at], preferred_element_type=F32).astype(BF)


def out_rows_grad(features, pieces, members):
    tokens, width = pieces[0].shape
    count = features.shape[1]
    return pl.pallas_call(
        out_rows_kernel,
        grid_spec=pltpu.PrefetchScalarGridSpec(
            num_scalar_prefetch=1,
            grid=(1,),
            in_specs=[pl.BlockSpec(features.shape, lambda i, m: (0, 0, 0))]
            + [pl.BlockSpec(memory_space=pl.ANY)] * 4,
            out_specs=pl.BlockSpec((count, width), lambda i, m: (0, 0)),
            scratch_shapes=[pltpu.VMEM((4 * tokens, width), BF), pltpu.SemaphoreType.DMA((4,))],
        ),
        out_shape=jax.ShapeDtypeStruct((count, width), BF),
        name="out_rows",
    )(members, features, *pieces)


def partner(array, bits):
    return lax.ppermute(array, "dp", [(i, i ^ bits) for i in range(4)])


class Quad:
    def __init__(self, index):
        self.index = index

    def gather_direct(self, block):
        return [block] + [partner(block, k) for k in (1, 2, 3)]

    def gather(self, first, second):
        a = {0: [first], 1: [partner(first, 1)]}
        b = {0: [second], 2: [partner(second, 2)]}
        a[2], b[1] = [partner(first, 2)], [partner(second, 1)]
        a[3], b[3] = [partner(a[1][0], 2)], [partner(b[2][0], 1)]
        return a, b

    def gather_late(self, first, second, first_high, second_high):
        rows = first_high.shape[0]
        a = {0: [first], 1: [partner(first, 1)]}
        b = {0: [second], 2: [partner(second, 2)]}
        a[2], b[1] = [partner(first_high, 2)], [partner(second_high, 1)]

        def late(*earlier):
            first_low, second_low, near_a, near_b = (
                after(v, *earlier) for v in (first[rows:], second[rows:], a[1][0], b[2][0])
            )
            a[2].append(partner(first_low, 2))
            b[1].append(partner(second_low, 1))
            a[3], b[3] = [partner(near_a, 2)], [partner(near_b, 1)]
            return a, b

        return late


def add(*terms):
    total = terms[0].astype(F32)
    for term in terms[1:]:
        total = total + term.astype(F32)
    return total.astype(BF)


class PairSum:
    def __init__(self, first, second):
        (send_a, *self.keep_a), (send_b, *self.keep_b) = first, second
        self.sent_a = partner(send_a, 1)
        self.sent_b = partner(send_b, 2)

    def second(self):
        rows = self.keep_a[0].shape[0]
        send_a = add(self.keep_a[0], self.sent_a[rows:])
        send_b = add(self.keep_b[0], self.sent_b[:rows])
        self.far_a = partner(send_a, 2)
        self.far_b = partner(send_b, 1)

    def total(self):
        rows = self.keep_a[0].shape[0]
        return jnp.concatenate(
            [
                add(self.keep_a[1], self.sent_a[:rows], self.far_a),
                add(self.keep_b[1], self.sent_b[rows:], self.far_b),
            ],
            1,
        )


def sum_direct(blocks):
    others = [partner(blocks[p], GRAY[p]) for p in (1, 2, 3)]
    return add(blocks[0], *others)


def reduce_plain(left, right):
    return lax.psum_scatter(
        contract_first(left, right).astype(BF), "dp", scatter_dimension=0, tiled=True
    )


def over_seq(values):
    return lax.all_gather(values, "seq", axis=0, tiled=True)


def sum_over_seq(values):
    return lax.psum_scatter(values.astype(BF), "seq", scatter_dimension=0, tiled=True)


def sum_over_pairs(mine, theirs, group_count, *earlier):
    received = lax.ppermute(theirs, "seq", [(i, i ^ 1) for i in range(group_count)])
    total = after(add(mine, received), *earlier)
    return lax.psum_scatter(
        total, "seq", scatter_dimension=0, tiled=True,
        axis_index_groups=[list(range(odd, group_count, 2)) for odd in range(2)],
    )


def exchange(values, axes):
    return lax.all_to_all(values, axes, split_axis=0, concat_axis=0, tiled=True)


def exchange_rows(values, group_count):
    return exchange(
        values.reshape(group_count, values.shape[0] // group_count, values.shape[1]), "seq"
    )


def feed_forward_plain(xn, dy, gate_up_full, down_full, hidden):
    gate_up = jnp.dot(xn, gate_up_full, preferred_element_type=F32)
    gate, up_part = gate_up[:, :hidden], gate_up[:, hidden:]
    sigmoid_gate = jax.nn.sigmoid(gate)
    act = (gate * sigmoid_gate * up_part).astype(BF)
    grad_act = jnp.dot(dy, down_full, preferred_element_type=F32)
    grad_gate = grad_act * up_part * sigmoid_gate * (1.0 + gate * (1.0 - sigmoid_gate))
    grad_up = grad_act * gate * sigmoid_gate
    grad_gate_up = jnp.concatenate([grad_gate, grad_up], 1).astype(BF)
    return act, grad_gate_up, contract_last(grad_gate_up, gate_up_full).astype(BF)


def shards(
    layer_in, norm1_gain, qkv_weight, out_weight, norm2_gain, gate_up_weight, down_weight, cotangent
):
    token_rows, model_width = layer_in.shape
    group_count = lax.axis_size("seq")
    dp_count = lax.axis_size("dp")
    group = lax.axis_index("seq")
    member = lax.axis_index("dp")
    length = token_rows * group_count
    dp_rows = model_width // dp_count
    shard_rows = dp_rows // group_count
    hidden_units = down_weight.shape[1]
    hidden = hidden_units // group_count
    width = model_width // group_count
    quad = Quad(member) if dp_count == 4 else None
    strided = quad is not None and shard_rows == HD

    blocks_at = jnp.arange(4, dtype=jnp.int32)
    if quad:
        orders = (blocks_at ^ (blocks_at >> 1)) ^ member
        places = blocks_at ^ member
        places = places ^ (places >> 1)
    else:
        orders, places = blocks_at, blocks_at
    gain1, gain2 = norm1_gain[None, :], norm2_gain[None, :]

    xn1_own, dy_own = on_rows(norm_in_kernel, orders, (layer_in, gain1, cotangent), (BF, BF))
    xn1 = over_seq(xn1_own)

    if strided:
        left, right = strided_heads(qkv_weight, group, group_count)
    else:
        qkv_piece = jnp.concatenate(
            [
                lax.dynamic_slice_in_dim(qkv_weight, part * model_width + group * width, width, 1)
                for part in range(3)
            ],
            1,
        )
    gate_piece = lax.dynamic_slice_in_dim(gate_up_weight, group * hidden, hidden, 1)
    up_piece = lax.dynamic_slice_in_dim(gate_up_weight, hidden_units + group * hidden, hidden, 1)
    down_piece = lax.dynamic_slice_in_dim(down_weight, group * hidden, hidden, 1)
    if quad:
        if not strided:
            cut = qkv_piece.shape[1] // 2
            left, right = qkv_piece[:, :cut], qkv_piece[:, cut:]
        left, right = quad.gather(left, right)
        blocks = (left[3][0], right[3][0])
        qkv_pieces = [part[k][0] for k in GRAY for part in (left, right)]
        per_row = 2
        half = hidden // 2
        part_a = after(jnp.concatenate([gate_piece, up_piece[:, :half]], 1), *blocks)
        part_b = after(jnp.concatenate([up_piece[:, half:], down_piece], 1), *blocks)
        high = dp_rows // 2
        high_a, high_b = part_a[:high], part_b[:high]
        xn1, high_a, high_b = lax.optimization_barrier((xn1, high_a, high_b))
        rest_of_weights = quad.gather_late(part_a, part_b, high_a, high_b)
    else:
        qkv_pieces, per_row = [lax.all_gather(qkv_piece, "dp", axis=0, tiled=True)], 1
        gate_up_full = lax.all_gather(
            jnp.concatenate([gate_piece, up_piece], 1), "dp", axis=0, tiled=True
        )
        down_full = lax.all_gather(down_piece, "dp", axis=0, tiled=True)

    cosine, sine = rotary_tables(length)
    attn, query, key, value, lse = attention_forward(
        xn1, qkv_pieces, per_row, cosine, sine, token_rows
    )

    dy = over_seq(after(dy_own, attn))

    def to_features(by_head):
        if strided:
            moved = exchange(by_head.reshape(-1, HD, token_rows), ("dp", "seq"))
        else:
            by_tokens = by_head.transpose(1, 0, 2, 3).reshape(group_count, width, token_rows)
            moved = exchange(exchange(by_tokens, "seq").reshape(dp_count, dp_rows, token_rows), "dp")
        return moved.reshape(dp_count, dp_rows, token_rows)

    def to_heads(features):
        if strided:
            moved = exchange(features.reshape(-1, HD, token_rows), ("dp", "seq"))
            return moved.reshape(-1, group_count, HD, token_rows)
        moved = exchange(features, "dp").reshape(group_count, width, token_rows)
        moved = exchange(moved, "seq").reshape(group_count, width // HD, HD, token_rows)
        return moved.transpose(1, 0, 2, 3)

    features = to_features(attn)
    if quad:
        parts = [
            contract_first(
                lax.dynamic_index_in_dim(features, member ^ k, 0, False), out_weight
            )
            for k in range(4)
        ]
        others = [partner(parts[k].astype(BF), k) for k in (1, 2, 3)]
        partials = (parts[0], *others)
    else:
        partials = (
            lax.psum_scatter(
                jnp.einsum("dft,fn->dtn", features, out_weight, preferred_element_type=F32)
                .astype(BF)
                .reshape(dp_count * token_rows, model_width),
                "dp", scatter_dimension=0, tiled=True,
            ).astype(F32),
        )

    hidden_res, xn2_own = on_rows(norm_mid_kernel, orders, (layer_in, *partials, gain2), (F32, BF))
    xn2 = over_seq(xn2_own)
    if quad:
        part_a, part_b = rest_of_weights(*partials)
        act, grad_gate_up, partial_xn2 = feed_forward(xn2, dy, part_a, part_b, hidden)
        feed_halves = feed_out(after(act, partial_xn2), part_b, model_width, group, token_rows)
    else:
        act, grad_gate_up, partial_xn2 = feed_forward_plain(
            xn2, dy, gate_up_full, down_full, hidden
        )
        feed_sum = contract_last(act, down_full).astype(BF)
    raw_xn2 = sum_over_seq(partial_xn2)
    grad_hidden, hidden_low = on_rows(
        norm_grad_kernel, places, (hidden_res, cotangent, raw_xn2, gain2), (F32, BF)
    )
    if quad:
        feed_sum = sum_over_pairs(*feed_halves, group_count, raw_xn2)
    else:
        feed_sum = sum_over_seq(after(feed_sum, raw_xn2))
    if quad:
        sides = (OVER_X_FIRST, OVER_Y_FIRST)
        down_sum = PairSum(*outer_blocks(dy, act, sides, 1))
        gate_sum = PairSum(*outer_blocks(xn2, grad_gate_up, sides, 1, 0))
        up_sum = PairSum(*outer_blocks(xn2, grad_gate_up, sides, 1, 1))
        rows_low = quad.gather_direct(hidden_low)
    else:
        down_rows = reduce_plain(dy, act)
        gate_rows = reduce_plain(xn2, grad_gate_up[:, :hidden])
        up_rows = reduce_plain(xn2, grad_gate_up[:, hidden:])
        rows_low = list(lax.all_gather(hidden_low, "dp", axis=0))

    grad_features = jnp.einsum(
        "fn,ktn->kft", out_weight, jnp.stack(rows_low), preferred_element_type=F32
    ).astype(BF)
    if quad:
        grad_features = jnp.stack(
            [lax.dynamic_index_in_dim(grad_features, member ^ j, 0, False) for j in range(4)]
        )
    grad_attn = to_heads(grad_features)
    if quad:
        down_sum.second()
        gate_sum.second()
        up_sum.second()
    if quad:
        out_rows = out_rows_grad(features, rows_low, blocks_at ^ member)
    else:
        out_rows = jnp.einsum(
            "kft,ktn->fn", features, jnp.stack(rows_low), preferred_element_type=F32
        ).astype(BF)
    out_grad = sum_over_seq(out_rows).astype(F32)
    grad_qkv, partial_xn1 = attention_backward(
        group, False,
        query, key, value, attn, grad_attn, lse, cosine, sine, qkv_pieces, per_row,
    )
    raw_xn1 = sum_over_seq(partial_xn1)
    (input_grad,) = on_rows(
        norm_grad_kernel, places, (layer_in, grad_hidden, raw_xn1, gain1), (F32,)
    )
    (layer_out,) = on_rows(
        add_placed_kernel, places, (hidden_res, after(feed_sum, grad_qkv)), (F32,)
    )

    if quad:
        (blocks,) = outer_blocks(xn1, grad_qkv, (ONE_EACH,))
        qkv_rows = sum_direct(blocks)
        down_rows, gate_rows, up_rows = down_sum.total(), gate_sum.total(), up_sum.total()
    else:
        qkv_rows = reduce_plain(xn1, grad_qkv)
    near_parts = exchange_rows(jnp.concatenate([down_rows, gate_rows], 1), group_count)
    far_parts = exchange_rows(jnp.concatenate([up_rows, qkv_rows], 1), group_count)
    own_at = member * dp_rows + group * shard_rows
    own1 = lax.dynamic_slice_in_dim(gain1, own_at, shard_rows, 1)
    own2 = lax.dynamic_slice_in_dim(gain2, own_at, shard_rows, 1)
    down_grad, _ = side_rows([(near_parts, 0)], hidden, down_weight, own2, group)
    gate_up_grad, norm2_grad = side_rows(
        [(near_parts, 1), (far_parts, 0)], hidden, gate_up_weight, own2, group
    )
    if strided:
        qkv_grad, norm1_grad = strided_rows(far_parts, hidden, qkv_weight, own1, group)
    else:
        qkv_parts = far_parts[:, :, hidden:]
        qkv_grad, norm1_grad = side_rows(
            [(qkv_parts, i) for i in range(3)], width, qkv_weight, own1, group
        )

    return (
        layer_out,
        input_grad,
        norm1_grad.reshape(shard_rows),
        qkv_grad,
        out_grad,
        norm2_grad.reshape(shard_rows),
        gate_up_grad,
        down_grad,
    )


def solution(mesh):
    rows = P(("dp", "seq"), None)
    in_specs = (
        rows, P(), P("dp", None), P("dp", None), P(), P("dp", None), P("dp", None), rows,
    )
    vector = P(("dp", "seq"))
    out_specs = (rows, rows, vector, rows, rows, vector, rows, rows)
    return jax.shard_map(shards, mesh=mesh, in_specs=in_specs, out_specs=out_specs, check_vma=False)
```

```python
import functools

import jax
import jax.numpy as jnp
from jax import lax
from jax.experimental import pallas as pl
from jax.experimental.pallas import tpu as pltpu
from jax.sharding import PartitionSpec as P


HD = 64
EPS = 1e-05
THETA = 130000.0
BF = jnp.bfloat16
F32 = jnp.float32

GRAY = (0, 1, 3, 2)


def after(values, *earlier):
    return lax.optimization_barrier((values, *earlier))[0]


def rotary_kernel(inverse_ref, cos_ref, sin_ref):
    step = min(32, cos_ref.shape[0])

    @pl.loop(0, cos_ref.shape[0] // step)
    def _(i):
        at = pl.ds(pl.multiple_of(i * step, step), step)
        position = i * step + lax.broadcasted_iota(jnp.int32, (step, 128), 0)
        angles = position.astype(F32) * inverse_ref[...]
        lane = lax.broadcasted_iota(jnp.int32, (step, 128), 1)
        sine = jnp.sin(angles)
        cos_ref[at, :] = jnp.cos(angles)
        sin_ref[at, :] = jnp.where((lane & (HD // 2)) != 0, sine, -sine)


def rotary_tables(length):
    half = HD // 2
    inverse = THETA ** (-(jnp.arange(half).astype(F32) * 2.0) / HD)
    table = jax.ShapeDtypeStruct((length, 128), F32)
    return pl.pallas_call(rotary_kernel, out_shape=[table, table], name="rotary")(
        jnp.tile(inverse, 4)[None, :]
    )


def contract_last(left, right):
    return lax.dot_general(left, right, (((1,), (1,)), ((), ())), preferred_element_type=F32)


def contract_first(left, right):
    return lax.dot_general(left, right, (((0,), (0,)), ((), ())), preferred_element_type=F32)


def half_turn(values):
    lane = lax.broadcasted_iota(jnp.int32, values.shape, 1)
    upper = (lane & (HD // 2)) != 0
    return jnp.where(
        upper, pltpu.roll(values, HD // 2, 1), pltpu.roll(values, 128 - HD // 2, 1)
    )


def head_only(values, head):
    lane = lax.broadcasted_iota(jnp.int32, values.shape, 1)
    return jnp.where(lane // HD == head, values, jnp.zeros_like(values))


def causal(block):
    key_pos = lax.broadcasted_iota(jnp.int32, (block, block), 0)
    query_pos = lax.broadcasted_iota(jnp.int32, (block, block), 1)
    return key_pos <= query_pos


def assembled(pieces, per_row, target_ref, sems):
    copies, row = [], 0
    for first in range(0, len(pieces), per_row):
        column = 0
        for piece in pieces[first : first + per_row]:
            rows, columns = piece.shape
            place = target_ref.at[pl.ds(row, rows), pl.ds(column, columns)]
            copies.append(pltpu.make_async_copy(piece, place, sems.at[len(copies)]))
            column += columns
        row += rows
    return copies


def attention_forward_kernel(block, count, per_row, xn_ref, *refs):
    pieces, refs = refs[:count], refs[count:]
    cos_ref, sin_ref, attn_ref, q_ref, k_ref, v_ref, lse_ref, weight_ref, vt_ref, sems = refs
    head = pl.program_id(0)
    length, width = q_ref.shape
    tokens = attn_ref.shape[3]
    scale = HD ** (-0.5)

    @pl.when(head == 0)
    def _():
        copies = assembled(pieces, per_row, weight_ref, sems)
        for copy in copies:
            copy.start()
        for copy in copies:
            copy.wait()

        @pl.loop(0, length // block)
        def _(i):
            at = pl.ds(pl.multiple_of(i * block, block), block)
            qkv = jnp.dot(xn_ref[at, :], weight_ref[...], preferred_element_type=F32).astype(BF)
            v_ref[at, :] = qkv[:, 2 * width :]
            for c in range(width // 128):
                for source, target, factor in ((0, q_ref, scale), (width, k_ref, 1.0)):
                    u = qkv[:, source + c * 128 : source + (c + 1) * 128].astype(F32)
                    turned = u * cos_ref[at, :] + half_turn(u) * sin_ref[at, :]
                    target[at, c * 128 : (c + 1) * 128] = turned.astype(BF) * factor

        for c in range(width // 128):
            cols = slice(c * 128, (c + 1) * 128)
            vt_ref[cols, :] = v_ref[:, cols].astype(F32).T.astype(BF)

    rows = pl.ds(pl.multiple_of(head * HD, HD), HD)
    for i in range(length // block):
        low, high = i * block, (i + 1) * block
        query = head_only(q_ref[low:high, :], head)
        near = contract_last(k_ref[low:high, :], query)
        near = jnp.where(causal(block), near, -1e30)
        top = jnp.max(near, axis=0, keepdims=True)
        if i:
            far = contract_last(k_ref[0:low, :], query)
            top = jnp.maximum(top, jnp.max(far, axis=0, keepdims=True))
        near = jnp.exp(near - top)
        total = jnp.sum(near, axis=0, keepdims=True)
        mixed = jnp.dot(vt_ref[rows, low:high], near.astype(BF), preferred_element_type=F32)
        if i:
            far = jnp.exp(far - top)
            total = total + jnp.sum(far, axis=0, keepdims=True)
            mixed = mixed + jnp.dot(
                vt_ref[rows, 0:low], far.astype(BF), preferred_element_type=F32
            )
        mixed = (mixed / total).astype(BF)
        for part in range(block // tokens):
            attn_ref[head, low // tokens + part] = mixed[:, part * tokens : (part + 1) * tokens]
        lse_ref[pl.ds(head, 1), low:high] = top + jnp.log(total)


def attention_backward_kernel(
    block, count, per_row, paired, group_ref,
    q_ref, k_ref, v_ref, attn_ref, grad_ref, lse_ref, cos_ref, sin_ref, *refs
):
    pieces, refs = refs[:count], refs[count:]
    if paired:
        out_ref, mine_ref, theirs_ref, dxn_ref, half_sems, *refs = refs
    else:
        out_ref, dxn_ref, *refs = refs
    weight_ref, dq_ref, dk_ref, dv_ref, delta_ref, flat_ref, sems = refs
    head = pl.program_id(0)
    length, width = q_ref.shape
    tokens = attn_ref.shape[3]
    scale = HD ** (-0.5)

    @pl.when(head == 0)
    def _():
        for copy in assembled(pieces, per_row, weight_ref, sems):
            copy.start()
        dq_ref[...] = jnp.zeros_like(dq_ref)
        dk_ref[...] = jnp.zeros_like(dk_ref)
        dv_ref[...] = jnp.zeros_like(dv_ref)
        for c in range(width // 128):
            for j in range(length // tokens):
                pair = jnp.concatenate([grad_ref[2 * c, j], grad_ref[2 * c + 1, j]], 0)
                flat_ref[j * tokens : (j + 1) * tokens, c * 128 : (c + 1) * 128] = (
                    pair.astype(F32).T.astype(BF)
                )

    for j in range(length // tokens):
        product = grad_ref[head, j].astype(F32) * attn_ref[head, j].astype(F32)
        delta_ref[:, j * tokens : (j + 1) * tokens] = jnp.sum(product, axis=0, keepdims=True)

    def piece(keys, low, high, query, grad, diagonal):
        prob = jnp.exp(contract_last(k_ref[keys, :], query) - lse_ref[pl.ds(head, 1), low:high])
        if diagonal:
            prob = jnp.where(causal(block), prob, 0.0)
        dprob = contract_last(v_ref[keys, :], grad)
        dscore = (prob * (dprob - delta_ref[:, low:high])).astype(BF)
        dv_ref[keys, :] += jnp.dot(prob.astype(BF), grad, preferred_element_type=F32)
        dk_ref[keys, :] += jnp.dot(dscore, query, preferred_element_type=F32)
        dq_ref[low:high, :] += contract_first(dscore, head_only(k_ref[keys, :], head))

    for i in range(length // block):
        low, high = i * block, (i + 1) * block
        query = head_only(q_ref[low:high, :], head)
        grad = head_only(flat_ref[low:high, :], head)
        piece(slice(low, high), low, high, query, grad, True)
        if i:
            piece(slice(0, low), low, high, query, grad, False)

    @pl.when(head == pl.num_programs(0) - 1)
    def _():
        for copy in assembled(pieces, per_row, weight_ref, sems):
            copy.wait()

        @pl.loop(0, length // block)
        def _(i):
            at = pl.ds(pl.multiple_of(i * block, block), block)
            for c in range(width // 128):
                cols = slice(c * 128, (c + 1) * 128)
                for source, target, factor in ((dq_ref, 0, scale), (dk_ref, width, 1.0)):
                    u = source[at, cols] * factor
                    turned = u * cos_ref[at, :] - half_turn(u) * sin_ref[at, :]
                    out_ref[at, target + c * 128 : target + (c + 1) * 128] = turned.astype(BF)
            out_ref[at, 2 * width : 3 * width] = dv_ref[at, :].astype(BF)
            dxn_ref[at, :] = contract_last(out_ref[at, :], weight_ref[...]).astype(BF)

        if paired:
            copies = []
            for i in range(length // (2 * tokens)):
                to = pl.ds(i * tokens, tokens)
                for target, odd in ((theirs_ref, 1), (mine_ref, 0)):
                    row = 2 * i * tokens + (group_ref[0] % 2 ^ odd) * tokens
                    source = dxn_ref.at[pl.ds(pl.multiple_of(row, tokens), tokens)]
                    copies.append(
                        pltpu.make_async_copy(source, target.at[to], half_sems.at[len(copies)])
                    )
            for copy in copies:
                copy.start()
            for copy in copies:
                copy.wait()


def resident(shape):
    return pl.BlockSpec(shape, lambda h: tuple(0 for _ in shape))


def attention_forward(xn, pieces, per_row, cosine, sine, tokens):
    length, model_width = xn.shape
    width = sum(piece.shape[1] for piece in pieces[:per_row]) // 3
    heads = width // HD
    block = min(256, length)
    pairs = heads * length * length
    out = (heads, length // tokens, HD, tokens)
    return pl.pallas_call(
        functools.partial(attention_forward_kernel, block, len(pieces), per_row),
        grid=(heads,),
        in_specs=[resident(xn.shape)]
        + [pl.BlockSpec(memory_space=pl.ANY)] * len(pieces)
        + [resident(cosine.shape)] * 2,
        out_specs=[resident(out)] + [resident((length, width))] * 3 + [resident((8, length))],
        out_shape=[jax.ShapeDtypeStruct(out, BF)]
        + [jax.ShapeDtypeStruct((length, width), BF)] * 3
        + [jax.ShapeDtypeStruct((8, length), F32)],
        scratch_shapes=[
            pltpu.VMEM((model_width, 3 * width), BF),
            pltpu.VMEM((width, length), BF),
            pltpu.SemaphoreType.DMA((len(pieces),)),
        ],
        cost_estimate=pl.CostEstimate(
            flops=2 * pairs * HD + 6 * length * model_width * width,
            bytes_accessed=8 * length * width + 2 * model_width * (length + 3 * width),
            transcendentals=pairs // 2,
        ),
        name="attention_forward",
    )(xn, *pieces, cosine, sine)


def attention_backward(
    group, paired, query, key, value, attn, grad, lse, cosine, sine, pieces, per_row
):
    length, width = query.shape
    tokens = attn.shape[3]
    model_width = sum(piece.shape[0] for piece in pieces[::per_row])
    heads = width // HD
    block = min(256, length)
    pairs = heads * length * length
    flat = resident((length, width))
    anywhere = pl.BlockSpec(memory_space=pl.ANY)
    if paired:
        dxn_specs, dxn_shapes = [anywhere] * 2, [(length // 2, model_width)] * 2
        dxn_scratch = [
            pltpu.VMEM((length, model_width), BF), pltpu.SemaphoreType.DMA((length // tokens,))
        ]
    else:
        dxn_specs, dxn_shapes = [resident((length, model_width))], [(length, model_width)]
        dxn_scratch = []
    return pl.pallas_call(
        functools.partial(attention_backward_kernel, block, len(pieces), per_row, paired),
        grid=(heads,),
        in_specs=[pl.BlockSpec(memory_space=pltpu.SMEM)]
        + [flat, flat, flat, resident(attn.shape), resident(attn.shape)]
        + [resident((8, length))]
        + [resident(cosine.shape)] * 2
        + [anywhere] * len(pieces),
        out_specs=[resident((length, 3 * width))] + dxn_specs,
        out_shape=[
            jax.ShapeDtypeStruct(shape, BF) for shape in [(length, 3 * width)] + dxn_shapes
        ],
        scratch_shapes=dxn_scratch
        + [pltpu.VMEM((model_width, 3 * width), BF)]
        + [pltpu.VMEM((length, width), F32)] * 3
        + [
            pltpu.VMEM((1, length), F32),
            pltpu.VMEM((length, width), BF),
            pltpu.SemaphoreType.DMA((len(pieces),)),
        ],
        cost_estimate=pl.CostEstimate(
            flops=5 * pairs * HD + 6 * length * model_width * width,
            bytes_accessed=20 * length * width + 2 * model_width * (length + 3 * width),
            transcendentals=pairs // 2,
        ),
        name="attention_backward",
    )(group.reshape(1), query, key, value, attn, grad, lse, cosine, sine, *pieces)


def strided_heads_kernel(which_ref, *refs):
    runs, outs = refs[:-2], refs[-2:]
    parity = which_ref[0] % 2
    half = len(runs) // 2

    for odd in range(2):

        @pl.when(parity == odd)
        def _():
            cols = slice(odd * HD, (odd + 1) * HD)
            for out, first in zip(outs, (0, half)):
                for r in range(0, half, 2):
                    out[:, r * HD : (r + 2) * HD] = jnp.concatenate(
                        [runs[first + r][:, cols], runs[first + r + 1][:, cols]], 1
                    )


def strided_heads(weight, group, group_count):
    rows, columns = weight.shape
    run = group_count * HD // 128
    runs = columns // (group_count * HD)

    def spec(r):
        return pl.BlockSpec((rows, 128), lambda g, w: (0, r * run + w[0] // 2))

    half = (rows, runs // 2 * HD)
    return pl.pallas_call(
        strided_heads_kernel,
        grid_spec=pltpu.PrefetchScalarGridSpec(
            num_scalar_prefetch=1,
            grid=(1,),
            in_specs=[spec(r) for r in range(runs)],
            out_specs=[pl.BlockSpec(half, lambda g, w: (0, 0))] * 2,
        ),
        out_shape=[jax.ShapeDtypeStruct(half, weight.dtype)] * 2,
        name="strided_heads",
    )(group.reshape(1), *[weight] * runs)


def lane_sums(values):
    return jnp.sum(values.T, axis=0, keepdims=True)


def last_rows_kernel(
    piece, which_ref, in_ref, up_ref, qkv_ref, gain1_ref, gain2_ref, part_ref, before_ref,
    out_ref, sum2_ref, strided_ref, sum1_ref,
):
    groups, rows, width = in_ref.shape

    def step(s, total):
        values = in_ref[s, :, :piece].astype(F32)
        cols = pl.ds(pl.multiple_of(s * piece, piece), piece)
        out_ref[:, cols] = values
        product = values * up_ref[:, cols].astype(F32)
        for c in range(piece // 128):
            total = total + product[:, c * 128 : (c + 1) * 128]
        return total

    total = lax.fori_loop(0, groups, step, jnp.zeros((rows, 128), F32))
    sum2_ref[...] = part_ref[...] + lane_sums(total) / gain2_ref[...]

    total = jnp.zeros((rows, 128), F32)
    for b in range((width - piece) // HD):
        cols = slice(piece + b * HD, piece + (b + 1) * HD)
        for pair in range(groups // 2):
            both = jnp.concatenate(
                [in_ref[2 * pair, :, cols], in_ref[2 * pair + 1, :, cols]], 1
            ).astype(F32)
            at = (b * groups + 2 * pair) * HD
            strided_ref[:, at : at + 128] = both
            total = total + both * qkv_ref[:, at : at + 128].astype(F32)
    sum1_ref[...] = lane_sums(total) / gain1_ref[...]


def last_rows(parts, piece, up_weight, qkv_weight, gain1, gain2, part, before, group):
    groups, rows, _ = parts.shape
    half = groups * piece

    def spec(columns, row=False, place=0):
        return pl.BlockSpec((rows, columns), lambda g, w: (w[0] if row else 0, place))

    line = pl.BlockSpec((1, rows), lambda g, w: (0, 0))
    return pl.pallas_call(
        functools.partial(last_rows_kernel, piece),
        grid_spec=pltpu.PrefetchScalarGridSpec(
            num_scalar_prefetch=1,
            grid=(1,),
            in_specs=[
                pl.BlockSpec(parts.shape, lambda g, w: (0, 0, 0)),
                spec(half, True, 1),
                spec(qkv_weight.shape[1], True),
                line, line, line,
                pl.BlockSpec(memory_space=pl.ANY),
            ],
            out_specs=[spec(half, False, 1), line, spec(qkv_weight.shape[1]), line],
        ),
        out_shape=[
            jax.ShapeDtypeStruct((rows, 2 * half), F32),
            jax.ShapeDtypeStruct((1, rows), F32),
            jax.ShapeDtypeStruct((rows, qkv_weight.shape[1]), F32),
            jax.ShapeDtypeStruct((1, rows), F32),
        ],
        input_output_aliases={7: 0},
        name="last_rows",
    )(group.reshape(1), parts, up_weight, qkv_weight, gain1, gain2, part, before)


def side_rows_kernel(runs, which_ref, *refs):
    parts, (weight_ref, gain_ref, out_ref, sum_ref) = refs[:runs], refs[runs:]
    groups, rows, piece = parts[0].shape

    @pl.when(pl.program_id(0) == 0)
    def _():
        sum_ref[...] = jnp.zeros_like(sum_ref)

    for run in range(runs):

        @pl.when(pl.program_id(0) == run)
        def _():
            def step(s, total):
                values = parts[run][s].astype(F32)
                cols = pl.ds(pl.multiple_of(s * piece, piece), piece)
                out_ref[:, cols] = values
                product = values * weight_ref[:, cols].astype(F32)
                for c in range(piece // 128):
                    total = total + product[:, c * 128 : (c + 1) * 128]
                return total

            total = lax.fori_loop(0, groups, step, jnp.zeros((rows, 128), F32))
            sum_ref[...] += lane_sums(total) / gain_ref[...]


def side_rows(parts, piece, weight, gain, group, columns=None):
    groups, rows, _ = parts[0][0].shape
    runs = len(parts)
    columns = columns or runs * groups * piece

    def spec(place):
        return pl.BlockSpec((groups, rows, piece), lambda c, w: (0, 0, place))

    return pl.pallas_call(
        functools.partial(side_rows_kernel, runs),
        grid_spec=pltpu.PrefetchScalarGridSpec(
            num_scalar_prefetch=1,
            grid=(runs,),
            in_specs=[spec(place) for _, place in parts]
            + [
                pl.BlockSpec((rows, groups * piece), lambda c, w: (w[0], c)),
                pl.BlockSpec((1, rows), lambda c, w: (0, 0)),
            ],
            out_specs=[
                pl.BlockSpec((rows, groups * piece), lambda c, w: (0, c)),
                pl.BlockSpec((1, rows), lambda c, w: (0, 0)),
            ],
        ),
        out_shape=[
            jax.ShapeDtypeStruct((rows, columns), F32),
            jax.ShapeDtypeStruct((1, rows), F32),
        ],
        name="side_rows",
    )(group.reshape(1), *[array for array, _ in parts], weight, gain)


BLOCKS = 4


def at_block(ref, rows, index):
    width = ref.shape[1] // BLOCKS
    return ref.at[rows, pl.ds(pl.multiple_of(index * width, width), width)]


def by_rows(kernel):
    def run(table_ref, x_ref, *refs):
        step = min(32, x_ref.shape[0])

        @pl.loop(0, x_ref.shape[0] // step)
        def _(i):
            kernel(pl.ds(pl.multiple_of(i * step, step), step), table_ref, x_ref, *refs)

    return run


ALL = slice(None)


def norm_in_kernel(rows, orders_ref, x_ref, gain_ref, grad_ref, xn_ref, dy_ref):
    x = x_ref[rows, :]
    inv = lax.rsqrt(jnp.mean(x * x, axis=1, keepdims=True) + EPS)
    for p in range(BLOCKS):
        block = orders_ref[p]
        normed = at_block(x_ref, rows, block)[...] * inv * at_block(gain_ref, ALL, block)[...]
        at_block(xn_ref, rows, p)[...] = normed.astype(BF)
        at_block(dy_ref, rows, p)[...] = at_block(grad_ref, rows, block)[...].astype(BF)


def norm_mid_kernel(rows, orders_ref, x_ref, own_ref, *refs):
    others, (gain_ref, mid_ref, xn_ref) = refs[:-3], refs[-3:]
    mid = x_ref[rows, :] + own_ref[rows, :]
    for other in others:
        mid = mid + other[rows, :].astype(F32)
    mid_ref[rows, :] = mid
    inv = lax.rsqrt(jnp.mean(mid * mid, axis=1, keepdims=True) + EPS)
    for p in range(BLOCKS):
        block = orders_ref[p]
        normed = at_block(mid_ref, rows, block)[...] * inv * at_block(gain_ref, ALL, block)[...]
        at_block(xn_ref, rows, p)[...] = normed.astype(BF)


def norm_grad_kernel(rows, places_ref, x_ref, base_ref, grad_ref, gain_ref, out_ref, *low_ref):
    x = x_ref[rows, :]
    inv = lax.rsqrt(jnp.mean(x * x, axis=1, keepdims=True) + EPS)
    grad = jnp.concatenate(
        [at_block(grad_ref, rows, places_ref[j])[...] for j in range(BLOCKS)], 1
    ).astype(F32)
    normed = x * inv
    grad_hat = grad * gain_ref[...]
    mean = jnp.mean(grad_hat * normed, axis=1, keepdims=True)
    out = base_ref[rows, :] + inv * (grad_hat - normed * mean)
    out_ref[rows, :] = out
    for ref in low_ref:
        ref[rows, :] = out.astype(BF)


def add_placed_kernel(rows, places_ref, base_ref, part_ref, out_ref):
    for j in range(BLOCKS):
        part = at_block(part_ref, rows, places_ref[j])[...].astype(F32)
        at_block(out_ref, rows, j)[...] = at_block(base_ref, rows, j)[...] + part


def on_rows(kernel, table, inputs, out_types):
    rows, width = inputs[0].shape
    block = rows

    def spec(shape):
        if shape[0] == 1:
            return pl.BlockSpec(shape, lambda i, t: (0, 0))
        return pl.BlockSpec((block, width), lambda i, t: (i, 0))

    return pl.pallas_call(
        by_rows(kernel),
        grid_spec=pltpu.PrefetchScalarGridSpec(
            num_scalar_prefetch=1,
            grid=(rows // block,),
            in_specs=[spec(v.shape) for v in inputs],
            out_specs=[spec((rows, width)) for _ in out_types],
        ),
        out_shape=[jax.ShapeDtypeStruct((rows, width), t) for t in out_types],
    )(table, *inputs)


def placed(pieces, column, columns, target_ref, at_column, sems, copies):
    row = 0
    for piece in pieces:
        rows = piece.shape[0]
        source = piece.at[:, pl.ds(column, columns)]
        place = target_ref.at[pl.ds(row, rows), pl.ds(at_column, columns)]
        copies.append(pltpu.make_async_copy(source, place, sems.at[len(copies)]))
        row += rows


def feed_kernel(count_a, count_b, xn_ref, dy_ref, *refs):
    part_a, part_b, refs = refs[:count_a], refs[count_a : count_a + count_b], refs[count_a + count_b :]
    act_ref, grad_ref, dxn_ref, gate_up_ref, down_ref, sems = refs
    cut = part_a[0].shape[1]
    hidden = act_ref.shape[1]
    split = 2 * hidden - cut

    copies = []
    placed(part_a, 0, cut, gate_up_ref, 0, sems, copies)
    placed(part_b, 0, split, gate_up_ref, cut, sems, copies)
    placed(part_b, split, hidden, down_ref, 0, sems, copies)

    @pl.when(pl.program_id(0) == 0)
    def _():
        for copy in copies:
            copy.start()
        for copy in copies[: count_a + count_b]:
            copy.wait()

    gate_up = jnp.dot(xn_ref[...], gate_up_ref[...], preferred_element_type=F32)
    gate, up_part = gate_up[:, :hidden], gate_up[:, hidden:]
    sigmoid_gate = jax.nn.sigmoid(gate)
    gated = gate * sigmoid_gate
    act_ref[...] = (gated * up_part).astype(BF)

    @pl.when(pl.program_id(0) == 0)
    def _():
        for copy in copies[count_a + count_b :]:
            copy.wait()

    grad_act = jnp.dot(dy_ref[...], down_ref[...], preferred_element_type=F32)
    grad_gate = grad_act * up_part * sigmoid_gate * (1.0 + gate * (1.0 - sigmoid_gate))
    grad_ref[:, :hidden] = grad_gate.astype(BF)
    grad_ref[:, hidden:] = (grad_act * gated).astype(BF)
    columns_last(grad_ref, gate_up_ref, dxn_ref)


def columns_last(left_ref, right_ref, out_ref):
    chunk = min(1024, out_ref.shape[1])

    @pl.loop(0, out_ref.shape[1] // chunk)
    def _(c):
        at = pl.ds(pl.multiple_of(c * chunk, chunk), chunk)
        out_ref[:, at] = contract_last(left_ref[...], right_ref[at, :]).astype(BF)


OVER_X_FIRST = ((1, 3), (3, 4), (0, 1))
OVER_Y_FIRST = ((2, 4), (1, 2), (0, 1))
ONE_EACH = ((0, 1), (1, 2), (2, 3), (3, 4))


def outer_kernel(layouts, left_ref, right_ref, *out_refs):
    step = pl.program_id(0)
    steps = pl.num_programs(0) // 4
    product = contract_first(left_ref[...], right_ref[...]).astype(BF)
    column = 0
    refs = iter(out_refs)
    for layout in layouts:
        targets = [next(refs) for _ in layout]
        width = targets[0].shape[1]
        block = product[:, column : column + width]
        column += width
        for target, (first, end) in zip(targets, layout):

            @pl.when((step >= first * steps) & (step < end * steps))
            def _():
                target[...] = block


def outer_blocks(left, right, layouts, steps=2, side=None):
    tokens, rows = left.shape
    columns = right.shape[1] if side is None else right.shape[1] // 2
    width = columns // len(layouts)
    block = rows // (4 * steps)
    held = [blocks for layout in layouts for blocks in layout]

    def spec(first, end):
        return pl.BlockSpec(
            (block, width),
            lambda p: (jnp.clip(p - first * steps, 0, (end - first) * steps - 1), 0),
        )

    outs = pl.pallas_call(
        functools.partial(outer_kernel, layouts),
        grid=(4 * steps,),
        in_specs=[
            pl.BlockSpec((tokens, block), lambda p: (0, p)),
            pl.BlockSpec((tokens, columns), lambda p: (0, side or 0)),
        ],
        out_specs=[spec(*blocks) for blocks in held],
        out_shape=[
            jax.ShapeDtypeStruct(((end - first) * rows // 4, width), BF) for first, end in held
        ],
        cost_estimate=pl.CostEstimate(
            flops=2 * tokens * rows * columns,
            bytes_accessed=2 * (tokens * (rows + columns) + rows * columns),
            transcendentals=0,
        ),
        name="outer_blocks",
    )(left, right)
    outs = iter(outs)
    return [[next(outs) for _ in layout] for layout in layouts]


def in_order(parts):
    return [piece for k in GRAY for piece in parts[k]]


def feed_forward(xn, dy, part_a, part_b, hidden):
    tokens, model_width = xn.shape
    block = min(256, tokens)
    part_a, part_b = in_order(part_a), in_order(part_b)

    def blocks(columns):
        return pl.BlockSpec((block, columns), lambda i: (i, 0))

    return pl.pallas_call(
        functools.partial(feed_kernel, len(part_a), len(part_b)),
        grid=(tokens // block,),
        in_specs=[blocks(model_width)] * 2
        + [pl.BlockSpec(memory_space=pl.ANY)] * (len(part_a) + len(part_b)),
        out_specs=[blocks(hidden), blocks(2 * hidden), blocks(model_width)],
        out_shape=[
            jax.ShapeDtypeStruct((tokens, columns), BF)
            for columns in (hidden, 2 * hidden, model_width)
        ],
        scratch_shapes=[
            pltpu.VMEM((model_width, 2 * hidden), BF),
            pltpu.VMEM((model_width, hidden), BF),
            pltpu.SemaphoreType.DMA((len(part_a) + 2 * len(part_b),)),
        ],
        cost_estimate=pl.CostEstimate(
            flops=10 * tokens * model_width * hidden,
            bytes_accessed=2 * (4 * tokens * model_width + 3 * model_width * hidden),
            transcendentals=tokens * hidden,
        ),
        name="feed_forward",
    )(xn, dy, *part_a, *part_b)


def feed_out_kernel(count, group_ref, act_ref, *refs):
    pieces, (mine_ref, theirs_ref, out_ref, down_ref, sems) = refs[:count], refs[count:]
    hidden = act_ref.shape[1]
    tokens = mine_ref.shape[0]

    @pl.when(pl.program_id(0) == 0)
    def _():
        copies = []
        placed(pieces, pieces[0].shape[1] - hidden, hidden, down_ref, 0, sems, copies)
        for copy in copies:
            copy.start()
        for copy in copies:
            copy.wait()

    columns_last(act_ref, down_ref, out_ref)
    odd = group_ref[0] % 2
    mine_ref[...] = out_ref[pl.ds(pl.multiple_of(odd * tokens, tokens), tokens), :]
    theirs_ref[...] = out_ref[pl.ds(pl.multiple_of((1 - odd) * tokens, tokens), tokens), :]


def feed_out(act, part_b, model_width, group, run):
    tokens, hidden = act.shape
    block = 2 * run
    pieces = in_order(part_b)
    half = jax.ShapeDtypeStruct((tokens // 2, model_width), BF)
    return pl.pallas_call(
        functools.partial(feed_out_kernel, len(pieces)),
        grid=(tokens // block,),
        in_specs=[pl.BlockSpec(memory_space=pltpu.SMEM)]
        + [pl.BlockSpec((block, hidden), lambda i: (i, 0))]
        + [pl.BlockSpec(memory_space=pl.ANY)] * len(pieces),
        out_specs=[pl.BlockSpec((run, model_width), lambda i: (i, 0))] * 2,
        out_shape=[half, half],
        scratch_shapes=[
            pltpu.VMEM((block, model_width), BF),
            pltpu.VMEM((model_width, hidden), BF),
            pltpu.SemaphoreType.DMA((len(pieces),)),
        ],
        cost_estimate=pl.CostEstimate(
            flops=2 * tokens * model_width * hidden,
            bytes_accessed=2 * (tokens + model_width) * hidden + 2 * tokens * model_width,
            transcendentals=0,
        ),
        name="feed_out",
    )(group.reshape(1), act, *pieces)


def project_kernel(members_ref, features_ref, weight_ref, own_ref, *other_refs):
    product = contract_first(features_ref[0], weight_ref[...])

    @pl.when(pl.program_id(0) == 0)
    def _():
        own_ref[...] = product

    for k, other in enumerate(other_refs):

        @pl.when(pl.program_id(0) == k + 1)
        def _():
            other[...] = product.astype(BF)


def project(features, weight, members):
    _, count, tokens = features.shape
    width = weight.shape[1]
    place = pl.BlockSpec((tokens, width), lambda k, m: (0, 0))
    return pl.pallas_call(
        project_kernel,
        grid_spec=pltpu.PrefetchScalarGridSpec(
            num_scalar_prefetch=1,
            grid=(4,),
            in_specs=[
                pl.BlockSpec((1, count, tokens), lambda k, m: (m[k], 0, 0)),
                pl.BlockSpec(weight.shape, lambda k, m: (0, 0)),
            ],
            out_specs=[place] * 4,
        ),
        out_shape=[jax.ShapeDtypeStruct((tokens, width), F32)]
        + [jax.ShapeDtypeStruct((tokens, width), BF)] * 3,
        name="project",
    )(members, features, weight)


def rows_by_member(pieces, places_ref, target_ref, sems):
    height = pieces[0].shape[0]
    copies = [
        pltpu.make_async_copy(
            piece,
            target_ref.at[pl.ds(pl.multiple_of(places_ref[k] * height, height), height)],
            sems.at[k],
        )
        for k, piece in enumerate(pieces)
    ]
    for copy in copies:
        copy.start()
    for copy in copies:
        copy.wait()


def out_rows_kernel(members_ref, features_ref, *refs):
    pieces, (out_ref, rows_ref, sems) = refs[:4], refs[4:]
    rows_by_member(pieces, members_ref, rows_ref, sems)
    left = jnp.concatenate([features_ref[d] for d in range(4)], 1)
    chunk = 512

    @pl.loop(0, out_ref.shape[1] // chunk)
    def _(c):
        at = pl.ds(pl.multiple_of(c * chunk, chunk), chunk)
        out_ref[:, at] = jnp.dot(left, rows_ref[:, at], preferred_element_type=F32).astype(BF)


def out_rows_grad(features, pieces, members):
    tokens, width = pieces[0].shape
    count = features.shape[1]
    return pl.pallas_call(
        out_rows_kernel,
        grid_spec=pltpu.PrefetchScalarGridSpec(
            num_scalar_prefetch=1,
            grid=(1,),
            in_specs=[pl.BlockSpec(features.shape, lambda i, m: (0, 0, 0))]
            + [pl.BlockSpec(memory_space=pl.ANY)] * 4,
            out_specs=pl.BlockSpec((count, width), lambda i, m: (0, 0)),
            scratch_shapes=[pltpu.VMEM((4 * tokens, width), BF), pltpu.SemaphoreType.DMA((4,))],
        ),
        out_shape=jax.ShapeDtypeStruct((count, width), BF),
        name="out_rows",
    )(members, features, *pieces)


def partner(array, bits):
    return lax.ppermute(array, "dp", [(i, i ^ bits) for i in range(4)])


class Quad:
    def __init__(self, index):
        self.index = index

    def gather_direct(self, block):
        return [block] + [partner(block, k) for k in (1, 2, 3)]

    def gather(self, first, second):
        a = {0: [first], 1: [partner(first, 1)]}
        b = {0: [second], 2: [partner(second, 2)]}
        a[2], b[1] = [partner(first, 2)], [partner(second, 1)]
        a[3], b[3] = [partner(a[1][0], 2)], [partner(b[2][0], 1)]
        return a, b

    def gather_late(self, first, second, first_high, second_high):
        rows = first_high.shape[0]
        a = {0: [first], 1: [partner(first, 1)]}
        b = {0: [second], 2: [partner(second, 2)]}
        a[2], b[1] = [partner(first_high, 2)], [partner(second_high, 1)]

        def late(*earlier):
            first_low, second_low, near_a, near_b = (
                after(v, *earlier) for v in (first[rows:], second[rows:], a[1][0], b[2][0])
            )
            a[2].append(partner(first_low, 2))
            b[1].append(partner(second_low, 1))
            a[3], b[3] = [partner(near_a, 2)], [partner(near_b, 1)]
            return a, b

        return late


def add(*terms):
    total = terms[0].astype(F32)
    for term in terms[1:]:
        total = total + term.astype(F32)
    return total.astype(BF)


class PairSum:
    def __init__(self, first, second):
        (send_a, *self.keep_a), (send_b, *self.keep_b) = first, second
        self.sent_a = partner(send_a, 1)
        self.sent_b = partner(send_b, 2)

    def second(self):
        rows = self.keep_a[0].shape[0]
        send_a = add(self.keep_a[0], self.sent_a[rows:])
        send_b = add(self.keep_b[0], self.sent_b[:rows])
        self.far_a = partner(send_a, 2)
        self.far_b = partner(send_b, 1)

    def total(self):
        rows = self.keep_a[0].shape[0]
        return jnp.concatenate(
            [
                add(self.keep_a[1], self.sent_a[:rows], self.far_a),
                add(self.keep_b[1], self.sent_b[rows:], self.far_b),
            ],
            1,
        )


def sum_direct(blocks):
    others = [partner(blocks[p], GRAY[p]) for p in (1, 2, 3)]
    return add(blocks[0], *others)


def reduce_plain(left, right):
    return lax.psum_scatter(
        contract_first(left, right).astype(BF), "dp", scatter_dimension=0, tiled=True
    )


def over_seq(values):
    return lax.all_gather(values, "seq", axis=0, tiled=True)


def sum_over_seq(values):
    return lax.psum_scatter(values.astype(BF), "seq", scatter_dimension=0, tiled=True)


def sum_over_pairs(mine, theirs, group_count, *earlier):
    received = lax.ppermute(theirs, "seq", [(i, i ^ 1) for i in range(group_count)])
    total = after(add(mine, received), *earlier)
    return lax.psum_scatter(
        total, "seq", scatter_dimension=0, tiled=True,
        axis_index_groups=[list(range(odd, group_count, 2)) for odd in range(2)],
    )


def exchange(values, axes):
    return lax.all_to_all(values, axes, split_axis=0, concat_axis=0, tiled=True)


def exchange_rows(values, group_count):
    return exchange(
        values.reshape(group_count, values.shape[0] // group_count, values.shape[1]), "seq"
    )


def feed_forward_plain(xn, dy, gate_up_full, down_full, hidden):
    gate_up = jnp.dot(xn, gate_up_full, preferred_element_type=F32)
    gate, up_part = gate_up[:, :hidden], gate_up[:, hidden:]
    sigmoid_gate = jax.nn.sigmoid(gate)
    act = (gate * sigmoid_gate * up_part).astype(BF)
    grad_act = jnp.dot(dy, down_full, preferred_element_type=F32)
    grad_gate = grad_act * up_part * sigmoid_gate * (1.0 + gate * (1.0 - sigmoid_gate))
    grad_up = grad_act * gate * sigmoid_gate
    grad_gate_up = jnp.concatenate([grad_gate, grad_up], 1).astype(BF)
    return act, grad_gate_up, contract_last(grad_gate_up, gate_up_full).astype(BF)


def shards(
    layer_in, norm1_gain, qkv_weight, out_weight, norm2_gain, gate_up_weight, down_weight, cotangent
):
    token_rows, model_width = layer_in.shape
    group_count = lax.axis_size("seq")
    dp_count = lax.axis_size("dp")
    group = lax.axis_index("seq")
    member = lax.axis_index("dp")
    length = token_rows * group_count
    dp_rows = model_width // dp_count
    shard_rows = dp_rows // group_count
    hidden_units = down_weight.shape[1]
    hidden = hidden_units // group_count
    width = model_width // group_count
    quad = Quad(member) if dp_count == 4 else None
    strided = quad is not None and shard_rows == HD

    blocks_at = jnp.arange(4, dtype=jnp.int32)
    if quad:
        orders = (blocks_at ^ (blocks_at >> 1)) ^ member
        places = blocks_at ^ member
        places = places ^ (places >> 1)
    else:
        orders, places = blocks_at, blocks_at
    gain1, gain2 = norm1_gain[None, :], norm2_gain[None, :]

    xn1_own, dy_own = on_rows(norm_in_kernel, orders, (layer_in, gain1, cotangent), (BF, BF))
    xn1 = over_seq(xn1_own)

    if strided:
        left, right = strided_heads(qkv_weight, group, group_count)
    else:
        qkv_piece = jnp.concatenate(
            [
                lax.dynamic_slice_in_dim(qkv_weight, part * model_width + group * width, width, 1)
                for part in range(3)
            ],
            1,
        )
    gate_piece = lax.dynamic_slice_in_dim(gate_up_weight, group * hidden, hidden, 1)
    up_piece = lax.dynamic_slice_in_dim(gate_up_weight, hidden_units + group * hidden, hidden, 1)
    down_piece = lax.dynamic_slice_in_dim(down_weight, group * hidden, hidden, 1)
    if quad:
        if not strided:
            cut = qkv_piece.shape[1] // 2
            left, right = qkv_piece[:, :cut], qkv_piece[:, cut:]
        left, right = quad.gather(left, right)
        blocks = (left[3][0], right[3][0])
        qkv_pieces = [part[k][0] for k in GRAY for part in (left, right)]
        per_row = 2
        half = hidden // 2
        part_a = after(jnp.concatenate([gate_piece, up_piece[:, :half]], 1), *blocks)
        part_b = after(jnp.concatenate([up_piece[:, half:], down_piece], 1), *blocks)
        high = dp_rows // 2
        high_a, high_b = part_a[:high], part_b[:high]
        xn1, high_a, high_b = lax.optimization_barrier((xn1, high_a, high_b))
        rest_of_weights = quad.gather_late(part_a, part_b, high_a, high_b)
    else:
        qkv_pieces, per_row = [lax.all_gather(qkv_piece, "dp", axis=0, tiled=True)], 1
        gate_up_full = lax.all_gather(
            jnp.concatenate([gate_piece, up_piece], 1), "dp", axis=0, tiled=True
        )
        down_full = lax.all_gather(down_piece, "dp", axis=0, tiled=True)

    cosine, sine = rotary_tables(length)
    attn, query, key, value, lse = attention_forward(
        xn1, qkv_pieces, per_row, cosine, sine, token_rows
    )

    dy = over_seq(after(dy_own, attn))

    def to_features(by_head):
        if strided:
            moved = exchange(by_head.reshape(-1, HD, token_rows), ("dp", "seq"))
        else:
            by_tokens = by_head.transpose(1, 0, 2, 3).reshape(group_count, width, token_rows)
            moved = exchange(exchange(by_tokens, "seq").reshape(dp_count, dp_rows, token_rows), "dp")
        return moved.reshape(dp_count, dp_rows, token_rows)

    def to_heads(features):
        if strided:
            moved = exchange(features.reshape(-1, HD, token_rows), ("dp", "seq"))
            return moved.reshape(-1, group_count, HD, token_rows)
        moved = exchange(features, "dp").reshape(group_count, width, token_rows)
        moved = exchange(moved, "seq").reshape(group_count, width // HD, HD, token_rows)
        return moved.transpose(1, 0, 2, 3)

    features = to_features(attn)
    if quad:
        parts = project(features, out_weight, blocks_at ^ member)
        others = [partner(parts[k], k) for k in (1, 2, 3)]
        partials = (parts[0], *others)
    else:
        partials = (
            lax.psum_scatter(
                jnp.einsum("dft,fn->dtn", features, out_weight, preferred_element_type=F32)
                .astype(BF)
                .reshape(dp_count * token_rows, model_width),
                "dp", scatter_dimension=0, tiled=True,
            ).astype(F32),
        )

    hidden_res, xn2_own = on_rows(norm_mid_kernel, orders, (layer_in, *partials, gain2), (F32, BF))
    xn2 = over_seq(xn2_own)
    if quad:
        part_a, part_b = rest_of_weights(*partials)
        act, grad_gate_up, partial_xn2 = feed_forward(xn2, dy, part_a, part_b, hidden)
        feed_halves = feed_out(after(act, partial_xn2), part_b, model_width, group, token_rows)
    else:
        act, grad_gate_up, partial_xn2 = feed_forward_plain(
            xn2, dy, gate_up_full, down_full, hidden
        )
        feed_sum = contract_last(act, down_full).astype(BF)
    raw_xn2 = sum_over_seq(partial_xn2)
    grad_hidden, hidden_low = on_rows(
        norm_grad_kernel, places, (hidden_res, cotangent, raw_xn2, gain2), (F32, BF)
    )
    if quad:
        feed_sum = sum_over_pairs(*feed_halves, group_count, raw_xn2)
    else:
        feed_sum = sum_over_seq(after(feed_sum, raw_xn2))
    if quad:
        sides = (OVER_X_FIRST, OVER_Y_FIRST)
        down_sum = PairSum(*outer_blocks(dy, act, sides, 1))
        gate_sum = PairSum(*outer_blocks(xn2, grad_gate_up, sides, 1, 0))
        up_sum = PairSum(*outer_blocks(xn2, grad_gate_up, sides, 1, 1))
        rows_low = quad.gather_direct(hidden_low)
    else:
        down_rows = reduce_plain(dy, act)
        gate_rows = reduce_plain(xn2, grad_gate_up[:, :hidden])
        up_rows = reduce_plain(xn2, grad_gate_up[:, hidden:])
        rows_low = list(lax.all_gather(hidden_low, "dp", axis=0))

    grad_features = jnp.einsum(
        "fn,ktn->kft", out_weight, jnp.stack(rows_low), preferred_element_type=F32
    ).astype(BF)
    if quad:
        grad_features = jnp.stack(
            [lax.dynamic_index_in_dim(grad_features, member ^ j, 0, False) for j in range(4)]
        )
    grad_attn = to_heads(grad_features)
    if quad:
        down_sum.second()
        gate_sum.second()
        up_sum.second()
    if quad:
        out_rows = out_rows_grad(features, rows_low, blocks_at ^ member)
    else:
        out_rows = jnp.einsum(
            "kft,ktn->fn", features, jnp.stack(rows_low), preferred_element_type=F32
        ).astype(BF)
    out_grad = sum_over_seq(out_rows).astype(F32)
    grad_qkv, *partial_xn1 = attention_backward(
        group, quad is not None,
        query, key, value, attn, grad_attn, lse, cosine, sine, qkv_pieces, per_row,
    )
    if quad:
        raw_xn1 = sum_over_pairs(*partial_xn1, group_count)
    else:
        raw_xn1 = sum_over_seq(partial_xn1[0])
    (input_grad,) = on_rows(
        norm_grad_kernel, places, (layer_in, grad_hidden, raw_xn1, gain1), (F32,)
    )
    (layer_out,) = on_rows(
        add_placed_kernel, places, (hidden_res, after(feed_sum, grad_qkv)), (F32,)
    )

    if quad:
        (blocks,) = outer_blocks(xn1, grad_qkv, (ONE_EACH,))
        qkv_rows = sum_direct(blocks)
        down_rows, gate_rows, up_rows = down_sum.total(), gate_sum.total(), up_sum.total()
    else:
        qkv_rows = reduce_plain(xn1, grad_qkv)
    near_parts = exchange_rows(jnp.concatenate([down_rows, gate_rows], 1), group_count)
    far_parts = exchange_rows(jnp.concatenate([up_rows, qkv_rows], 1), group_count)
    own_at = member * dp_rows + group * shard_rows
    own1 = lax.dynamic_slice_in_dim(gain1, own_at, shard_rows, 1)
    own2 = lax.dynamic_slice_in_dim(gain2, own_at, shard_rows, 1)
    down_grad, _ = side_rows([(near_parts, 0)], hidden, down_weight, own2, group)
    if strided:
        before, part = side_rows(
            [(near_parts, 1)], hidden, gate_up_weight, own2, group, 2 * hidden_units
        )
        gate_up_grad, norm2_grad, qkv_grad, norm1_grad = last_rows(
            far_parts, hidden, gate_up_weight, qkv_weight, own1, own2, part, before, group
        )
    else:
        gate_up_grad, norm2_grad = side_rows(
            [(near_parts, 1), (far_parts, 0)], hidden, gate_up_weight, own2, group
        )
        qkv_parts = far_parts[:, :, hidden:]
        qkv_grad, norm1_grad = side_rows(
            [(qkv_parts, i) for i in range(3)], width, qkv_weight, own1, group
        )

    return (
        layer_out,
        input_grad,
        norm1_grad.reshape(shard_rows),
        qkv_grad,
        out_grad,
        norm2_grad.reshape(shard_rows),
        gate_up_grad,
        down_grad,
    )


def solution(mesh):
    rows = P(("dp", "seq"), None)
    in_specs = (
        rows, P(), P("dp", None), P("dp", None), P(), P("dp", None), P("dp", None), rows,
    )
    vector = P(("dp", "seq"))
    out_specs = (rows, rows, vector, rows, rows, vector, rows, rows)
    return jax.shard_map(shards, mesh=mesh, in_specs=in_specs, out_specs=out_specs, check_vma=False)
```

```python
import functools

import jax
import jax.numpy as jnp
from jax import lax
from jax.experimental import pallas as pl
from jax.experimental.pallas import tpu as pltpu
from jax.sharding import PartitionSpec as P


HD = 64
EPS = 1e-05
THETA = 130000.0
BF = jnp.bfloat16
F32 = jnp.float32

GRAY = (0, 1, 3, 2)


def after(values, *earlier):
    return lax.optimization_barrier((values, *earlier))[0]


def rotary_kernel(inverse_ref, cos_ref, sin_ref):
    step = min(32, cos_ref.shape[0])

    @pl.loop(0, cos_ref.shape[0] // step)
    def _(i):
        at = pl.ds(pl.multiple_of(i * step, step), step)
        position = i * step + lax.broadcasted_iota(jnp.int32, (step, 128), 0)
        angles = position.astype(F32) * inverse_ref[...]
        lane = lax.broadcasted_iota(jnp.int32, (step, 128), 1)
        sine = jnp.sin(angles)
        cos_ref[at, :] = jnp.cos(angles)
        sin_ref[at, :] = jnp.where((lane & (HD // 2)) != 0, sine, -sine)


def rotary_tables(length):
    half = HD // 2
    inverse = THETA ** (-(jnp.arange(half).astype(F32) * 2.0) / HD)
    table = jax.ShapeDtypeStruct((length, 128), F32)
    return pl.pallas_call(rotary_kernel, out_shape=[table, table], name="rotary")(
        jnp.tile(inverse, 4)[None, :]
    )


def contract_last(left, right):
    return lax.dot_general(left, right, (((1,), (1,)), ((), ())), preferred_element_type=F32)


def contract_first(left, right):
    return lax.dot_general(left, right, (((0,), (0,)), ((), ())), preferred_element_type=F32)


def half_turn(values):
    lane = lax.broadcasted_iota(jnp.int32, values.shape, 1)
    upper = (lane & (HD // 2)) != 0
    return jnp.where(
        upper, pltpu.roll(values, HD // 2, 1), pltpu.roll(values, 128 - HD // 2, 1)
    )


def head_only(values, head):
    lane = lax.broadcasted_iota(jnp.int32, values.shape, 1)
    return jnp.where(lane // HD == head, values, jnp.zeros_like(values))


def causal(block):
    key_pos = lax.broadcasted_iota(jnp.int32, (block, block), 0)
    query_pos = lax.broadcasted_iota(jnp.int32, (block, block), 1)
    return key_pos <= query_pos


def assembled(pieces, per_row, target_ref, sems):
    copies, row = [], 0
    for first in range(0, len(pieces), per_row):
        column = 0
        for piece in pieces[first : first + per_row]:
            rows, columns = piece.shape
            place = target_ref.at[pl.ds(row, rows), pl.ds(column, columns)]
            copies.append(pltpu.make_async_copy(piece, place, sems.at[len(copies)]))
            column += columns
        row += rows
    return copies


def attention_forward_kernel(block, count, per_row, xn_ref, *refs):
    pieces, refs = refs[:count], refs[count:]
    cos_ref, sin_ref, attn_ref, q_ref, k_ref, v_ref, lse_ref, weight_ref, vt_ref, sems = refs
    head = pl.program_id(0)
    length, width = q_ref.shape
    tokens = attn_ref.shape[3]
    scale = HD ** (-0.5)

    @pl.when(head == 0)
    def _():
        copies = assembled(pieces, per_row, weight_ref, sems)
        for copy in copies:
            copy.start()
        for copy in copies:
            copy.wait()

        @pl.loop(0, length // block)
        def _(i):
            at = pl.ds(pl.multiple_of(i * block, block), block)
            qkv = jnp.dot(xn_ref[at, :], weight_ref[...], preferred_element_type=F32).astype(BF)
            v_ref[at, :] = qkv[:, 2 * width :]
            for c in range(width // 128):
                for source, target, factor in ((0, q_ref, scale), (width, k_ref, 1.0)):
                    u = qkv[:, source + c * 128 : source + (c + 1) * 128].astype(F32)
                    turned = u * cos_ref[at, :] + half_turn(u) * sin_ref[at, :]
                    target[at, c * 128 : (c + 1) * 128] = turned.astype(BF) * factor

        for c in range(width // 128):
            cols = slice(c * 128, (c + 1) * 128)
            vt_ref[cols, :] = v_ref[:, cols].astype(F32).T.astype(BF)

    rows = pl.ds(pl.multiple_of(head * HD, HD), HD)
    for i in range(length // block):
        low, high = i * block, (i + 1) * block
        query = head_only(q_ref[low:high, :], head)
        near = contract_last(k_ref[low:high, :], query)
        near = jnp.where(causal(block), near, -1e30)
        top = jnp.max(near, axis=0, keepdims=True)
        if i:
            far = contract_last(k_ref[0:low, :], query)
            top = jnp.maximum(top, jnp.max(far, axis=0, keepdims=True))
        near = jnp.exp(near - top)
        total = jnp.sum(near, axis=0, keepdims=True)
        mixed = jnp.dot(vt_ref[rows, low:high], near.astype(BF), preferred_element_type=F32)
        if i:
            far = jnp.exp(far - top)
            total = total + jnp.sum(far, axis=0, keepdims=True)
            mixed = mixed + jnp.dot(
                vt_ref[rows, 0:low], far.astype(BF), preferred_element_type=F32
            )
        mixed = (mixed / total).astype(BF)
        for part in range(block // tokens):
            attn_ref[head, low // tokens + part] = mixed[:, part * tokens : (part + 1) * tokens]
        lse_ref[pl.ds(head, 1), low:high] = top + jnp.log(total)


def attention_backward_kernel(
    block, count, per_row, paired, group_ref,
    q_ref, k_ref, v_ref, attn_ref, grad_ref, lse_ref, cos_ref, sin_ref, *refs
):
    pieces, refs = refs[:count], refs[count:]
    if paired:
        out_ref, mine_ref, theirs_ref, dxn_ref, half_sems, *refs = refs
    else:
        out_ref, dxn_ref, *refs = refs
    weight_ref, dq_ref, dk_ref, dv_ref, delta_ref, flat_ref, sems = refs
    head = pl.program_id(0)
    length, width = q_ref.shape
    tokens = attn_ref.shape[3]
    scale = HD ** (-0.5)

    @pl.when(head == 0)
    def _():
        for copy in assembled(pieces, per_row, weight_ref, sems):
            copy.start()
        dq_ref[...] = jnp.zeros_like(dq_ref)
        dk_ref[...] = jnp.zeros_like(dk_ref)
        dv_ref[...] = jnp.zeros_like(dv_ref)
        for c in range(width // 128):
            for j in range(length // tokens):
                pair = jnp.concatenate([grad_ref[2 * c, j], grad_ref[2 * c + 1, j]], 0)
                flat_ref[j * tokens : (j + 1) * tokens, c * 128 : (c + 1) * 128] = (
                    pair.astype(F32).T.astype(BF)
                )

    for j in range(length // tokens):
        product = grad_ref[head, j].astype(F32) * attn_ref[head, j].astype(F32)
        delta_ref[:, j * tokens : (j + 1) * tokens] = jnp.sum(product, axis=0, keepdims=True)

    def piece(keys, low, high, query, grad, diagonal):
        prob = jnp.exp(contract_last(k_ref[keys, :], query) - lse_ref[pl.ds(head, 1), low:high])
        if diagonal:
            prob = jnp.where(causal(block), prob, 0.0)
        dprob = contract_last(v_ref[keys, :], grad)
        dscore = (prob * (dprob - delta_ref[:, low:high])).astype(BF)
        dv_ref[keys, :] += jnp.dot(prob.astype(BF), grad, preferred_element_type=F32)
        dk_ref[keys, :] += jnp.dot(dscore, query, preferred_element_type=F32)
        dq_ref[low:high, :] += contract_first(dscore, head_only(k_ref[keys, :], head))

    for i in range(length // block):
        low, high = i * block, (i + 1) * block
        query = head_only(q_ref[low:high, :], head)
        grad = head_only(flat_ref[low:high, :], head)
        piece(slice(low, high), low, high, query, grad, True)
        if i:
            piece(slice(0, low), low, high, query, grad, False)

    @pl.when(head == pl.num_programs(0) - 1)
    def _():
        for copy in assembled(pieces, per_row, weight_ref, sems):
            copy.wait()

        @pl.loop(0, length // block)
        def _(i):
            at = pl.ds(pl.multiple_of(i * block, block), block)
            for c in range(width // 128):
                cols = slice(c * 128, (c + 1) * 128)
                for source, target, factor in ((dq_ref, 0, scale), (dk_ref, width, 1.0)):
                    u = source[at, cols] * factor
                    turned = u * cos_ref[at, :] - half_turn(u) * sin_ref[at, :]
                    out_ref[at, target + c * 128 : target + (c + 1) * 128] = turned.astype(BF)
            out_ref[at, 2 * width : 3 * width] = dv_ref[at, :].astype(BF)
            dxn_ref[at, :] = contract_last(out_ref[at, :], weight_ref[...]).astype(BF)

        if paired:
            copies = []
            for i in range(length // (2 * tokens)):
                to = pl.ds(i * tokens, tokens)
                for target, odd in ((theirs_ref, 1), (mine_ref, 0)):
                    row = 2 * i * tokens + (group_ref[0] % 2 ^ odd) * tokens
                    source = dxn_ref.at[pl.ds(pl.multiple_of(row, tokens), tokens)]
                    copies.append(
                        pltpu.make_async_copy(source, target.at[to], half_sems.at[len(copies)])
                    )
            for copy in copies:
                copy.start()
            for copy in copies:
                copy.wait()


def resident(shape):
    return pl.BlockSpec(shape, lambda h: tuple(0 for _ in shape))


def attention_forward(xn, pieces, per_row, cosine, sine, tokens):
    length, model_width = xn.shape
    width = sum(piece.shape[1] for piece in pieces[:per_row]) // 3
    heads = width // HD
    block = min(256, length)
    pairs = heads * length * length
    out = (heads, length // tokens, HD, tokens)
    return pl.pallas_call(
        functools.partial(attention_forward_kernel, block, len(pieces), per_row),
        grid=(heads,),
        in_specs=[resident(xn.shape)]
        + [pl.BlockSpec(memory_space=pl.ANY)] * len(pieces)
        + [resident(cosine.shape)] * 2,
        out_specs=[resident(out)] + [resident((length, width))] * 3 + [resident((8, length))],
        out_shape=[jax.ShapeDtypeStruct(out, BF)]
        + [jax.ShapeDtypeStruct((length, width), BF)] * 3
        + [jax.ShapeDtypeStruct((8, length), F32)],
        scratch_shapes=[
            pltpu.VMEM((model_width, 3 * width), BF),
            pltpu.VMEM((width, length), BF),
            pltpu.SemaphoreType.DMA((len(pieces),)),
        ],
        cost_estimate=pl.CostEstimate(
            flops=2 * pairs * HD + 6 * length * model_width * width,
            bytes_accessed=8 * length * width + 2 * model_width * (length + 3 * width),
            transcendentals=pairs // 2,
        ),
        name="attention_forward",
    )(xn, *pieces, cosine, sine)


def attention_backward(
    group, paired, query, key, value, attn, grad, lse, cosine, sine, pieces, per_row
):
    length, width = query.shape
    tokens = attn.shape[3]
    model_width = sum(piece.shape[0] for piece in pieces[::per_row])
    heads = width // HD
    block = min(256, length)
    pairs = heads * length * length
    flat = resident((length, width))
    anywhere = pl.BlockSpec(memory_space=pl.ANY)
    if paired:
        dxn_specs, dxn_shapes = [anywhere] * 2, [(length // 2, model_width)] * 2
        dxn_scratch = [
            pltpu.VMEM((length, model_width), BF), pltpu.SemaphoreType.DMA((length // tokens,))
        ]
    else:
        dxn_specs, dxn_shapes = [resident((length, model_width))], [(length, model_width)]
        dxn_scratch = []
    return pl.pallas_call(
        functools.partial(attention_backward_kernel, block, len(pieces), per_row, paired),
        grid=(heads,),
        in_specs=[pl.BlockSpec(memory_space=pltpu.SMEM)]
        + [flat, flat, flat, resident(attn.shape), resident(attn.shape)]
        + [resident((8, length))]
        + [resident(cosine.shape)] * 2
        + [anywhere] * len(pieces),
        out_specs=[resident((length, 3 * width))] + dxn_specs,
        out_shape=[
            jax.ShapeDtypeStruct(shape, BF) for shape in [(length, 3 * width)] + dxn_shapes
        ],
        scratch_shapes=dxn_scratch
        + [pltpu.VMEM((model_width, 3 * width), BF)]
        + [pltpu.VMEM((length, width), F32)] * 3
        + [
            pltpu.VMEM((1, length), F32),
            pltpu.VMEM((length, width), BF),
            pltpu.SemaphoreType.DMA((len(pieces),)),
        ],
        cost_estimate=pl.CostEstimate(
            flops=5 * pairs * HD + 6 * length * model_width * width,
            bytes_accessed=20 * length * width + 2 * model_width * (length + 3 * width),
            transcendentals=pairs // 2,
        ),
        name="attention_backward",
    )(group.reshape(1), query, key, value, attn, grad, lse, cosine, sine, *pieces)


def strided_heads_kernel(which_ref, *refs):
    runs, outs = refs[:-2], refs[-2:]
    parity = which_ref[0] % 2
    half = len(runs) // 2

    for odd in range(2):

        @pl.when(parity == odd)
        def _():
            cols = slice(odd * HD, (odd + 1) * HD)
            for out, first in zip(outs, (0, half)):
                for r in range(0, half, 2):
                    out[:, r * HD : (r + 2) * HD] = jnp.concatenate(
                        [runs[first + r][:, cols], runs[first + r + 1][:, cols]], 1
                    )


def strided_heads(weight, group, group_count):
    rows, columns = weight.shape
    run = group_count * HD // 128
    runs = columns // (group_count * HD)

    def spec(r):
        return pl.BlockSpec((rows, 128), lambda g, w: (0, r * run + w[0] // 2))

    half = (rows, runs // 2 * HD)
    return pl.pallas_call(
        strided_heads_kernel,
        grid_spec=pltpu.PrefetchScalarGridSpec(
            num_scalar_prefetch=1,
            grid=(1,),
            in_specs=[spec(r) for r in range(runs)],
            out_specs=[pl.BlockSpec(half, lambda g, w: (0, 0))] * 2,
        ),
        out_shape=[jax.ShapeDtypeStruct(half, weight.dtype)] * 2,
        name="strided_heads",
    )(group.reshape(1), *[weight] * runs)


def lane_sums(values):
    return jnp.sum(values.T, axis=0, keepdims=True)


def last_rows_kernel(
    piece, which_ref, in_ref, up_ref, qkv_ref, gain1_ref, gain2_ref, part_ref, before_ref,
    out_ref, sum2_ref, strided_ref, sum1_ref,
):
    groups, rows, width = in_ref.shape

    def step(s, total):
        values = in_ref[s, :, :piece].astype(F32)
        cols = pl.ds(pl.multiple_of(s * piece, piece), piece)
        out_ref[:, cols] = values
        product = values * up_ref[:, cols].astype(F32)
        for c in range(piece // 128):
            total = total + product[:, c * 128 : (c + 1) * 128]
        return total

    total = lax.fori_loop(0, groups, step, jnp.zeros((rows, 128), F32))
    sum2_ref[...] = part_ref[...] + lane_sums(total) / gain2_ref[...]

    total = jnp.zeros((rows, 128), F32)
    for b in range((width - piece) // HD):
        cols = slice(piece + b * HD, piece + (b + 1) * HD)
        for pair in range(groups // 2):
            both = jnp.concatenate(
                [in_ref[2 * pair, :, cols], in_ref[2 * pair + 1, :, cols]], 1
            ).astype(F32)
            at = (b * groups + 2 * pair) * HD
            strided_ref[:, at : at + 128] = both
            total = total + both * qkv_ref[:, at : at + 128].astype(F32)
    sum1_ref[...] = lane_sums(total) / gain1_ref[...]


def last_rows(parts, piece, up_weight, qkv_weight, gain1, gain2, part, before, group):
    groups, rows, _ = parts.shape
    half = groups * piece

    def spec(columns, row=False, place=0):
        return pl.BlockSpec((rows, columns), lambda g, w: (w[0] if row else 0, place))

    line = pl.BlockSpec((1, rows), lambda g, w: (0, 0))
    return pl.pallas_call(
        functools.partial(last_rows_kernel, piece),
        grid_spec=pltpu.PrefetchScalarGridSpec(
            num_scalar_prefetch=1,
            grid=(1,),
            in_specs=[
                pl.BlockSpec(parts.shape, lambda g, w: (0, 0, 0)),
                spec(half, True, 1),
                spec(qkv_weight.shape[1], True),
                line, line, line,
                pl.BlockSpec(memory_space=pl.ANY),
            ],
            out_specs=[spec(half, False, 1), line, spec(qkv_weight.shape[1]), line],
        ),
        out_shape=[
            jax.ShapeDtypeStruct((rows, 2 * half), F32),
            jax.ShapeDtypeStruct((1, rows), F32),
            jax.ShapeDtypeStruct((rows, qkv_weight.shape[1]), F32),
            jax.ShapeDtypeStruct((1, rows), F32),
        ],
        input_output_aliases={7: 0},
        name="last_rows",
    )(group.reshape(1), parts, up_weight, qkv_weight, gain1, gain2, part, before)


def side_rows_kernel(runs, which_ref, *refs):
    parts, (weight_ref, gain_ref, out_ref, sum_ref) = refs[:runs], refs[runs:]
    groups, rows, piece = parts[0].shape

    @pl.when(pl.program_id(0) == 0)
    def _():
        sum_ref[...] = jnp.zeros_like(sum_ref)

    for run in range(runs):

        @pl.when(pl.program_id(0) == run)
        def _():
            def step(s, total):
                values = parts[run][s].astype(F32)
                cols = pl.ds(pl.multiple_of(s * piece, piece), piece)
                out_ref[:, cols] = values
                product = values * weight_ref[:, cols].astype(F32)
                for c in range(piece // 128):
                    total = total + product[:, c * 128 : (c + 1) * 128]
                return total

            total = lax.fori_loop(0, groups, step, jnp.zeros((rows, 128), F32))
            sum_ref[...] += lane_sums(total) / gain_ref[...]


def side_rows(parts, piece, weight, gain, group, columns=None):
    groups, rows, _ = parts[0][0].shape
    runs = len(parts)
    columns = columns or runs * groups * piece

    def spec(place):
        return pl.BlockSpec((groups, rows, piece), lambda c, w: (0, 0, place))

    return pl.pallas_call(
        functools.partial(side_rows_kernel, runs),
        grid_spec=pltpu.PrefetchScalarGridSpec(
            num_scalar_prefetch=1,
            grid=(runs,),
            in_specs=[spec(place) for _, place in parts]
            + [
                pl.BlockSpec((rows, groups * piece), lambda c, w: (w[0], c)),
                pl.BlockSpec((1, rows), lambda c, w: (0, 0)),
            ],
            out_specs=[
                pl.BlockSpec((rows, groups * piece), lambda c, w: (0, c)),
                pl.BlockSpec((1, rows), lambda c, w: (0, 0)),
            ],
        ),
        out_shape=[
            jax.ShapeDtypeStruct((rows, columns), F32),
            jax.ShapeDtypeStruct((1, rows), F32),
        ],
        name="side_rows",
    )(group.reshape(1), *[array for array, _ in parts], weight, gain)


BLOCKS = 4


def at_block(ref, rows, index):
    width = ref.shape[1] // BLOCKS
    return ref.at[rows, pl.ds(pl.multiple_of(index * width, width), width)]


def by_rows(kernel):
    def run(table_ref, x_ref, *refs):
        step = min(32, x_ref.shape[0])

        @pl.loop(0, x_ref.shape[0] // step)
        def _(i):
            kernel(pl.ds(pl.multiple_of(i * step, step), step), table_ref, x_ref, *refs)

    return run


ALL = slice(None)


def cast_kernel(rows, orders_ref, grad_ref, dy_ref):
    for p in range(BLOCKS):
        at_block(dy_ref, rows, p)[...] = at_block(grad_ref, rows, orders_ref[p])[...].astype(BF)


def norm_in_kernel(rows, orders_ref, x_ref, gain_ref, xn_ref):
    x = x_ref[rows, :]
    inv = lax.rsqrt(jnp.mean(x * x, axis=1, keepdims=True) + EPS)
    for p in range(BLOCKS):
        block = orders_ref[p]
        normed = at_block(x_ref, rows, block)[...] * inv * at_block(gain_ref, ALL, block)[...]
        at_block(xn_ref, rows, p)[...] = normed.astype(BF)


def norm_mid_kernel(rows, orders_ref, x_ref, own_ref, *refs):
    others, (gain_ref, mid_ref, xn_ref) = refs[:-3], refs[-3:]
    mid = x_ref[rows, :] + own_ref[rows, :]
    for other in others:
        mid = mid + other[rows, :].astype(F32)
    mid_ref[rows, :] = mid
    inv = lax.rsqrt(jnp.mean(mid * mid, axis=1, keepdims=True) + EPS)
    for p in range(BLOCKS):
        block = orders_ref[p]
        normed = at_block(mid_ref, rows, block)[...] * inv * at_block(gain_ref, ALL, block)[...]
        at_block(xn_ref, rows, p)[...] = normed.astype(BF)


def norm_grad_kernel(rows, places_ref, x_ref, base_ref, grad_ref, gain_ref, out_ref, *low_ref):
    x = x_ref[rows, :]
    inv = lax.rsqrt(jnp.mean(x * x, axis=1, keepdims=True) + EPS)
    grad = jnp.concatenate(
        [at_block(grad_ref, rows, places_ref[j])[...] for j in range(BLOCKS)], 1
    ).astype(F32)
    normed = x * inv
    grad_hat = grad * gain_ref[...]
    mean = jnp.mean(grad_hat * normed, axis=1, keepdims=True)
    out = base_ref[rows, :] + inv * (grad_hat - normed * mean)
    out_ref[rows, :] = out
    for ref in low_ref:
        ref[rows, :] = out.astype(BF)


def add_placed_kernel(rows, places_ref, base_ref, part_ref, out_ref):
    for j in range(BLOCKS):
        part = at_block(part_ref, rows, places_ref[j])[...].astype(F32)
        at_block(out_ref, rows, j)[...] = at_block(base_ref, rows, j)[...] + part


def on_rows(kernel, table, inputs, out_types):
    rows, width = inputs[0].shape
    block = rows

    def spec(shape):
        if shape[0] == 1:
            return pl.BlockSpec(shape, lambda i, t: (0, 0))
        return pl.BlockSpec((block, width), lambda i, t: (i, 0))

    return pl.pallas_call(
        by_rows(kernel),
        grid_spec=pltpu.PrefetchScalarGridSpec(
            num_scalar_prefetch=1,
            grid=(rows // block,),
            in_specs=[spec(v.shape) for v in inputs],
            out_specs=[spec((rows, width)) for _ in out_types],
        ),
        out_shape=[jax.ShapeDtypeStruct((rows, width), t) for t in out_types],
    )(table, *inputs)


def placed(pieces, column, columns, target_ref, at_column, sems, copies):
    row = 0
    for piece in pieces:
        rows = piece.shape[0]
        source = piece.at[:, pl.ds(column, columns)]
        place = target_ref.at[pl.ds(row, rows), pl.ds(at_column, columns)]
        copies.append(pltpu.make_async_copy(source, place, sems.at[len(copies)]))
        row += rows


def feed_kernel(count_a, count_b, xn_ref, dy_ref, *refs):
    part_a, part_b, refs = refs[:count_a], refs[count_a : count_a + count_b], refs[count_a + count_b :]
    act_ref, grad_ref, dxn_ref, gate_up_ref, down_ref, sems = refs
    cut = part_a[0].shape[1]
    hidden = act_ref.shape[1]
    split = 2 * hidden - cut

    copies = []
    placed(part_a, 0, cut, gate_up_ref, 0, sems, copies)
    placed(part_b, 0, split, gate_up_ref, cut, sems, copies)
    placed(part_b, split, hidden, down_ref, 0, sems, copies)

    @pl.when(pl.program_id(0) == 0)
    def _():
        for copy in copies:
            copy.start()
        for copy in copies[: count_a + count_b]:
            copy.wait()

    gate_up = jnp.dot(xn_ref[...], gate_up_ref[...], preferred_element_type=F32)
    gate, up_part = gate_up[:, :hidden], gate_up[:, hidden:]
    sigmoid_gate = jax.nn.sigmoid(gate)
    gated = gate * sigmoid_gate
    act_ref[...] = (gated * up_part).astype(BF)

    @pl.when(pl.program_id(0) == 0)
    def _():
        for copy in copies[count_a + count_b :]:
            copy.wait()

    grad_act = jnp.dot(dy_ref[...], down_ref[...], preferred_element_type=F32)
    grad_gate = grad_act * up_part * sigmoid_gate * (1.0 + gate * (1.0 - sigmoid_gate))
    grad_ref[:, :hidden] = grad_gate.astype(BF)
    grad_ref[:, hidden:] = (grad_act * gated).astype(BF)
    columns_last(grad_ref, gate_up_ref, dxn_ref)


def columns_last(left_ref, right_ref, out_ref):
    chunk = min(1024, out_ref.shape[1])

    @pl.loop(0, out_ref.shape[1] // chunk)
    def _(c):
        at = pl.ds(pl.multiple_of(c * chunk, chunk), chunk)
        out_ref[:, at] = contract_last(left_ref[...], right_ref[at, :]).astype(BF)


OVER_X_FIRST = ((1, 3), (3, 4), (0, 1))
OVER_Y_FIRST = ((2, 4), (1, 2), (0, 1))
ONE_EACH = ((0, 1), (1, 2), (2, 3), (3, 4))


def outer_kernel(layouts, left_ref, right_ref, *out_refs):
    step = pl.program_id(0)
    steps = pl.num_programs(0) // 4
    product = contract_first(left_ref[...], right_ref[...]).astype(BF)
    column = 0
    refs = iter(out_refs)
    for layout in layouts:
        targets = [next(refs) for _ in layout]
        width = targets[0].shape[1]
        block = product[:, column : column + width]
        column += width
        for target, (first, end) in zip(targets, layout):

            @pl.when((step >= first * steps) & (step < end * steps))
            def _():
                target[...] = block


def outer_blocks(left, right, layouts, steps=2, side=None):
    tokens, rows = left.shape
    columns = right.shape[1] if side is None else right.shape[1] // 2
    width = columns // len(layouts)
    block = rows // (4 * steps)
    held = [blocks for layout in layouts for blocks in layout]

    def spec(first, end):
        return pl.BlockSpec(
            (block, width),
            lambda p: (jnp.clip(p - first * steps, 0, (end - first) * steps - 1), 0),
        )

    outs = pl.pallas_call(
        functools.partial(outer_kernel, layouts),
        grid=(4 * steps,),
        in_specs=[
            pl.BlockSpec((tokens, block), lambda p: (0, p)),
            pl.BlockSpec((tokens, columns), lambda p: (0, side or 0)),
        ],
        out_specs=[spec(*blocks) for blocks in held],
        out_shape=[
            jax.ShapeDtypeStruct(((end - first) * rows // 4, width), BF) for first, end in held
        ],
        cost_estimate=pl.CostEstimate(
            flops=2 * tokens * rows * columns,
            bytes_accessed=2 * (tokens * (rows + columns) + rows * columns),
            transcendentals=0,
        ),
        name="outer_blocks",
    )(left, right)
    outs = iter(outs)
    return [[next(outs) for _ in layout] for layout in layouts]


def in_order(parts):
    return [piece for k in GRAY for piece in parts[k]]


def feed_forward(xn, dy, part_a, part_b, hidden):
    tokens, model_width = xn.shape
    block = min(256, tokens)
    part_a, part_b = in_order(part_a), in_order(part_b)

    def blocks(columns):
        return pl.BlockSpec((block, columns), lambda i: (i, 0))

    return pl.pallas_call(
        functools.partial(feed_kernel, len(part_a), len(part_b)),
        grid=(tokens // block,),
        in_specs=[blocks(model_width)] * 2
        + [pl.BlockSpec(memory_space=pl.ANY)] * (len(part_a) + len(part_b)),
        out_specs=[blocks(hidden), blocks(2 * hidden), blocks(model_width)],
        out_shape=[
            jax.ShapeDtypeStruct((tokens, columns), BF)
            for columns in (hidden, 2 * hidden, model_width)
        ],
        scratch_shapes=[
            pltpu.VMEM((model_width, 2 * hidden), BF),
            pltpu.VMEM((model_width, hidden), BF),
            pltpu.SemaphoreType.DMA((len(part_a) + 2 * len(part_b),)),
        ],
        cost_estimate=pl.CostEstimate(
            flops=10 * tokens * model_width * hidden,
            bytes_accessed=2 * (4 * tokens * model_width + 3 * model_width * hidden),
            transcendentals=tokens * hidden,
        ),
        name="feed_forward",
    )(xn, dy, *part_a, *part_b)


def feed_out_kernel(count, group_ref, act_ref, *refs):
    pieces, (mine_ref, theirs_ref, out_ref, down_ref, sems) = refs[:count], refs[count:]
    hidden = act_ref.shape[1]
    tokens = mine_ref.shape[0]

    @pl.when(pl.program_id(0) == 0)
    def _():
        copies = []
        placed(pieces, pieces[0].shape[1] - hidden, hidden, down_ref, 0, sems, copies)
        for copy in copies:
            copy.start()
        for copy in copies:
            copy.wait()

    columns_last(act_ref, down_ref, out_ref)
    odd = group_ref[0] % 2
    mine_ref[...] = out_ref[pl.ds(pl.multiple_of(odd * tokens, tokens), tokens), :]
    theirs_ref[...] = out_ref[pl.ds(pl.multiple_of((1 - odd) * tokens, tokens), tokens), :]


def feed_out(act, part_b, model_width, group, run):
    tokens, hidden = act.shape
    block = 2 * run
    pieces = in_order(part_b)
    half = jax.ShapeDtypeStruct((tokens // 2, model_width), BF)
    return pl.pallas_call(
        functools.partial(feed_out_kernel, len(pieces)),
        grid=(tokens // block,),
        in_specs=[pl.BlockSpec(memory_space=pltpu.SMEM)]
        + [pl.BlockSpec((block, hidden), lambda i: (i, 0))]
        + [pl.BlockSpec(memory_space=pl.ANY)] * len(pieces),
        out_specs=[pl.BlockSpec((run, model_width), lambda i: (i, 0))] * 2,
        out_shape=[half, half],
        scratch_shapes=[
            pltpu.VMEM((block, model_width), BF),
            pltpu.VMEM((model_width, hidden), BF),
            pltpu.SemaphoreType.DMA((len(pieces),)),
        ],
        cost_estimate=pl.CostEstimate(
            flops=2 * tokens * model_width * hidden,
            bytes_accessed=2 * (tokens + model_width) * hidden + 2 * tokens * model_width,
            transcendentals=0,
        ),
        name="feed_out",
    )(group.reshape(1), act, *pieces)


def project_kernel(members_ref, features_ref, weight_ref, own_ref, *other_refs):
    product = contract_first(features_ref[0], weight_ref[...])

    @pl.when(pl.program_id(0) == 0)
    def _():
        own_ref[...] = product

    for k, other in enumerate(other_refs):

        @pl.when(pl.program_id(0) == k + 1)
        def _():
            other[...] = product.astype(BF)


def project(features, weight, members):
    _, count, tokens = features.shape
    width = weight.shape[1]
    place = pl.BlockSpec((tokens, width), lambda k, m: (0, 0))
    return pl.pallas_call(
        project_kernel,
        grid_spec=pltpu.PrefetchScalarGridSpec(
            num_scalar_prefetch=1,
            grid=(4,),
            in_specs=[
                pl.BlockSpec((1, count, tokens), lambda k, m: (m[k], 0, 0)),
                pl.BlockSpec(weight.shape, lambda k, m: (0, 0)),
            ],
            out_specs=[place] * 4,
        ),
        out_shape=[jax.ShapeDtypeStruct((tokens, width), F32)]
        + [jax.ShapeDtypeStruct((tokens, width), BF)] * 3,
        name="project",
    )(members, features, weight)


def rows_by_member(pieces, places_ref, target_ref, sems):
    height = pieces[0].shape[0]
    copies = [
        pltpu.make_async_copy(
            piece,
            target_ref.at[pl.ds(pl.multiple_of(places_ref[k] * height, height), height)],
            sems.at[k],
        )
        for k, piece in enumerate(pieces)
    ]
    for copy in copies:
        copy.start()
    for copy in copies:
        copy.wait()


def out_rows_kernel(members_ref, features_ref, *refs):
    pieces, (out_ref, rows_ref, sems) = refs[:4], refs[4:]
    rows_by_member(pieces, members_ref, rows_ref, sems)
    left = jnp.concatenate([features_ref[d] for d in range(4)], 1)
    chunk = 512

    @pl.loop(0, out_ref.shape[1] // chunk)
    def _(c):
        at = pl.ds(pl.multiple_of(c * chunk, chunk), chunk)
        out_ref[:, at] = jnp.dot(left, rows_ref[:, at], preferred_element_type=F32).astype(BF)


def out_rows_grad(features, pieces, members):
    tokens, width = pieces[0].shape
    count = features.shape[1]
    return pl.pallas_call(
        out_rows_kernel,
        grid_spec=pltpu.PrefetchScalarGridSpec(
            num_scalar_prefetch=1,
            grid=(1,),
            in_specs=[pl.BlockSpec(features.shape, lambda i, m: (0, 0, 0))]
            + [pl.BlockSpec(memory_space=pl.ANY)] * 4,
            out_specs=pl.BlockSpec((count, width), lambda i, m: (0, 0)),
            scratch_shapes=[pltpu.VMEM((4 * tokens, width), BF), pltpu.SemaphoreType.DMA((4,))],
        ),
        out_shape=jax.ShapeDtypeStruct((count, width), BF),
        name="out_rows",
    )(members, features, *pieces)


def partner(array, bits):
    return lax.ppermute(array, "dp", [(i, i ^ bits) for i in range(4)])


class Quad:
    def __init__(self, index):
        self.index = index

    def gather_direct(self, block):
        return [block] + [partner(block, k) for k in (1, 2, 3)]

    def gather(self, first, second):
        a = {0: [first], 1: [partner(first, 1)]}
        b = {0: [second], 2: [partner(second, 2)]}
        a[2], b[1] = [partner(first, 2)], [partner(second, 1)]
        a[3], b[3] = [partner(a[1][0], 2)], [partner(b[2][0], 1)]
        return a, b

    def gather_late(self, first, second, first_high, second_high):
        rows = first_high.shape[0]
        a = {0: [first], 1: [partner(first, 1)]}
        b = {0: [second], 2: [partner(second, 2)]}
        a[2], b[1] = [partner(first_high, 2)], [partner(second_high, 1)]

        def late(*earlier):
            first_low, second_low, near_a, near_b = (
                after(v, *earlier) for v in (first[rows:], second[rows:], a[1][0], b[2][0])
            )
            a[2].append(partner(first_low, 2))
            b[1].append(partner(second_low, 1))
            a[3], b[3] = [partner(near_a, 2)], [partner(near_b, 1)]
            return a, b

        return late


def add(*terms):
    total = terms[0].astype(F32)
    for term in terms[1:]:
        total = total + term.astype(F32)
    return total.astype(BF)


class PairSum:
    def __init__(self, first, second):
        (send_a, *self.keep_a), (send_b, *self.keep_b) = first, second
        self.sent_a = partner(send_a, 1)
        self.sent_b = partner(send_b, 2)

    def second(self):
        rows = self.keep_a[0].shape[0]
        send_a = add(self.keep_a[0], self.sent_a[rows:])
        send_b = add(self.keep_b[0], self.sent_b[:rows])
        self.far_a = partner(send_a, 2)
        self.far_b = partner(send_b, 1)

    def total(self):
        rows = self.keep_a[0].shape[0]
        return jnp.concatenate(
            [
                add(self.keep_a[1], self.sent_a[:rows], self.far_a),
                add(self.keep_b[1], self.sent_b[rows:], self.far_b),
            ],
            1,
        )


def sum_direct(blocks):
    others = [partner(blocks[p], GRAY[p]) for p in (1, 2, 3)]
    return add(blocks[0], *others)


def reduce_plain(left, right):
    return lax.psum_scatter(
        contract_first(left, right).astype(BF), "dp", scatter_dimension=0, tiled=True
    )


def over_seq(values):
    return lax.all_gather(values, "seq", axis=0, tiled=True)


def sum_over_seq(values):
    return lax.psum_scatter(values.astype(BF), "seq", scatter_dimension=0, tiled=True)


def sum_over_pairs(mine, theirs, group_count, *earlier):
    received = lax.ppermute(theirs, "seq", [(i, i ^ 1) for i in range(group_count)])
    total = after(add(mine, received), *earlier)
    return lax.psum_scatter(
        total, "seq", scatter_dimension=0, tiled=True,
        axis_index_groups=[list(range(odd, group_count, 2)) for odd in range(2)],
    )


def exchange(values, axes):
    return lax.all_to_all(values, axes, split_axis=0, concat_axis=0, tiled=True)


def exchange_rows(values, group_count):
    return exchange(
        values.reshape(group_count, values.shape[0] // group_count, values.shape[1]), "seq"
    )


def feed_forward_plain(xn, dy, gate_up_full, down_full, hidden):
    gate_up = jnp.dot(xn, gate_up_full, preferred_element_type=F32)
    gate, up_part = gate_up[:, :hidden], gate_up[:, hidden:]
    sigmoid_gate = jax.nn.sigmoid(gate)
    act = (gate * sigmoid_gate * up_part).astype(BF)
    grad_act = jnp.dot(dy, down_full, preferred_element_type=F32)
    grad_gate = grad_act * up_part * sigmoid_gate * (1.0 + gate * (1.0 - sigmoid_gate))
    grad_up = grad_act * gate * sigmoid_gate
    grad_gate_up = jnp.concatenate([grad_gate, grad_up], 1).astype(BF)
    return act, grad_gate_up, contract_last(grad_gate_up, gate_up_full).astype(BF)


def shards(
    layer_in, norm1_gain, qkv_weight, out_weight, norm2_gain, gate_up_weight, down_weight, cotangent
):
    token_rows, model_width = layer_in.shape
    group_count = lax.axis_size("seq")
    dp_count = lax.axis_size("dp")
    group = lax.axis_index("seq")
    member = lax.axis_index("dp")
    length = token_rows * group_count
    dp_rows = model_width // dp_count
    shard_rows = dp_rows // group_count
    hidden_units = down_weight.shape[1]
    hidden = hidden_units // group_count
    width = model_width // group_count
    quad = Quad(member) if dp_count == 4 else None
    strided = quad is not None and shard_rows == HD

    blocks_at = jnp.arange(4, dtype=jnp.int32)
    if quad:
        orders = (blocks_at ^ (blocks_at >> 1)) ^ member
        places = blocks_at ^ member
        places = places ^ (places >> 1)
    else:
        orders, places = blocks_at, blocks_at
    gain1, gain2 = norm1_gain[None, :], norm2_gain[None, :]

    (xn1_own,) = on_rows(norm_in_kernel, orders, (layer_in, gain1), (BF,))
    xn1 = over_seq(xn1_own)
    (dy_own,) = on_rows(cast_kernel, orders, (cotangent,), (BF,))

    if strided:
        left, right = strided_heads(qkv_weight, group, group_count)
    else:
        qkv_piece = jnp.concatenate(
            [
                lax.dynamic_slice_in_dim(qkv_weight, part * model_width + group * width, width, 1)
                for part in range(3)
            ],
            1,
        )
    gate_piece = lax.dynamic_slice_in_dim(gate_up_weight, group * hidden, hidden, 1)
    up_piece = lax.dynamic_slice_in_dim(gate_up_weight, hidden_units + group * hidden, hidden, 1)
    down_piece = lax.dynamic_slice_in_dim(down_weight, group * hidden, hidden, 1)
    if quad:
        if not strided:
            cut = qkv_piece.shape[1] // 2
            left, right = qkv_piece[:, :cut], qkv_piece[:, cut:]
        left, right = quad.gather(left, right)
        blocks = (left[3][0], right[3][0])
        qkv_pieces = [part[k][0] for k in GRAY for part in (left, right)]
        per_row = 2
        half = hidden // 2
        part_a = after(jnp.concatenate([gate_piece, up_piece[:, :half]], 1), *blocks)
        part_b = after(jnp.concatenate([up_piece[:, half:], down_piece], 1), *blocks)
        high = dp_rows // 2
        high_a, high_b = part_a[:high], part_b[:high]
        xn1, high_a, high_b = lax.optimization_barrier((xn1, high_a, high_b))
        rest_of_weights = quad.gather_late(part_a, part_b, high_a, high_b)
    else:
        qkv_pieces, per_row = [lax.all_gather(qkv_piece, "dp", axis=0, tiled=True)], 1
        gate_up_full = lax.all_gather(
            jnp.concatenate([gate_piece, up_piece], 1), "dp", axis=0, tiled=True
        )
        down_full = lax.all_gather(down_piece, "dp", axis=0, tiled=True)

    cosine, sine = rotary_tables(length)
    attn, query, key, value, lse = attention_forward(
        xn1, qkv_pieces, per_row, cosine, sine, token_rows
    )

    dy = over_seq(after(dy_own, attn))

    def to_features(by_head):
        if strided:
            moved = exchange(by_head.reshape(-1, HD, token_rows), ("dp", "seq"))
        else:
            by_tokens = by_head.transpose(1, 0, 2, 3).reshape(group_count, width, token_rows)
            moved = exchange(exchange(by_tokens, "seq").reshape(dp_count, dp_rows, token_rows), "dp")
        return moved.reshape(dp_count, dp_rows, token_rows)

    def to_heads(features):
        if strided:
            moved = exchange(features.reshape(-1, HD, token_rows), ("dp", "seq"))
            return moved.reshape(-1, group_count, HD, token_rows)
        moved = exchange(features, "dp").reshape(group_count, width, token_rows)
        moved = exchange(moved, "seq").reshape(group_count, width // HD, HD, token_rows)
        return moved.transpose(1, 0, 2, 3)

    features = to_features(attn)
    if quad:
        parts = project(features, out_weight, blocks_at ^ member)
        others = [partner(parts[k], k) for k in (1, 2, 3)]
        partials = (parts[0], *others)
    else:
        partials = (
            lax.psum_scatter(
                jnp.einsum("dft,fn->dtn", features, out_weight, preferred_element_type=F32)
                .astype(BF)
                .reshape(dp_count * token_rows, model_width),
                "dp", scatter_dimension=0, tiled=True,
            ).astype(F32),
        )

    hidden_res, xn2_own = on_rows(norm_mid_kernel, orders, (layer_in, *partials, gain2), (F32, BF))
    xn2 = over_seq(xn2_own)
    if quad:
        part_a, part_b = rest_of_weights(*partials)
        act, grad_gate_up, partial_xn2 = feed_forward(xn2, dy, part_a, part_b, hidden)
        feed_halves = feed_out(after(act, partial_xn2), part_b, model_width, group, token_rows)
    else:
        act, grad_gate_up, partial_xn2 = feed_forward_plain(
            xn2, dy, gate_up_full, down_full, hidden
        )
        feed_sum = contract_last(act, down_full).astype(BF)
    raw_xn2 = sum_over_seq(partial_xn2)
    grad_hidden, hidden_low = on_rows(
        norm_grad_kernel, places, (hidden_res, cotangent, raw_xn2, gain2), (F32, BF)
    )
    if quad:
        feed_sum = sum_over_pairs(*feed_halves, group_count, raw_xn2)
    else:
        feed_sum = sum_over_seq(after(feed_sum, raw_xn2))
    if quad:
        sides = (OVER_X_FIRST, OVER_Y_FIRST)
        down_sum = PairSum(*outer_blocks(dy, act, sides, 1))
        gate_sum = PairSum(*outer_blocks(xn2, grad_gate_up, sides, 1, 0))
        up_sum = PairSum(*outer_blocks(xn2, grad_gate_up, sides, 1, 1))
        rows_low = quad.gather_direct(hidden_low)
    else:
        down_rows = reduce_plain(dy, act)
        gate_rows = reduce_plain(xn2, grad_gate_up[:, :hidden])
        up_rows = reduce_plain(xn2, grad_gate_up[:, hidden:])
        rows_low = list(lax.all_gather(hidden_low, "dp", axis=0))

    grad_features = jnp.einsum(
        "fn,ktn->kft", out_weight, jnp.stack(rows_low), preferred_element_type=F32
    ).astype(BF)
    if quad:
        grad_features = jnp.stack(
            [lax.dynamic_index_in_dim(grad_features, member ^ j, 0, False) for j in range(4)]
        )
    grad_attn = to_heads(grad_features)
    if quad:
        down_sum.second()
        gate_sum.second()
        up_sum.second()
    if quad:
        out_rows = out_rows_grad(features, rows_low, blocks_at ^ member)
    else:
        out_rows = jnp.einsum(
            "kft,ktn->fn", features, jnp.stack(rows_low), preferred_element_type=F32
        ).astype(BF)
    out_grad = sum_over_seq(out_rows).astype(F32)
    grad_qkv, *partial_xn1 = attention_backward(
        group, quad is not None,
        query, key, value, attn, grad_attn, lse, cosine, sine, qkv_pieces, per_row,
    )
    if quad:
        raw_xn1 = sum_over_pairs(*partial_xn1, group_count)
    else:
        raw_xn1 = sum_over_seq(partial_xn1[0])
    (input_grad,) = on_rows(
        norm_grad_kernel, places, (layer_in, grad_hidden, raw_xn1, gain1), (F32,)
    )
    (layer_out,) = on_rows(
        add_placed_kernel, places, (hidden_res, after(feed_sum, grad_qkv)), (F32,)
    )

    if quad:
        (blocks,) = outer_blocks(xn1, grad_qkv, (ONE_EACH,))
        qkv_rows = sum_direct(blocks)
        down_rows, gate_rows, up_rows = down_sum.total(), gate_sum.total(), up_sum.total()
    else:
        qkv_rows = reduce_plain(xn1, grad_qkv)
    near_parts = exchange_rows(jnp.concatenate([down_rows, gate_rows], 1), group_count)
    far_parts = exchange_rows(jnp.concatenate([up_rows, qkv_rows], 1), group_count)
    own_at = member * dp_rows + group * shard_rows
    own1 = lax.dynamic_slice_in_dim(gain1, own_at, shard_rows, 1)
    own2 = lax.dynamic_slice_in_dim(gain2, own_at, shard_rows, 1)
    down_grad, _ = side_rows([(near_parts, 0)], hidden, down_weight, own2, group)
    if strided:
        before, part = side_rows(
            [(near_parts, 1)], hidden, gate_up_weight, own2, group, 2 * hidden_units
        )
        gate_up_grad, norm2_grad, qkv_grad, norm1_grad = last_rows(
            far_parts, hidden, gate_up_weight, qkv_weight, own1, own2, part, before, group
        )
    else:
        gate_up_grad, norm2_grad = side_rows(
            [(near_parts, 1), (far_parts, 0)], hidden, gate_up_weight, own2, group
        )
        qkv_parts = far_parts[:, :, hidden:]
        qkv_grad, norm1_grad = side_rows(
            [(qkv_parts, i) for i in range(3)], width, qkv_weight, own1, group
        )

    return (
        layer_out,
        input_grad,
        norm1_grad.reshape(shard_rows),
        qkv_grad,
        out_grad,
        norm2_grad.reshape(shard_rows),
        gate_up_grad,
        down_grad,
    )


def solution(mesh):
    rows = P(("dp", "seq"), None)
    in_specs = (
        rows, P(), P("dp", None), P("dp", None), P(), P("dp", None), P("dp", None), rows,
    )
    vector = P(("dp", "seq"))
    out_specs = (rows, rows, vector, rows, rows, vector, rows, rows)
    return jax.shard_map(shards, mesh=mesh, in_specs=in_specs, out_specs=out_specs, check_vma=False)
```
